32 devices in a mesh: groups: 2 (over y), obs: 4 (over z), hid: 2 (over x), rep: 2 (over core).
Axes of the slice: x: 2, y: 2, z: 4, core: 2. Of those that a mesh axis runs over, the one named last changes fastest.
Arguments:
- particles: float32 [8, 128, 512], P(('groups', 'obs')), parts along dimension 0, may hold values from -6 to 6
- obs_embed: bfloat16 [32768, 256], P(('groups', 'obs', 'rep')), parts along dimension 0, may hold values from -6 to 6
- step_index: int32 [2], P('groups'), parts along dimension 0, may hold values from 1 to 63
- noise: float32 [8, 128, 512], P('groups', 'obs'), parts along dimension 0, may hold values from -6 to 6
- w_query: bfloat16 [512, 2048], P(None, 'hid'), may hold values from -0.25 to 0.25
- w_key: bfloat16 [256, 2048], P(None, 'hid'), may hold values from -0.375 to 0.375
- w_value: bfloat16 [256, 2048], P(None, 'hid'), may hold values from -0.375 to 0.375
- w_time: bfloat16 [256, 16], P(None, 'hid'), may hold values from -0.375 to 0.375
- w_score: bfloat16 [2048, 512], P('hid'), may hold values from -0.0009765625 to 0.0009765625
- prior_in: bfloat16 [512, 2048], P(None, 'hid'), may hold values from -0.25 to 0.25
- prior_time: bfloat16 [256, 2048], P(None, 'hid'), may hold values from -0.375 to 0.375
- prior_out: bfloat16 [2048, 512], P('hid'), may hold values from -7.6293945e-06 to 7.6293945e-06
Outputs:
- updated: float32 [8, 128, 512], P('groups', 'obs'), parts along dimension 0
- score_total: float32 [8, 128, 512], P('groups', 'obs'), parts along dimension 0
The draws below stay inside these ranges and needn't reach their ends.
There are 2 independent parts, one for each index of `groups`. The reference program is written for one: setup_inputs(seed, part) draws one part's arguments, and reference() takes and returns one part's arrays. A program takes and returns all parts, laid end to end along the dimension named above; an argument that names none is the same for every part. Nothing has to cross between parts.
All inputs are finite; a program needn't handle non-finite values.
Results may differ from the reference program's by a relative error of at most 0.0042.
Values may be sent and summed in bfloat16 or wider, within the bound.
No kernel may reach another device: no remote copies, remote signals or barrier semaphores. Data moves between devices by JAX's collectives and lax.ppermute only.
A program may use at most 64 MiB of HBM per device.

```python
import math
import jax
import jax.numpy as jnp
from jax import lax

P_SIZE = 512
H = 2048
DH = 128
EMB = 256
TF = 256
STEPS = 64
BLK = 128
NH = 16
NPART = 512
NOBS = 16384
N_OBS = 4


def block_scale(rng, shape, shards, low, largest):
    gain, own = 1.0, jax.random.fold_in(rng, 6)
    for dim, parts in shards:
        steps = jnp.exp(jax.random.uniform(jax.random.fold_in(own, dim), (parts,), jnp.float32, low / len(shards), largest / len(shards)))
        gain = gain * jnp.repeat(steps, shape[dim] // parts).reshape([-1 if axis == dim else 1 for axis in range(len(shape))])
    return gain


def normal_values(stream_key, extent, spread, limit, cuts=(), dtype=jnp.bfloat16):
    loudness = block_scale(stream_key, extent, cuts, -0.22, 0.18) if cuts else 1.0
    drawn = jax.random.normal(stream_key, extent, jnp.float32) * spread * loudness
    return jnp.minimum(jnp.maximum(drawn, -limit), limit).astype(dtype)


def setup_inputs(seed: int = 0, part: int = 0) -> dict:
    key_of = jax.random.split(jax.random.key(seed), 13)
    part_keys = jax.random.split(jax.random.fold_in(key_of[12], part), 13)
    return {
        "particles": normal_values(part_keys[0], (N_OBS, BLK, P_SIZE), 1.0, 6.0, ((0, 4),), jnp.float32),
        "obs_embed": normal_values(part_keys[1], (NOBS, EMB), 1.0, 6.0, ((0, 8),)),
        "step_index": jax.random.randint(part_keys[2], (1,), 1, STEPS).astype(jnp.int32),
        "noise": normal_values(part_keys[3], (N_OBS, BLK, P_SIZE), 1.0, 6.0, ((1, 4),), jnp.float32),
        "w_query": normal_values(key_of[4], (P_SIZE, H), P_SIZE ** -0.5, 0.25, ((1, 2),)),
        "w_key": normal_values(key_of[5], (EMB, H), EMB ** -0.5, 0.375, ((1, 2),)),
        "w_value": normal_values(key_of[6], (EMB, H), EMB ** -0.5, 0.375, ((1, 2),)),
        "w_time": normal_values(key_of[7], (TF, NH), TF ** -0.5, 0.375, ((1, 2),)),
        "w_score": normal_values(key_of[8], (H, P_SIZE), (H * NOBS) ** -0.5, 0.0009765625, ((0, 2),)),
        "prior_in": normal_values(key_of[9], (P_SIZE, H), P_SIZE ** -0.5, 0.25, ((1, 2),)),
        "prior_time": normal_values(key_of[10], (TF, H), TF ** -0.5, 0.375, ((1, 2),)),
        "prior_out": normal_values(key_of[11], (H, P_SIZE), (H * NOBS * NOBS) ** -0.5, 7.62939453125e-06, ((0, 2),)),
    }


SIG_LO = 0.05
SIG_HI = 1.0

def plan(step_index, feature_count):
    level = step_index[0].astype(jnp.float32)
    growth = math.log(SIG_HI / SIG_LO) / (STEPS - 1)
    sigma_now = SIG_LO * jnp.exp(growth * level)
    sigma_prev = SIG_LO * jnp.exp(growth * (level - 1.0))
    delta = sigma_now * sigma_now - sigma_prev * sigma_prev
    halves = feature_count // 2
    frequency = jnp.exp(-math.log(1000.0) / halves * jnp.arange(halves).astype(jnp.float32))
    angles = 10.0 * jnp.log(sigma_now) * frequency
    features = jnp.concatenate([jnp.sin(angles), jnp.cos(angles)])[None, :].astype(jnp.bfloat16)
    return (features, delta)

def pooled_block(queries, keys, values, head_bias):
    count = queries.shape[0]
    query_heads = queries.astype(jnp.float32).reshape(count, -1, DH)
    key_heads = keys.astype(jnp.float32).reshape(keys.shape[0], -1, DH)
    value_heads = values.astype(jnp.float32).reshape(values.shape[0], -1, DH)
    scores = jnp.einsum('phd,jhd->phj', query_heads, key_heads)
    weights = jax.nn.silu(scores * (1.0 / math.sqrt(DH)) + head_bias[None, :, None]).astype(jnp.bfloat16)
    pooled = jnp.einsum('phj,jhd->phd', weights.astype(jnp.float32), value_heads)
    return pooled.reshape(count, -1)

def reference(particles, obs_embed, step_index, noise, w_query, w_key, w_value, w_time, w_score, prior_in, prior_time, prior_out):
    features, delta = plan(step_index, w_time.shape[0])
    theta = particles.reshape(NPART, P_SIZE).astype(jnp.bfloat16)
    queries = jnp.dot(theta, w_query, preferred_element_type=jnp.float32).astype(jnp.bfloat16)
    keys = jnp.dot(obs_embed, w_key, preferred_element_type=jnp.float32).astype(jnp.bfloat16)
    values = jnp.dot(obs_embed, w_value, preferred_element_type=jnp.float32).astype(jnp.bfloat16)
    head_bias = jnp.dot(features, w_time, preferred_element_type=jnp.float32)[0]
    pooled = lax.map(lambda query_block: pooled_block(query_block, keys, values, head_bias), queries.reshape(N_OBS, BLK, H))
    pooled = pooled.reshape(NPART, H)
    obs_score = jnp.dot(pooled, w_score.astype(jnp.float32), precision=lax.Precision.HIGHEST, preferred_element_type=jnp.float32)
    prior_pre = jnp.dot(theta, prior_in, preferred_element_type=jnp.float32) + jnp.dot(features, prior_time, preferred_element_type=jnp.float32)
    prior_hidden = jax.nn.silu(prior_pre).astype(jnp.bfloat16)
    prior_score = jnp.dot(prior_hidden, prior_out, preferred_element_type=jnp.float32)
    score_total = (obs_score - (NOBS - 1) * prior_score).reshape(N_OBS, BLK, P_SIZE)
    updated = particles + delta * score_total + jnp.sqrt(delta) * noise
    return (updated, score_total)
```

```python
import functools
import math

import jax
import jax.numpy as jnp
from jax import lax
from jax.experimental import pallas as pl
from jax.experimental.pallas import tpu as pltpu
from jax.sharding import PartitionSpec as P

DH = 128
STEPS = 64

SIG_LO = 0.05
SIG_HI = 1.0

F32 = jnp.float32
BF16 = jnp.bfloat16
NT = (((1,), (1,)), ((), ()))
TILE = 512


def passed_along(shard, axis, by):
    size = lax.axis_size(axis)
    return lax.ppermute(shard, axis, [(i, (i + by) % size) for i in range(size)])


def plan(step_index, feature_count):
    level = step_index[0].astype(F32)
    growth = math.log(SIG_HI / SIG_LO) / (STEPS - 1)
    sigma_now = SIG_LO * jnp.exp(growth * level)
    sigma_prev = SIG_LO * jnp.exp(growth * (level - 1.0))
    delta = sigma_now * sigma_now - sigma_prev * sigma_prev
    halves = feature_count // 2
    frequency = jnp.exp(-math.log(1000.0) / halves * jnp.arange(halves).astype(F32))
    angles = 10.0 * jnp.log(sigma_now) * frequency
    features = jnp.concatenate([jnp.sin(angles), jnp.cos(angles)])[None, :].astype(BF16)
    return (features, delta)


def dot(a, b):
    return jnp.dot(a, b, preferred_element_type=F32)


def wrap(index, size):
    return lax.rem(index, jnp.int32(size))


def halves_of(x):
    high = x.astype(BF16)
    return high, (x - high.astype(F32)).astype(BF16)


def split_dot(x, weight):
    rows = x.shape[0]
    both = dot(jnp.concatenate(halves_of(x), 0), weight)
    return both[:rows] + both[rows:]


def half_silu(y):
    return y + y * jnp.tanh(y)


def put_stripes(stage, first, count, values):
    sub = stage.shape[1]
    for s in range(count):
        stage[first + s] = values[s * sub : (s + 1) * sub]


def spec():
    return pl.BlockSpec(memory_space=pltpu.VMEM)


def smem():
    return pl.BlockSpec(memory_space=pltpu.SMEM)


def call(body, name, out_shape, n_in, scratch=(), flops=0, limit=None):
    return pl.pallas_call(
        body,
        name=name,
        out_shape=out_shape,
        in_specs=[smem()] + [spec()] * n_in,
        out_specs=jax.tree.map(lambda _: spec(), out_shape),
        scratch_shapes=list(scratch),
        cost_estimate=pl.CostEstimate(flops=flops, bytes_accessed=flops // 1000, transcendentals=0),
        compiler_params=pltpu.CompilerParams(vmem_limit_bytes=limit),
    )


def prep_body(size, at_ref, home_ref, theta_ref, mine_ref, *rest):
    sends, stage = rest[:-1], rest[-1]
    z, r = at_ref[0], at_ref[1]
    sub = home_ref.shape[2]
    for s in range(size):
        stage[s * sub : (s + 1) * sub, :] = home_ref[s, r]
    theta = stage[...].astype(BF16)
    theta_ref[...] = theta
    mine_ref[...] = home_ref[z, r]
    rows = theta.shape[0]
    for shift, send in enumerate(sends, 1):
        left = home_ref[wrap(z + shift, size), r]
        send[:rows, :] = theta
        send[rows:, :] = halves_of(left)[1]


def pair_terms(theta, scale, e_refs, wq_ref, wk_ref, wv_ref, ws_ref, bias_ref, qk_ref, pool_ref):
    blocks = len(theta)
    rows = theta[0].shape[0]
    heads = wk_ref.shape[1] // DH
    every = theta[0] if blocks == 1 else jnp.concatenate(theta, 0)
    queries = dot(every, wq_ref[...]).astype(BF16)
    for h in range(heads):
        cols = slice(h * DH, (h + 1) * DH)
        turned = lax.dot_general(queries[:, cols], wk_ref[:, cols], NT, preferred_element_type=F32)
        turned = (turned * scale).astype(BF16)
        for b in range(blocks):
            at = (b * heads + h) * rows
            qk_ref[at : at + rows, :] = turned[b * rows : (b + 1) * rows]

    def weights(scores):
        parts = []
        for h in range(heads):
            bias = jnp.tile(bias_ref[h : h + 1, :], (1, scores.shape[1] // 128))
            parts.append(half_silu(scores[h * rows : (h + 1) * rows] + bias).astype(BF16))
        return jnp.concatenate(parts, 0)

    for b in range(blocks):
        span = slice(b * heads * rows, (b + 1) * heads * rows)
        total = None
        for e_ref in e_refs:
            tile = math.gcd(TILE, e_ref.shape[0])
            for j in range(e_ref.shape[0] // tile):
                seen = e_ref[j * tile : (j + 1) * tile, :]
                scores = lax.dot_general(qk_ref[span, :], seen, NT, preferred_element_type=F32)
                term = dot(weights(scores), seen)
                total = term if total is None else total + term
        for h in range(heads):
            cols = slice(h * DH, (h + 1) * DH)
            pool_ref[b * rows : (b + 1) * rows, cols] = split_dot(
                total[h * rows : (h + 1) * rows], wv_ref[:, cols]
            )
    return split_dot(pool_ref[...], ws_ref[...])


def home_body(size, nrep, count, at_ref, theta_ref, *rest):
    e_refs, rest = rest[:nrep], rest[nrep:]
    wq_ref, wk_ref, wv_ref, ws_ref, feat_ref, wt_ref, pin_ref, pt_ref, pout_ref = rest[:9]
    own_ref, bias_ref = rest[9:11]
    sends = rest[11 : 10 + size]
    qk_ref, pool_ref, stage = rest[10 + size :]
    z = at_ref[0]
    heads = wk_ref.shape[1] // DH
    feat = jnp.broadcast_to(feat_ref[...], (16, feat_ref.shape[1]))
    head_bias = dot(feat, wt_ref[...]) * 0.5
    for h in range(heads):
        bias_ref[h : h + 1, :] = jnp.broadcast_to(head_bias[0:1, h : h + 1], (1, 128))
    theta = theta_ref[...]
    pre = dot(theta, pin_ref[...]) + dot(feat, pt_ref[...])[0:1]
    prior = dot(half_silu(0.5 * pre).astype(BF16), pout_ref[...])
    terms = pair_terms(
        [theta], 0.5 / math.sqrt(DH), e_refs, wq_ref, wk_ref, wv_ref, ws_ref, bias_ref, qk_ref, pool_ref
    )
    put_stripes(stage, 0, size, terms - count * prior)
    own_ref[...] = stage[z]
    for shift, send in enumerate(sends, 1):
        send[...] = stage[wrap(z + shift, size)].astype(BF16)


def away_body(size, nrep, nblk, at_ref, *rest):
    got, rest = rest[:nblk], rest[nblk:]
    e_refs, rest = rest[:nrep], rest[nrep:]
    wq_ref, wk_ref, wv_ref, ws_ref, bias_ref = rest[:5]
    own_ref, part_ref = rest[5:7]
    sends = rest[7 : 6 + size]
    qk_ref, pool_ref, stage = rest[6 + size :]
    z = at_ref[0]
    sub = own_ref.shape[1]
    rows = size * sub
    theta = [ref[:rows, :] for ref in got]
    for b in range(nblk):
        put_stripes(stage, b * size, size, theta[b].astype(F32))
        part_ref[b] = stage[b * size + z] + got[b][rows:, :].astype(F32)
    terms = pair_terms(
        theta, 0.5 / math.sqrt(DH), e_refs, wq_ref, wk_ref, wv_ref, ws_ref, bias_ref, qk_ref, pool_ref
    )
    for b in range(nblk):
        put_stripes(stage, b * size, size, terms[b * rows : (b + 1) * rows])
        own_ref[b] = stage[b * size + z]
        for shift, send in enumerate(sends, 1):
            send[b] = stage[b * size + wrap(z + shift, size)].astype(BF16)


def sum_body(size, at_ref, own_home, own_away, *rest):
    home, away, out_ref = rest[: size - 1], rest[size - 1 : -1], rest[-1]
    for k in range(size):
        total = own_home[...] if k == 0 else home[k - 1][...].astype(F32)
        for d in range(1, size):
            by = (k - d) % size
            total = total + (own_away[d - 1] if by == 0 else away[by - 1][d - 1].astype(F32))
        out_ref[k] = total.astype(out_ref.dtype)


def last_body(size, nrep, at_ref, mix_ref, noise_ref, *rest):
    updated_ref, score_ref = rest[-2:]
    z, r = at_ref[0], at_ref[1]
    per = 3 if len(rest) == 2 + 3 * nrep else 2
    for shift in range(nrep):
        part = rest[per * shift]
        terms = rest[per * shift + 1 : per * (shift + 1)]
        rep = wrap(r + nrep - shift, nrep)
        for k in range(size):
            block = wrap(z + size - k, size)
            total = terms[0][k].astype(F32)
            for term in terms[1:]:
                total = total + term[k].astype(F32)
            score_ref[block, rep] = total
            updated_ref[block, rep] = (
                part[k] + mix_ref[0] * total + mix_ref[1] * noise_ref[block, rep]
            )


def on_device(
    particles,
    obs_embed,
    step_index,
    noise,
    w_query,
    w_key,
    w_value,
    w_time,
    w_score,
    prior_in,
    prior_time,
    prior_out,
):
    size, nrep, nhid = lax.axis_size("obs"), lax.axis_size("rep"), lax.axis_size("hid")
    at = jnp.stack([lax.axis_index("obs"), lax.axis_index("rep")]).astype(jnp.int32)
    features, delta = plan(step_index, w_time.shape[0])
    mix = jnp.stack([delta, jnp.sqrt(delta)])
    home = particles[0]
    block_rows, width = home.shape
    stripe = block_rows // size
    sub = stripe // nrep
    rows = size * sub
    heads = w_key.shape[1] // DH
    emb = obs_embed.shape[1]
    count = obs_embed.shape[0] * size * nrep - 1
    shifts = range(1, size)

    def shape(*dims, dtype=F32):
        return jax.ShapeDtypeStruct(dims, dtype)

    theta, mine, *sends = call(
        functools.partial(prep_body, size),
        "prep",
        [shape(rows, width, dtype=BF16), shape(sub, width)]
        + [shape(rows + sub, width, dtype=BF16) for _ in shifts],
        1,
        [pltpu.VMEM((rows, width), F32)],
    )(at, home.reshape(size, nrep, sub, width))
    seen = [obs_embed] + [passed_along(obs_embed, "rep", by) for by in range(1, nrep)]
    got = [passed_along(send, "obs", by) for by, send in zip(shifts, sends)]

    pair_flops = 4 * rows * heads * obs_embed.shape[0] * nrep * emb

    def scratch(blocks):
        return [
            pltpu.VMEM((blocks * heads * rows, emb), BF16),
            pltpu.VMEM((blocks * rows, heads * DH), F32),
            pltpu.VMEM((blocks * size, sub, width), F32),
        ]

    own_home, bias, *home_sends = call(
        functools.partial(home_body, size, nrep, float(count)),
        "home_block",
        [shape(sub, width), shape(heads, 128)] + [shape(sub, width, dtype=BF16) for _ in shifts],
        10 + nrep,
        scratch(1),
        pair_flops,
        32 << 20,
    )(
        at, theta, *seen, w_query, w_key, w_value, w_score, features, w_time, prior_in, prior_time, prior_out
    )
    from_home = [passed_along(send, "obs", by) for by, send in zip(shifts, home_sends)]
    own_away, part, *away_sends = call(
        functools.partial(away_body, size, nrep, size - 1),
        "away_blocks",
        [shape(size - 1, sub, width), shape(size - 1, sub, width)]
        + [shape(size - 1, sub, width, dtype=BF16) for _ in shifts],
        size - 1 + nrep + 5,
        scratch(size - 1),
        pair_flops * (size - 1),
        32 << 20,
    )(at, *got, *seen, w_query, w_key, w_value, w_score, bias)
    from_away = [passed_along(send, "obs", by) for by, send in zip(shifts, away_sends)]
    part = jnp.concatenate([mine[None], part], 0)
    parts = [part] + [passed_along(part, "rep", by) for by in range(1, nrep)]
    two = nhid == 2
    summed = call(
        functools.partial(sum_body, size),
        "sum_obs",
        shape(size, sub, width, dtype=BF16 if two else F32),
        2 * size,
    )(at, own_home, own_away, *from_home, *from_away)
    terms = []
    if two:
        pairs = [(h, r) for h in range(2) for r in range(nrep)]
        for by in range(nrep):
            for flip in range(2):
                if by == flip == 0:
                    moved = summed
                else:
                    perm = [
                        (h * nrep + r, (h ^ flip) * nrep + (r + by) % nrep) for h, r in pairs
                    ]
                    moved = lax.ppermute(summed, ("hid", "rep"), perm)
                terms.append(moved)
        terms = [terms[2 * by : 2 * by + 2] for by in range(nrep)]
    else:
        summed = lax.psum(summed, "hid")
        terms = [[summed]] + [[passed_along(summed, "rep", by)] for by in range(1, nrep)]
    tail = []
    for by in range(nrep):
        tail += [parts[by], *terms[by]]
    whole = shape(size, nrep, sub, width)
    updated, score = pl.pallas_call(
        functools.partial(last_body, size, nrep),
        name="last",
        out_shape=[whole, whole],
        in_specs=[smem(), smem()] + [spec()] * (1 + len(tail)),
        out_specs=[spec(), spec()],
    )(at, mix, noise.reshape(size, nrep, sub, width), *tail)
    return (updated.reshape(noise.shape), score.reshape(noise.shape))


def solution(mesh):
    in_specs = (
        P(("groups", "obs"), None, None),
        P(("groups", "obs", "rep"), None),
        P("groups"),
        P("groups", "obs", None),
        P(None, "hid"),
        P(None, "hid"),
        P(None, "hid"),
        P(None, "hid"),
        P("hid", None),
        P(None, "hid"),
        P(None, "hid"),
        P("hid", None),
    )
    out_specs = (P("groups", "obs", None), P("groups", "obs", None))
    return jax.shard_map(
        on_device, mesh=mesh, in_specs=in_specs, out_specs=out_specs, check_vma=False
    )
```

```python
import functools
import math

import jax
import jax.numpy as jnp
from jax import lax
from jax.experimental import pallas as pl
from jax.experimental.pallas import tpu as pltpu
from jax.sharding import PartitionSpec as P

DH = 128
STEPS = 64

SIG_LO = 0.05
SIG_HI = 1.0

F32 = jnp.float32
BF16 = jnp.bfloat16
NT = (((1,), (1,)), ((), ()))
TILE = 512


def passed_along(shard, axis, by):
    size = lax.axis_size(axis)
    return lax.ppermute(shard, axis, [(i, (i + by) % size) for i in range(size)])


def plan(step_index, feature_count):
    level = step_index[0].astype(F32)
    growth = math.log(SIG_HI / SIG_LO) / (STEPS - 1)
    sigma_now = SIG_LO * jnp.exp(growth * level)
    sigma_prev = SIG_LO * jnp.exp(growth * (level - 1.0))
    delta = sigma_now * sigma_now - sigma_prev * sigma_prev
    halves = feature_count // 2
    frequency = jnp.exp(-math.log(1000.0) / halves * jnp.arange(halves).astype(F32))
    angles = 10.0 * jnp.log(sigma_now) * frequency
    features = jnp.concatenate([jnp.sin(angles), jnp.cos(angles)])[None, :].astype(BF16)
    return (features, delta)


def dot(a, b):
    return jnp.dot(a, b, preferred_element_type=F32)


def wrap(index, size):
    return lax.rem(index, jnp.int32(size))


def halves_of(x):
    high = x.astype(BF16)
    return high, (x - high.astype(F32)).astype(BF16)


def split_dot(x, weight):
    rows = x.shape[0]
    both = dot(jnp.concatenate(halves_of(x), 0), weight)
    return both[:rows] + both[rows:]


def half_silu(y):
    return y + y * jnp.tanh(y)


def put_stripes(stage, first, count, values):
    sub = stage.shape[1]
    for s in range(count):
        stage[first + s] = values[s * sub : (s + 1) * sub]


def spec():
    return pl.BlockSpec(memory_space=pltpu.VMEM)


def call(body, name, out_shape, in_specs, scratch=(), flops=0, limit=4):
    return pl.pallas_call(
        body,
        name=name,
        out_shape=out_shape,
        in_specs=in_specs,
        out_specs=jax.tree.map(lambda _: spec(), out_shape),
        scratch_shapes=list(scratch),
        cost_estimate=pl.CostEstimate(flops=flops, bytes_accessed=flops // 1000, transcendentals=0),
        compiler_params=pltpu.CompilerParams(vmem_limit_bytes=limit << 20),
    )


def prep_body(size, home_ref, theta_ref, mine_ref, *rest):
    sends, stage = rest[:-1], rest[-1]
    z, r = lax.axis_index("obs"), lax.axis_index("rep")
    sub = home_ref.shape[2]
    for s in range(size):
        stage[s * sub : (s + 1) * sub, :] = home_ref[s, r]
    theta = stage[...].astype(BF16)
    theta_ref[...] = theta
    mine_ref[...] = home_ref[z, r]
    rows = theta.shape[0]
    for shift, send in enumerate(sends, 1):
        left = home_ref[wrap(z + shift, size), r]
        send[:rows, :] = theta
        send[rows:, :] = halves_of(left)[1]


def pair_terms(
    theta, scale, e_refs, wq_ref, wk_ref, wv_ref, ws_ref, bias_ref, qk_ref, pool_ref, ready=lambda ref: None
):
    blocks = len(theta)
    rows = theta[0].shape[0]
    heads = wk_ref.shape[1] // DH
    every = theta[0] if blocks == 1 else jnp.concatenate(theta, 0)
    ready(wq_ref)
    queries = dot(every, wq_ref[...]).astype(BF16)
    ready(wk_ref)
    for h in range(heads):
        cols = slice(h * DH, (h + 1) * DH)
        turned = lax.dot_general(queries[:, cols], wk_ref[:, cols], NT, preferred_element_type=F32)
        turned = (turned * scale).astype(BF16)
        for b in range(blocks):
            at = (b * heads + h) * rows
            qk_ref[at : at + rows, :] = turned[b * rows : (b + 1) * rows]

    def weights(scores):
        parts = []
        for h in range(heads):
            bias = jnp.tile(bias_ref[h : h + 1, :], (1, scores.shape[1] // 128))
            parts.append(half_silu(scores[h * rows : (h + 1) * rows] + bias).astype(BF16))
        return jnp.concatenate(parts, 0)

    for b in range(blocks):
        span = slice(b * heads * rows, (b + 1) * heads * rows)
        total = None
        for e_ref in e_refs:
            tile = math.gcd(TILE, e_ref.shape[0])
            ready(e_ref)
            for j in range(e_ref.shape[0] // tile):
                seen = e_ref[j * tile : (j + 1) * tile, :]
                scores = lax.dot_general(qk_ref[span, :], seen, NT, preferred_element_type=F32)
                term = dot(weights(scores), seen)
                total = term if total is None else total + term
        ready(wv_ref)
        for h in range(heads):
            cols = slice(h * DH, (h + 1) * DH)
            pool_ref[b * rows : (b + 1) * rows, cols] = split_dot(
                total[h * rows : (h + 1) * rows], wv_ref[:, cols]
            )
    ready(ws_ref)
    return split_dot(pool_ref[...], ws_ref[...])


def home_body(size, nrep, count, *refs):
    n = 10 + nrep
    hbm, (terms_ref, bias_ref), held = refs[:n], refs[n : n + 2], refs[n + 2 : 2 * n + 2]
    qk_ref, pool_ref, sems = refs[2 * n + 2 :]
    copies = [pltpu.make_async_copy(hbm[i], held[i], sems.at[i]) for i in range(n)]
    for copy in copies:
        copy.start()

    def ready(ref):
        for copy, own in zip(copies, held):
            if own is ref:
                copy.wait()

    theta_ref, feat_ref, wt_ref, wq_ref, wk_ref = held[:5]
    e_refs = held[5 : 5 + nrep]
    wv_ref, ws_ref, pt_ref, pin_ref, pout_ref = held[5 + nrep :]
    heads = wk_ref.shape[1] // DH
    for ref in (theta_ref, feat_ref, wt_ref):
        ready(ref)
    feat = jnp.broadcast_to(feat_ref[...], (16, feat_ref.shape[1]))
    head_bias = dot(feat, wt_ref[...]) * 0.5
    for h in range(heads):
        bias_ref[h : h + 1, :] = jnp.broadcast_to(head_bias[0:1, h : h + 1], (1, 128))
    theta = theta_ref[...]
    terms = pair_terms(
        [theta],
        0.5 / math.sqrt(DH),
        e_refs,
        wq_ref,
        wk_ref,
        wv_ref,
        ws_ref,
        bias_ref,
        qk_ref,
        pool_ref,
        ready,
    )
    for ref in (pt_ref, pin_ref, pout_ref):
        ready(ref)
    pre = dot(theta, pin_ref[...]) + dot(feat, pt_ref[...])[0:1]
    prior = dot(half_silu(0.5 * pre).astype(BF16), pout_ref[...])
    put_stripes(terms_ref, 0, size, terms - count * prior)


def away_body(size, nrep, *refs):
    nblk = size - 1
    terms_ref, mine_ref = refs[:2]
    got, rest = refs[2 : 2 + nblk], refs[2 + nblk :]
    e_refs, rest = rest[:nrep], rest[nrep:]
    wq_ref, wk_ref, wv_ref, ws_ref, bias_ref = rest[:5]
    own_ref, part_ref = rest[5:7]
    sends = rest[7 : 7 + nblk]
    qk_ref, pool_ref, stage = rest[7 + nblk :]
    z = lax.axis_index("obs")
    sub = own_ref.shape[1]
    rows = size * sub
    theta = [ref[:rows, :] for ref in got]
    part_ref[0] = mine_ref[...]
    for b in range(nblk):
        put_stripes(stage, b * size, size, theta[b].astype(F32))
        part_ref[b + 1] = stage[b * size + z] + got[b][rows:, :].astype(F32)
    terms = pair_terms(
        theta, 0.5 / math.sqrt(DH), e_refs, wq_ref, wk_ref, wv_ref, ws_ref, bias_ref, qk_ref, pool_ref
    )
    own_ref[0] = terms_ref[z]
    for shift, send in enumerate(sends, 1):
        send[0] = terms_ref[wrap(z + shift, size)].astype(BF16)
    for b in range(nblk):
        put_stripes(stage, b * size, size, terms[b * rows : (b + 1) * rows])
        own_ref[b + 1] = stage[b * size + z]
        for shift, send in enumerate(sends, 1):
            send[b + 1] = stage[b * size + wrap(z + shift, size)].astype(BF16)


def sum_body(size, own_ref, *rest):
    away, out_ref = rest[:-1], rest[-1]
    for k in range(size):
        total = own_ref[k]
        for by in range(1, size):
            total = total + away[by - 1][(k - by) % size].astype(F32)
        out_ref[k] = total.astype(out_ref.dtype)


def join_body(size, *refs):
    terms, part_ref, out_ref = refs[:-2], refs[-2], refs[-1]
    for k in range(size):
        total = terms[0][k].astype(F32)
        for term in terms[1:]:
            total = total + term[k].astype(F32)
        out_ref[k] = total
        out_ref[size + k] = part_ref[k]


def last_body(size, nrep, mix_ref, noise_ref, *rest):
    joined, (updated_ref, score_ref) = rest[:nrep], rest[nrep:]
    z, r = lax.axis_index("obs"), lax.axis_index("rep")
    reach = noise_ref.shape[-1] // 128
    delta = jnp.tile(mix_ref[0:1, :], (1, reach))
    root = jnp.tile(mix_ref[1:2, :], (1, reach))
    for shift in range(nrep):
        rep = wrap(r + nrep - shift, nrep)
        for k in range(size):
            block = wrap(z + size - k, size)
            total = joined[shift][k]
            score_ref[block, rep] = total
            updated_ref[block, rep] = (
                joined[shift][size + k] + delta * total + root * noise_ref[block, rep]
            )


def on_device(
    particles,
    obs_embed,
    step_index,
    noise,
    w_query,
    w_key,
    w_value,
    w_time,
    w_score,
    prior_in,
    prior_time,
    prior_out,
):
    size, nrep, nhid = lax.axis_size("obs"), lax.axis_size("rep"), lax.axis_size("hid")
    features, delta = plan(step_index, w_time.shape[0])
    mix = jnp.broadcast_to(jnp.stack([delta, jnp.sqrt(delta)])[:, None], (2, 128))
    home = particles[0]
    block_rows, width = home.shape
    stripe = block_rows // size
    sub = stripe // nrep
    rows = size * sub
    heads = w_key.shape[1] // DH
    emb = obs_embed.shape[1]
    count = obs_embed.shape[0] * size * nrep - 1
    shifts = range(1, size)

    def shape(*dims, dtype=F32):
        return jax.ShapeDtypeStruct(dims, dtype)

    def scratch(blocks):
        return [
            pltpu.VMEM((blocks * heads * rows, emb), BF16),
            pltpu.VMEM((blocks * rows, heads * DH), F32),
        ]

    seen = [obs_embed] + [passed_along(obs_embed, "rep", by) for by in range(1, nrep)]
    theta, mine, *sends = call(
        functools.partial(prep_body, size),
        "prep",
        [shape(rows, width, dtype=BF16), shape(sub, width)]
        + [shape(rows + sub, width, dtype=BF16) for _ in shifts],
        [spec()],
        [pltpu.VMEM((rows, width), F32)],
    )(home.reshape(size, nrep, sub, width))
    got = [passed_along(send, "obs", by) for by, send in zip(shifts, sends)]

    pair_flops = 4 * rows * heads * obs_embed.shape[0] * nrep * emb
    operands = [theta, features, w_time, w_query, w_key, *seen, w_value, w_score]
    operands += [prior_time, prior_in, prior_out]
    terms, bias = call(
        functools.partial(home_body, size, nrep, float(count)),
        "home_block",
        [shape(size, sub, width), shape(heads, 128)],
        [pl.BlockSpec(memory_space=pl.ANY)] * len(operands),
        [pltpu.VMEM(x.shape, x.dtype) for x in operands]
        + scratch(1)
        + [pltpu.SemaphoreType.DMA((len(operands),))],
        pair_flops,
        24,
    )(*operands)
    own, part, *leave = call(
        functools.partial(away_body, size, nrep),
        "away_blocks",
        [shape(size, sub, width), shape(size, sub, width)]
        + [shape(size, sub, width, dtype=BF16) for _ in shifts],
        [spec()] * (2 + size - 1 + nrep + 5),
        scratch(size - 1) + [pltpu.VMEM(((size - 1) * size, sub, width), F32)],
        pair_flops * (size - 1),
        24,
    )(terms, mine, *got, *seen, w_query, w_key, w_value, w_score, bias)
    arrived = [passed_along(send, "obs", by) for by, send in zip(shifts, leave)]
    two = nhid == 2
    summed = call(
        functools.partial(sum_body, size),
        "sum_obs",
        shape(size, sub, width, dtype=BF16 if two else F32),
        [spec()] * size,
    )(own, *arrived)
    if two:
        partial_sums = [summed, passed_along(summed, "hid", 1)]
    else:
        partial_sums = [lax.psum(summed, "hid")]
    joined = call(
        functools.partial(join_body, size),
        "join",
        shape(2 * size, sub, width),
        [spec()] * (len(partial_sums) + 1),
    )(*partial_sums, part)
    joined = [joined] + [passed_along(joined, "rep", by) for by in range(1, nrep)]
    whole = shape(size, nrep, sub, width)
    updated, score = call(
        functools.partial(last_body, size, nrep),
        "last",
        [whole, whole],
        [spec()] * (2 + nrep),
    )(mix, noise.reshape(size, nrep, sub, width), *joined)
    return (updated.reshape(noise.shape), score.reshape(noise.shape))


def solution(mesh):
    in_specs = (
        P(("groups", "obs"), None, None),
        P(("groups", "obs", "rep"), None),
        P("groups"),
        P("groups", "obs", None),
        P(None, "hid"),
        P(None, "hid"),
        P(None, "hid"),
        P(None, "hid"),
        P("hid", None),
        P(None, "hid"),
        P(None, "hid"),
        P("hid", None),
    )
    out_specs = (P("groups", "obs", None), P("groups", "obs", None))
    return jax.shard_map(
        on_device, mesh=mesh, in_specs=in_specs, out_specs=out_specs, check_vma=False
    )
```

```python
import functools
import math

import jax
import jax.numpy as jnp
from jax import lax
from jax.experimental import pallas as pl
from jax.experimental.pallas import tpu as pltpu
from jax.sharding import PartitionSpec as P

DH = 128
STEPS = 64

SIG_LO = 0.05
SIG_HI = 1.0

F32 = jnp.float32
BF16 = jnp.bfloat16
NT = (((1,), (1,)), ((), ()))
TILE = 512


def partner(index, by, size):
    if size & (size - 1) == 0:
        return index ^ by
    return (index + by) % size


def source(index, by, size):
    return partner(index, by if size & (size - 1) == 0 else size - by, size)


def passed_along(shard, axis, by):
    size = lax.axis_size(axis)
    return lax.ppermute(shard, axis, [(i, partner(i, by, size)) for i in range(size)])


def plan(level, feature_count):
    growth = math.log(SIG_HI / SIG_LO) / (STEPS - 1)
    sigma_now = SIG_LO * jnp.exp(growth * level)
    sigma_prev = SIG_LO * jnp.exp(growth * (level - 1.0))
    delta = sigma_now * sigma_now - sigma_prev * sigma_prev
    halves = feature_count // 2
    lane = lax.broadcasted_iota(jnp.int32, (1, halves), 1).astype(F32)
    angles = 10.0 * jnp.log(sigma_now[:, :1]) * jnp.exp(-math.log(1000.0) / halves * lane)
    features = jnp.concatenate([jnp.sin(angles), jnp.cos(angles)], 1).astype(BF16)
    return (features, delta)


def dot(a, b):
    return jnp.dot(a, b, preferred_element_type=F32)


def halves_of(x):
    high = x.astype(BF16)
    return high, (x - high.astype(F32)).astype(BF16)


def split_dot(x, weight):
    rows = x.shape[0]
    both = dot(jnp.concatenate(halves_of(x), 0), weight)
    return both[:rows] + both[rows:]


def half_silu(y):
    return y + y * jnp.tanh(y)


def put_stripes(stage, first, count, values):
    sub = stage.shape[1]
    for s in range(count):
        stage[first + s] = values[s * sub : (s + 1) * sub]


def spec():
    return pl.BlockSpec(memory_space=pltpu.VMEM)


def in_hbm(x):
    return pltpu.with_memory_space_constraint(x, pltpu.HBM)


def call(body, name, out_shape, in_specs, scratch=(), flops=0, limit=4):
    return pl.pallas_call(
        body,
        name=name,
        out_shape=out_shape,
        in_specs=in_specs,
        out_specs=jax.tree.map(lambda _: spec(), out_shape),
        scratch_shapes=list(scratch),
        cost_estimate=pl.CostEstimate(flops=flops, bytes_accessed=flops // 1000, transcendentals=0),
        compiler_params=pltpu.CompilerParams(vmem_limit_bytes=limit << 20),
    )


def prep_body(size, home_ref, theta_ref, mine_ref, *rest):
    sends, (held, stage, sem) = rest[:-3], rest[-3:]
    z, r = lax.axis_index("obs"), lax.axis_index("rep")
    sub = held.shape[1]
    copy = pltpu.make_async_copy(home_ref.at[:, r], held, sem)
    copy.start()
    copy.wait()
    for s in range(size):
        stage[s * sub : (s + 1) * sub, :] = held[s]
    theta = stage[...].astype(BF16)
    theta_ref[...] = theta
    mine_ref[...] = held[z]
    rows = theta.shape[0]
    for by, send in enumerate(sends, 1):
        send[:rows, :] = theta
        send[rows:, :] = halves_of(held[partner(z, by, size)])[1]


def pair_terms(
    theta, scale, e_refs, wq_ref, wk_ref, wv_ref, ws_ref, bias_ref, qk_ref, pool_ref, ready=lambda ref: None
):
    blocks = len(theta)
    rows = theta[0].shape[0]
    heads = wk_ref.shape[1] // DH
    every = theta[0] if blocks == 1 else jnp.concatenate(theta, 0)
    ready(wq_ref)
    queries = dot(every, wq_ref[...]).astype(BF16)
    ready(wk_ref)
    for h in range(heads):
        cols = slice(h * DH, (h + 1) * DH)
        turned = lax.dot_general(queries[:, cols], wk_ref[:, cols], NT, preferred_element_type=F32)
        turned = (turned * scale).astype(BF16)
        for b in range(blocks):
            at = (b * heads + h) * rows
            qk_ref[at : at + rows, :] = turned[b * rows : (b + 1) * rows]

    def weights(scores):
        parts = []
        for h in range(heads):
            bias = jnp.tile(bias_ref[h : h + 1, :], (1, scores.shape[1] // 128))
            parts.append(half_silu(scores[h * rows : (h + 1) * rows] + bias).astype(BF16))
        return jnp.concatenate(parts, 0)

    for b in range(blocks):
        span = slice(b * heads * rows, (b + 1) * heads * rows)
        total = None
        for e_ref in e_refs:
            tile = math.gcd(TILE, e_ref.shape[0])
            ready(e_ref)
            for j in range(e_ref.shape[0] // tile):
                seen = e_ref[j * tile : (j + 1) * tile, :]
                scores = lax.dot_general(qk_ref[span, :], seen, NT, preferred_element_type=F32)
                term = dot(weights(scores), seen)
                total = term if total is None else total + term
        ready(wv_ref)
        for h in range(heads):
            cols = slice(h * DH, (h + 1) * DH)
            pool_ref[b * rows : (b + 1) * rows, cols] = split_dot(
                total[h * rows : (h + 1) * rows], wv_ref[:, cols]
            )
    ready(ws_ref)
    return split_dot(pool_ref[...], ws_ref[...])


def home_body(size, nrep, count, level_ref, theta_ref, *refs):
    others, refs = refs[: nrep - 1], refs[nrep - 1 :]
    n = 9
    hbm, (terms_ref, bias_ref, mix_ref), held = refs[:n], refs[n : n + 3], refs[n + 3 : 2 * n + 3]
    qk_ref, pool_ref, sems = refs[2 * n + 3 :]
    copies = [pltpu.make_async_copy(hbm[i], held[i], sems.at[i]) for i in range(n)]
    for copy in copies:
        copy.start()

    def ready(ref):
        for copy, own in zip(copies, held):
            if own is ref:
                copy.wait()

    wt_ref, wq_ref, wk_ref, e_ref, wv_ref, ws_ref, pt_ref, pin_ref, pout_ref = held
    e_refs = [e_ref, *others]
    heads = wk_ref.shape[1] // DH
    level = jnp.full((1, 128), level_ref[0], jnp.int32).astype(F32)
    features, delta = plan(level, wt_ref.shape[1])
    mix_ref[0:1, :] = delta
    mix_ref[1:2, :] = jnp.sqrt(delta)
    feat = jnp.broadcast_to(features, (16, features.shape[1]))
    ready(wt_ref)
    head_bias = lax.dot_general(wt_ref[...], feat, NT, preferred_element_type=F32) * 0.5
    bias_ref[...] = jnp.broadcast_to(head_bias[:, 0:1], (heads, 128))
    theta = theta_ref[...]
    terms = pair_terms(
        [theta],
        0.5 / math.sqrt(DH),
        e_refs,
        wq_ref,
        wk_ref,
        wv_ref,
        ws_ref,
        bias_ref,
        qk_ref,
        pool_ref,
        ready,
    )
    for ref in (pt_ref, pin_ref, pout_ref):
        ready(ref)
    pre = dot(theta, pin_ref[...]) + dot(feat, pt_ref[...])[0:1]
    prior = dot(half_silu(0.5 * pre).astype(BF16), pout_ref[...])
    put_stripes(terms_ref, 0, size, terms - count * prior)


def away_body(size, nrep, *refs):
    nblk = size - 1
    terms_ref, mine_ref = refs[:2]
    got, rest = refs[2 : 2 + nblk], refs[2 + nblk :]
    e_refs, rest = rest[:nrep], rest[nrep:]
    wq_ref, wk_ref, wv_ref, ws_ref, bias_ref = rest[:5]
    own_ref, part_ref = rest[5:7]
    sends = rest[7 : 7 + nblk]
    qk_ref, pool_ref, stage = rest[7 + nblk :]
    z = lax.axis_index("obs")
    sub = own_ref.shape[1]
    rows = size * sub
    theta = [ref[:rows, :] for ref in got]
    part_ref[0] = mine_ref[...]
    for b in range(nblk):
        put_stripes(stage, b * size, size, theta[b].astype(F32))
        part_ref[b + 1] = stage[b * size + z] + got[b][rows:, :].astype(F32)
    terms = pair_terms(
        theta, 0.5 / math.sqrt(DH), e_refs, wq_ref, wk_ref, wv_ref, ws_ref, bias_ref, qk_ref, pool_ref
    )
    own_ref[0] = terms_ref[z]
    for by, send in enumerate(sends, 1):
        send[0] = terms_ref[partner(z, by, size)].astype(BF16)
    for b in range(nblk):
        put_stripes(stage, b * size, size, terms[b * rows : (b + 1) * rows])
        own_ref[b + 1] = stage[b * size + z]
        for by, send in enumerate(sends, 1):
            send[b + 1] = stage[b * size + partner(z, by, size)].astype(BF16)


def sum_body(size, own_ref, *rest):
    away, out_ref = rest[:-1], rest[-1]
    for k in range(size):
        total = own_ref[k]
        for by in range(1, size):
            total = total + away[by - 1][source(k, by, size)].astype(F32)
        out_ref[k] = total.astype(out_ref.dtype)


def join_body(size, *refs):
    terms, part_ref, out_ref = refs[:-2], refs[-2], refs[-1]
    for k in range(size):
        total = terms[0][k].astype(F32)
        for term in terms[1:]:
            total = total + term[k].astype(F32)
        out_ref[k] = total
        out_ref[size + k] = part_ref[k]


def last_body(size, nrep, mix_ref, noise_ref, *rest):
    joined, (updated_ref, score_ref) = rest[:nrep], rest[nrep:]
    z, r = lax.axis_index("obs"), lax.axis_index("rep")
    reach = noise_ref.shape[-1] // 128
    delta = jnp.tile(mix_ref[0:1, :], (1, reach))
    root = jnp.tile(mix_ref[1:2, :], (1, reach))
    for away in range(nrep):
        rep = source(r, away, nrep)
        for k in range(size):
            block = source(z, k, size)
            total = joined[away][k]
            score_ref[block, rep] = total
            updated_ref[block, rep] = (
                joined[away][size + k] + delta * total + root * noise_ref[block, rep]
            )


def on_device(
    particles,
    obs_embed,
    step_index,
    noise,
    w_query,
    w_key,
    w_value,
    w_time,
    w_score,
    prior_in,
    prior_time,
    prior_out,
):
    size, nrep, nhid = lax.axis_size("obs"), lax.axis_size("rep"), lax.axis_size("hid")
    home = particles[0]
    block_rows, width = home.shape
    stripe = block_rows // size
    sub = stripe // nrep
    rows = size * sub
    heads = w_key.shape[1] // DH
    emb = obs_embed.shape[1]
    count = obs_embed.shape[0] * size * nrep - 1
    shifts = range(1, size)

    def shape(*dims, dtype=F32):
        return jax.ShapeDtypeStruct(dims, dtype)

    def scratch(blocks):
        return [
            pltpu.VMEM((blocks * heads * rows, emb), BF16),
            pltpu.VMEM((blocks * rows, heads * DH), F32),
        ]

    seen = [obs_embed] + [passed_along(obs_embed, "rep", by) for by in range(1, nrep)]
    theta, mine, *sends = call(
        functools.partial(prep_body, size),
        "prep",
        [shape(rows, width, dtype=BF16), shape(sub, width)]
        + [shape(rows + sub, width, dtype=BF16) for _ in shifts],
        [pl.BlockSpec(memory_space=pltpu.HBM)],
        [
            pltpu.VMEM((size, sub, width), F32),
            pltpu.VMEM((rows, width), F32),
            pltpu.SemaphoreType.DMA(()),
        ],
    )(in_hbm(home.reshape(size, nrep, sub, width)))
    got = [passed_along(send, "obs", by) for by, send in zip(shifts, sends)]

    pair_flops = 4 * rows * heads * obs_embed.shape[0] * nrep * emb
    operands = [w_time.T, w_query, w_key, obs_embed, w_value, w_score]
    operands = [in_hbm(x) for x in operands + [prior_time, prior_in, prior_out]]
    terms, bias, mix = call(
        functools.partial(home_body, size, nrep, float(count)),
        "home_block",
        [shape(size, sub, width), shape(heads, 128), shape(2, 128)],
        [pl.BlockSpec(memory_space=pltpu.SMEM)]
        + [spec()] * nrep
        + [pl.BlockSpec(memory_space=pltpu.HBM)] * len(operands),
        [pltpu.VMEM(x.shape, x.dtype) for x in operands]
        + scratch(1)
        + [pltpu.SemaphoreType.DMA((len(operands),))],
        pair_flops,
        24,
    )(step_index, theta, *seen[1:], *operands)
    own, part, *leave = call(
        functools.partial(away_body, size, nrep),
        "away_blocks",
        [shape(size, sub, width), shape(size, sub, width)]
        + [shape(size, sub, width, dtype=BF16) for _ in shifts],
        [spec()] * (2 + size - 1 + nrep + 5),
        scratch(size - 1) + [pltpu.VMEM(((size - 1) * size, sub, width), F32)],
        pair_flops * (size - 1),
        24,
    )(terms, mine, *got, *seen, w_query, w_key, w_value, w_score, bias)
    arrived = [passed_along(send, "obs", by) for by, send in zip(shifts, leave)]
    two = nhid == 2
    summed = call(
        functools.partial(sum_body, size),
        "sum_obs",
        shape(size, sub, width, dtype=BF16 if two else F32),
        [spec()] * size,
    )(own, *arrived)
    if two:
        partial_sums = [summed, passed_along(summed, "hid", 1)]
    else:
        partial_sums = [lax.psum(summed, "hid")]
    joined = call(
        functools.partial(join_body, size),
        "join",
        shape(2 * size, sub, width),
        [spec()] * (len(partial_sums) + 1),
    )(*partial_sums, part)
    joined = [joined] + [passed_along(joined, "rep", by) for by in range(1, nrep)]
    whole = shape(size, nrep, sub, width)
    updated, score = call(
        functools.partial(last_body, size, nrep),
        "last",
        [whole, whole],
        [spec()] * (2 + nrep),
    )(mix, noise.reshape(size, nrep, sub, width), *joined)
    return (updated.reshape(noise.shape), score.reshape(noise.shape))


def solution(mesh):
    in_specs = (
        P(("groups", "obs"), None, None),
        P(("groups", "obs", "rep"), None),
        P("groups"),
        P("groups", "obs", None),
        P(None, "hid"),
        P(None, "hid"),
        P(None, "hid"),
        P(None, "hid"),
        P("hid", None),
        P(None, "hid"),
        P(None, "hid"),
        P("hid", None),
    )
    out_specs = (P("groups", "obs", None), P("groups", "obs", None))
    return jax.shard_map(
        on_device, mesh=mesh, in_specs=in_specs, out_specs=out_specs, check_vma=False
    )
```

```python
import functools
import math

import jax
import jax.numpy as jnp
from jax import lax
from jax.experimental import pallas as pl
from jax.experimental.pallas import tpu as pltpu
from jax.sharding import PartitionSpec as P

DH = 128
STEPS = 64

SIG_LO = 0.05
SIG_HI = 1.0

F32 = jnp.float32
BF16 = jnp.bfloat16
NT = (((1,), (1,)), ((), ()))
TILE = 512


def partner(index, by, size):
    if size & (size - 1) == 0:
        return index ^ by
    return (index + by) % size


def source(index, by, size):
    return partner(index, by if size & (size - 1) == 0 else size - by, size)


def passed_along(shard, axis, by):
    size = lax.axis_size(axis)
    return lax.ppermute(shard, axis, [(i, partner(i, by, size)) for i in range(size)])


def plan(level, feature_count):
    growth = math.log(SIG_HI / SIG_LO) / (STEPS - 1)
    sigma_now = SIG_LO * jnp.exp(growth * level)
    sigma_prev = SIG_LO * jnp.exp(growth * (level - 1.0))
    delta = sigma_now * sigma_now - sigma_prev * sigma_prev
    halves = feature_count // 2
    lane = lax.broadcasted_iota(jnp.int32, (1, halves), 1).astype(F32)
    angles = 10.0 * jnp.log(sigma_now[:, :1]) * jnp.exp(-math.log(1000.0) / halves * lane)
    features = jnp.concatenate([jnp.sin(angles), jnp.cos(angles)], 1).astype(BF16)
    return (features, delta)


def dot(a, b):
    return jnp.dot(a, b, preferred_element_type=F32)


def halves_of(x):
    high = x.astype(BF16)
    return high, (x - high.astype(F32)).astype(BF16)


def split_dot(x, weight):
    rows = x.shape[0]
    both = dot(jnp.concatenate(halves_of(x), 0), weight)
    return both[:rows] + both[rows:]


def half_silu(y):
    return y + y * jnp.tanh(y)


def put_stripes(stage, first, count, values):
    sub = stage.shape[1]
    for s in range(count):
        stage[first + s] = values[s * sub : (s + 1) * sub]


def spec():
    return pl.BlockSpec(memory_space=pltpu.VMEM)


def in_hbm(x):
    return pltpu.with_memory_space_constraint(x, pltpu.HBM)


def call(body, name, out_shape, in_specs, scratch=(), flops=0, limit=4):
    return pl.pallas_call(
        body,
        name=name,
        out_shape=out_shape,
        in_specs=in_specs,
        out_specs=jax.tree.map(lambda _: spec(), out_shape),
        scratch_shapes=list(scratch),
        cost_estimate=pl.CostEstimate(flops=flops, bytes_accessed=flops // 1000, transcendentals=0),
        compiler_params=pltpu.CompilerParams(vmem_limit_bytes=limit << 20),
    )


def prep_body(size, early, home_ref, *refs):
    weights, refs = refs[:early], refs[early:]
    (theta_ref, mine_ref), refs = refs[:2], refs[2:]
    sends, refs = refs[: size - 1], refs[size - 1 :]
    copied, (held, stage, sems) = refs[:early], refs[early:]
    z, r = lax.axis_index("obs"), lax.axis_index("rep")
    sub = held.shape[1]
    copy = pltpu.make_async_copy(home_ref.at[:, r], held, sems.at[early])
    copy.start()
    others = [pltpu.make_async_copy(weights[i], copied[i], sems.at[i]) for i in range(early)]
    for other in others:
        other.start()
    copy.wait()
    for s in range(size):
        stage[s * sub : (s + 1) * sub, :] = held[s]
    theta = stage[...].astype(BF16)
    theta_ref[...] = theta
    mine_ref[...] = held[z]
    rows = theta.shape[0]
    for by, send in enumerate(sends, 1):
        send[:rows, :] = theta
        send[rows:, :] = halves_of(held[partner(z, by, size)])[1]
    for other in others:
        other.wait()


def pair_terms(
    theta, scale, e_refs, wq_ref, wk_ref, wv_ref, ws_ref, bias_ref, qk_ref, pool_ref, ready=lambda ref: None
):
    blocks = len(theta)
    rows = theta[0].shape[0]
    heads = wk_ref.shape[1] // DH
    every = theta[0] if blocks == 1 else jnp.concatenate(theta, 0)
    ready(wq_ref)
    queries = dot(every, wq_ref[...]).astype(BF16)
    ready(wk_ref)
    for h in range(heads):
        cols = slice(h * DH, (h + 1) * DH)
        turned = lax.dot_general(queries[:, cols], wk_ref[:, cols], NT, preferred_element_type=F32)
        turned = (turned * scale).astype(BF16)
        for b in range(blocks):
            at = (b * heads + h) * rows
            qk_ref[at : at + rows, :] = turned[b * rows : (b + 1) * rows]

    def weights(scores):
        parts = []
        for h in range(heads):
            bias = jnp.tile(bias_ref[h : h + 1, :], (1, scores.shape[1] // 128))
            parts.append(half_silu(scores[h * rows : (h + 1) * rows] + bias).astype(BF16))
        return jnp.concatenate(parts, 0)

    for b in range(blocks):
        span = slice(b * heads * rows, (b + 1) * heads * rows)
        total = None
        for e_ref in e_refs:
            tile = math.gcd(TILE, e_ref.shape[0])
            ready(e_ref)
            for j in range(e_ref.shape[0] // tile):
                seen = e_ref[j * tile : (j + 1) * tile, :]
                scores = lax.dot_general(qk_ref[span, :], seen, NT, preferred_element_type=F32)
                term = dot(weights(scores), seen)
                total = term if total is None else total + term
        ready(wv_ref)
        for h in range(heads):
            cols = slice(h * DH, (h + 1) * DH)
            pool_ref[b * rows : (b + 1) * rows, cols] = split_dot(
                total[h * rows : (h + 1) * rows], wv_ref[:, cols]
            )
    ready(ws_ref)
    return split_dot(pool_ref[...], ws_ref[...])


def near_body(size, nrep, heads, feats, *refs):
    level_ref, theta_ref, got_ref, wq_ref, wk_ref = refs[:5]
    others, refs = refs[5 : 4 + nrep], refs[4 + nrep :]
    hbm, (terms_ref, bias_ref, mix_ref, feat_ref, *held) = refs[:4], refs[4:11]
    wt_ref, qk_ref, pool_ref, sems = refs[11:]
    held = [wt_ref, *held]
    copies = [pltpu.make_async_copy(hbm[i], held[i], sems.at[i]) for i in range(4)]
    for copy in copies:
        copy.start()
    waiting = dict(zip(map(id, held), copies))

    def ready(ref):
        if id(ref) in waiting:
            waiting.pop(id(ref)).wait()

    e_ref, wv_ref, ws_ref = held[1:]
    features, delta = plan(level_ref[...], feats)
    mix_ref[0:1, :] = delta
    mix_ref[1:2, :] = jnp.sqrt(delta)
    feat = jnp.broadcast_to(features, (16, feats))
    feat_ref[...] = feat
    ready(wt_ref)
    head_bias = lax.dot_general(wt_ref[...], feat, NT, preferred_element_type=F32) * 0.5
    bias_ref[...] = jnp.broadcast_to(head_bias[:, 0:1], (heads, 128))
    rows = theta_ref.shape[0]
    terms = pair_terms(
        [theta_ref[...], got_ref[:rows, :]],
        0.5 / math.sqrt(DH),
        [*others, e_ref],
        wq_ref,
        wk_ref,
        wv_ref,
        ws_ref,
        bias_ref,
        qk_ref,
        pool_ref,
        ready,
    )
    put_stripes(terms_ref, 0, 2 * size, terms)


def far_body(size, nrep, *refs):
    nblk = size - 2
    terms_ref, mine_ref = refs[:2]
    got, rest = refs[2 : 1 + size], refs[1 + size :]
    e_refs, rest = rest[:nrep], rest[nrep:]
    wq_ref, wk_ref, wv_ref, ws_ref, bias_ref = rest[:5]
    own_ref, part_ref = rest[5:7]
    sends = rest[7 : 6 + size]
    qk_ref, pool_ref, stage = rest[6 + size :]
    z = lax.axis_index("obs")
    sub = own_ref.shape[1]
    rows = size * sub
    part_ref[0] = mine_ref[...]
    for b in range(1, size):
        put_stripes(stage, 0, size, got[b - 1][:rows, :].astype(F32))
        part_ref[b] = stage[z] + got[b - 1][rows:, :].astype(F32)
    terms = pair_terms(
        [ref[:rows, :] for ref in got[1:]],
        0.5 / math.sqrt(DH),
        e_refs,
        wq_ref,
        wk_ref,
        wv_ref,
        ws_ref,
        bias_ref,
        qk_ref,
        pool_ref,
    )
    put_stripes(stage, 0, nblk * size, terms)
    for k in range(size):
        held, first = (terms_ref, k * size) if k < 2 else (stage, (k - 2) * size)
        own_ref[k] = held[first + z]
        for by, send in enumerate(sends, 1):
            send[k] = held[first + partner(z, by, size)].astype(BF16)


def prior_body(size, count, part_ref, feat_ref, pt_ref, pin_ref, pout_ref, out_ref, stage):
    sub = part_ref.shape[1]
    for k in range(size):
        stage[k * sub : (k + 1) * sub, :] = part_ref[k]
    pre = dot(stage[...].astype(BF16), pin_ref[...]) + dot(feat_ref[...], pt_ref[...])[0:1]
    prior = dot(half_silu(0.5 * pre).astype(BF16), pout_ref[...])
    put_stripes(out_ref, 0, size, prior * -count)


def sum_body(size, own_ref, prior_ref, *rest):
    away, out_ref = rest[:-1], rest[-1]
    for k in range(size):
        total = own_ref[k] + prior_ref[k]
        for by in range(1, size):
            total = total + away[by - 1][source(k, by, size)].astype(F32)
        out_ref[k] = total.astype(out_ref.dtype)


def join_body(size, *refs):
    terms, part_ref, out_ref = refs[:-2], refs[-2], refs[-1]
    for k in range(size):
        total = terms[0][k].astype(F32)
        for term in terms[1:]:
            total = total + term[k].astype(F32)
        out_ref[k] = total
        out_ref[size + k] = part_ref[k]


def last_body(size, nrep, mix_ref, noise_ref, *rest):
    joined, (updated_ref, score_ref) = rest[:nrep], rest[nrep:]
    z, r = lax.axis_index("obs"), lax.axis_index("rep")
    reach = noise_ref.shape[-1] // 128
    delta = jnp.tile(mix_ref[0:1, :], (1, reach))
    root = jnp.tile(mix_ref[1:2, :], (1, reach))
    for away in range(nrep):
        rep = source(r, away, nrep)
        for k in range(size):
            block = source(z, k, size)
            total = joined[away][k]
            score_ref[block, rep] = total
            updated_ref[block, rep] = (
                joined[away][size + k] + delta * total + root * noise_ref[block, rep]
            )


def on_device(
    particles,
    obs_embed,
    step_index,
    noise,
    w_query,
    w_key,
    w_value,
    w_time,
    w_score,
    prior_in,
    prior_time,
    prior_out,
):
    size, nrep, nhid = lax.axis_size("obs"), lax.axis_size("rep"), lax.axis_size("hid")
    home = particles[0]
    block_rows, width = home.shape
    stripe = block_rows // size
    sub = stripe // nrep
    rows = size * sub
    heads = w_key.shape[1] // DH
    emb = obs_embed.shape[1]
    count = obs_embed.shape[0] * size * nrep - 1
    shifts = range(1, size)

    def shape(*dims, dtype=F32):
        return jax.ShapeDtypeStruct(dims, dtype)

    def scratch(blocks):
        return [
            pltpu.VMEM((blocks * heads * rows, emb), BF16),
            pltpu.VMEM((blocks * rows, heads * DH), F32),
        ]

    hbm = pl.BlockSpec(memory_space=pltpu.HBM)
    seen = [passed_along(obs_embed, "rep", by) for by in range(1, nrep)]
    early = [in_hbm(w_query), in_hbm(w_key)]
    prepared = call(
        functools.partial(prep_body, size, len(early)),
        "prep",
        [shape(rows, width, dtype=BF16), shape(sub, width)]
        + [shape(rows + sub, width, dtype=BF16) for _ in shifts]
        + [shape(*x.shape, dtype=x.dtype) for x in early],
        [hbm] * (1 + len(early)),
        [
            pltpu.VMEM((size, sub, width), F32),
            pltpu.VMEM((rows, width), F32),
            pltpu.SemaphoreType.DMA((len(early) + 1,)),
        ],
    )(in_hbm(home.reshape(size, nrep, sub, width)), *early)
    (theta, mine), sends, (query, key) = prepared[:2], prepared[2 : 1 + size], prepared[1 + size :]
    got = [passed_along(send, "obs", by) for by, send in zip(shifts, sends)]

    pair_flops = 4 * rows * heads * obs_embed.shape[0] * nrep * emb
    feats = w_time.shape[0]
    level = jnp.broadcast_to(step_index.astype(F32)[:, None], (1, 128))
    operands = [in_hbm(x) for x in (w_time.T, obs_embed, w_value, w_score)]
    terms, bias, mix, feat, e_home, value, out_weight = call(
        functools.partial(near_body, size, nrep, heads, feats),
        "near_blocks",
        [
            shape(2 * size, sub, width),
            shape(heads, 128),
            shape(2, 128),
            shape(16, feats, dtype=BF16),
        ]
        + [shape(*x.shape, dtype=x.dtype) for x in operands[1:]],
        [spec()] * (4 + nrep) + [hbm] * len(operands),
        [pltpu.VMEM(operands[0].shape, BF16)]
        + scratch(2)
        + [pltpu.SemaphoreType.DMA((len(operands),))],
        2 * pair_flops,
        24,
    )(level, theta, got[0], query, key, *seen, *operands)
    own, part, *leave = call(
        functools.partial(far_body, size, nrep),
        "far_blocks",
        [shape(size, sub, width), shape(size, sub, width)]
        + [shape(size, sub, width, dtype=BF16) for _ in shifts],
        [spec()] * (2 + size - 1 + nrep + 5),
        scratch(size - 2) + [pltpu.VMEM(((size - 2) * size, sub, width), F32)],
        pair_flops * (size - 2),
        24,
    )(terms, mine, *got, *seen, e_home, query, key, value, out_weight, bias)
    prior = call(
        functools.partial(prior_body, size, float(count)),
        "prior",
        shape(size, sub, width),
        [spec()] * 5,
        [pltpu.VMEM((rows, width), F32)],
        4 * rows * width * prior_in.shape[1],
        8,
    )(part, feat, prior_time, prior_in, prior_out)
    arrived = [passed_along(send, "obs", by) for by, send in zip(shifts, leave)]
    two = nhid == 2
    summed = call(
        functools.partial(sum_body, size),
        "sum_obs",
        shape(size, sub, width, dtype=BF16 if two else F32),
        [spec()] * (size + 1),
    )(own, prior, *arrived)
    if two:
        partial_sums = [summed, passed_along(summed, "hid", 1)]
    else:
        partial_sums = [lax.psum(summed, "hid")]
    joined = call(
        functools.partial(join_body, size),
        "join",
        shape(2 * size, sub, width),
        [spec()] * (len(partial_sums) + 1),
    )(*partial_sums, part)
    joined = [joined] + [passed_along(joined, "rep", by) for by in range(1, nrep)]
    whole = shape(size, nrep, sub, width)
    updated, score = call(
        functools.partial(last_body, size, nrep),
        "last",
        [whole, whole],
        [spec()] * (2 + nrep),
    )(mix, noise.reshape(size, nrep, sub, width), *joined)
    return (updated.reshape(noise.shape), score.reshape(noise.shape))


def solution(mesh):
    in_specs = (
        P(("groups", "obs"), None, None),
        P(("groups", "obs", "rep"), None),
        P("groups"),
        P("groups", "obs", None),
        P(None, "hid"),
        P(None, "hid"),
        P(None, "hid"),
        P(None, "hid"),
        P("hid", None),
        P(None, "hid"),
        P(None, "hid"),
        P("hid", None),
    )
    out_specs = (P("groups", "obs", None), P("groups", "obs", None))
    return jax.shard_map(
        on_device, mesh=mesh, in_specs=in_specs, out_specs=out_specs, check_vma=False
    )
```

```python
import functools
import math

import jax
import jax.numpy as jnp
from jax import lax
from jax.experimental import pallas as pl
from jax.experimental.pallas import tpu as pltpu
from jax.sharding import PartitionSpec as P

DH = 128
STEPS = 64

SIG_LO = 0.05
SIG_HI = 1.0

F32 = jnp.float32
BF16 = jnp.bfloat16
NT = (((1,), (1,)), ((), ()))
TILE = 512


def partner(index, by, size):
    if size & (size - 1) == 0:
        return index ^ by
    return (index + by) % size


def source(index, by, size):
    return partner(index, by if size & (size - 1) == 0 else size - by, size)


def passed_along(shard, axis, by):
    size = lax.axis_size(axis)
    return lax.ppermute(shard, axis, [(i, partner(i, by, size)) for i in range(size)])


def plan(level, feature_count):
    growth = math.log(SIG_HI / SIG_LO) / (STEPS - 1)
    sigma_now = SIG_LO * jnp.exp(growth * level)
    sigma_prev = SIG_LO * jnp.exp(growth * (level - 1.0))
    delta = sigma_now * sigma_now - sigma_prev * sigma_prev
    halves = feature_count // 2
    lane = lax.broadcasted_iota(jnp.int32, (1, halves), 1).astype(F32)
    angles = 10.0 * jnp.log(sigma_now[:, :1]) * jnp.exp(-math.log(1000.0) / halves * lane)
    features = jnp.concatenate([jnp.sin(angles), jnp.cos(angles)], 1).astype(BF16)
    return (features, delta)


def dot(a, b):
    return jnp.dot(a, b, preferred_element_type=F32)


def halves_of(x):
    high = x.astype(BF16)
    return high, (x - high.astype(F32)).astype(BF16)


def split_dot(x, weight):
    rows = x.shape[0]
    both = dot(jnp.concatenate(halves_of(x), 0), weight)
    return both[:rows] + both[rows:]


def half_silu(y):
    return y + y * jnp.tanh(y)


def put_stripes(stage, first, count, values):
    sub = stage.shape[1]
    for s in range(count):
        stage[first + s] = values[s * sub : (s + 1) * sub]


def spec():
    return pl.BlockSpec(memory_space=pltpu.VMEM)


def in_hbm(x):
    return pltpu.with_memory_space_constraint(x, pltpu.HBM)


def call(body, name, out_shape, in_specs, scratch=(), flops=0, limit=4):
    return pl.pallas_call(
        body,
        name=name,
        out_shape=out_shape,
        in_specs=in_specs,
        out_specs=jax.tree.map(lambda _: spec(), out_shape),
        scratch_shapes=list(scratch),
        cost_estimate=pl.CostEstimate(flops=flops, bytes_accessed=flops // 1000, transcendentals=0),
        compiler_params=pltpu.CompilerParams(vmem_limit_bytes=limit << 20),
    )


def prep_body(size, home_ref, wt_hbm, theta_ref, mine_ref, wt_ref, *refs):
    sends, (held, stage, sems) = refs[: size - 1], refs[size - 1 :]
    z, r = lax.axis_index("obs"), lax.axis_index("rep")
    sub = held.shape[1]
    pairs = [(home_ref.at[:, r], held), (wt_hbm, wt_ref)]
    copies = [pltpu.make_async_copy(*pair, sems.at[i]) for i, pair in enumerate(pairs)]
    for copy in copies:
        copy.start()
    copies[0].wait()
    for s in range(size):
        stage[s * sub : (s + 1) * sub, :] = held[s]
    theta = stage[...].astype(BF16)
    theta_ref[...] = theta
    mine_ref[...] = held[z]
    rows = theta.shape[0]
    for by, send in enumerate(sends, 1):
        send[:rows, :] = theta
        send[rows:, :] = halves_of(held[partner(z, by, size)])[1]
    for copy in copies[1:]:
        copy.wait()


def pair_terms(theta, e_refs, weight_refs, qk_ref, pool_ref, ready=lambda ref: None):
    wq_ref, wk_ref, wv_ref, ws_ref, bias_ref = weight_refs
    scale = 0.5 / math.sqrt(DH)
    blocks = len(theta)
    rows = theta[0].shape[0]
    heads = wk_ref.shape[1] // DH
    every = theta[0] if blocks == 1 else jnp.concatenate(theta, 0)
    ready(wq_ref)
    queries = dot(every, wq_ref[...]).astype(BF16)
    ready(wk_ref)
    for h in range(heads):
        cols = slice(h * DH, (h + 1) * DH)
        turned = lax.dot_general(queries[:, cols], wk_ref[:, cols], NT, preferred_element_type=F32)
        turned = (turned * scale).astype(BF16)
        for b in range(blocks):
            at = (b * heads + h) * rows
            qk_ref[at : at + rows, :] = turned[b * rows : (b + 1) * rows]

    def weights(scores):
        parts = []
        for h in range(heads):
            bias = jnp.tile(bias_ref[h : h + 1, :], (1, scores.shape[1] // 128))
            parts.append(half_silu(scores[h * rows : (h + 1) * rows] + bias).astype(BF16))
        return jnp.concatenate(parts, 0)

    for b in range(blocks):
        span = slice(b * heads * rows, (b + 1) * heads * rows)
        total = None
        for e_ref in e_refs:
            tile = math.gcd(TILE, e_ref.shape[0])
            ready(e_ref)
            for j in range(e_ref.shape[0] // tile):
                seen = e_ref[j * tile : (j + 1) * tile, :]
                scores = lax.dot_general(qk_ref[span, :], seen, NT, preferred_element_type=F32)
                term = dot(weights(scores), seen)
                total = term if total is None else total + term
        ready(wv_ref)
        for h in range(heads):
            cols = slice(h * DH, (h + 1) * DH)
            pool_ref[b * rows : (b + 1) * rows, cols] = split_dot(
                total[h * rows : (h + 1) * rows], wv_ref[:, cols]
            )
    ready(ws_ref)
    return split_dot(pool_ref[...], ws_ref[...])


def home_body(size, nrep, heads, feats, level_ref, wt_ref, theta_ref, *refs):
    others, refs = refs[: nrep - 1], refs[nrep - 1 :]
    hbm, (terms_ref, bias_ref, mix_ref, feat_ref, *held) = refs[:5], refs[5:14]
    qk_ref, pool_ref, sems = refs[14:]
    copies = [pltpu.make_async_copy(hbm[i], held[i], sems.at[i]) for i in range(5)]
    waiting = dict(zip(map(id, held), copies))

    def ready(ref):
        if id(ref) in waiting:
            waiting.pop(id(ref)).wait()

    for copy in copies[:2]:
        copy.start()
    level = jnp.full((1, 128), level_ref[0], jnp.int32).astype(F32)
    features, delta = plan(level, feats)
    mix_ref[0:1, :] = delta
    mix_ref[1:2, :] = jnp.sqrt(delta)
    feat = jnp.broadcast_to(features, (16, feats))
    feat_ref[...] = feat
    head_bias = lax.dot_general(wt_ref[...], feat, NT, preferred_element_type=F32) * 0.5
    bias_ref[...] = jnp.broadcast_to(head_bias[:, 0:1], (heads, 128))
    for copy in copies[2:]:
        copy.start()
    wq_ref, wk_ref, e_ref, wv_ref, ws_ref = held
    weights = (wq_ref, wk_ref, wv_ref, ws_ref, bias_ref)
    terms = pair_terms([theta_ref[...]], [*others, e_ref], weights, qk_ref, pool_ref, ready)
    put_stripes(terms_ref, 0, size, terms)


def mid_body(size, got_ref, *refs):
    e_refs, (terms_ref, qk_ref, pool_ref) = refs[:-8], refs[-3:]
    rows = terms_ref.shape[0] * terms_ref.shape[1]
    terms = pair_terms([got_ref[:rows, :]], e_refs, refs[-8:-3], qk_ref, pool_ref)
    put_stripes(terms_ref, 0, size, terms)


def far_body(size, nrep, *refs):
    nblk = size - 2
    home_ref, mid_ref, mine_ref = refs[:3]
    got, rest = refs[3 : 2 + size], refs[2 + size :]
    e_refs, rest = rest[:nrep], rest[nrep:]
    weights, (own_ref, part_ref) = rest[:5], rest[5:7]
    sends = rest[7 : 6 + size]
    qk_ref, pool_ref, stage = rest[6 + size :]
    z = lax.axis_index("obs")
    sub = own_ref.shape[1]
    rows = size * sub
    part_ref[0] = mine_ref[...]
    for b in range(1, size):
        put_stripes(stage, 0, size, got[b - 1][:rows, :].astype(F32))
        part_ref[b] = stage[z] + got[b - 1][rows:, :].astype(F32)
    theta = [ref[:rows, :] for ref in got[1:]]
    terms = pair_terms(theta, e_refs, weights, qk_ref, pool_ref)
    put_stripes(stage, 0, nblk * size, terms)
    for k in range(size):
        held, first = (stage, (k - 2) * size) if k >= 2 else ((home_ref, mid_ref)[k], 0)
        own_ref[k] = held[first + z]
        for by, send in enumerate(sends, 1):
            send[k] = held[first + partner(z, by, size)].astype(BF16)


def prior_body(size, count, part_ref, feat_ref, pt_ref, pin_ref, pout_ref, out_ref, stage):
    sub = part_ref.shape[1]
    for k in range(size):
        stage[k * sub : (k + 1) * sub, :] = part_ref[k]
    pre = dot(stage[...].astype(BF16), pin_ref[...]) + dot(feat_ref[...], pt_ref[...])[0:1]
    prior = dot(half_silu(0.5 * pre).astype(BF16), pout_ref[...])
    put_stripes(out_ref, 0, size, prior * -count)


def sum_body(size, own_ref, prior_ref, *rest):
    away, out_ref = rest[:-1], rest[-1]
    for k in range(size):
        total = own_ref[k] + prior_ref[k]
        for by in range(1, size):
            total = total + away[by - 1][source(k, by, size)].astype(F32)
        out_ref[k] = total.astype(out_ref.dtype)


def join_body(size, *refs):
    terms, part_ref, out_ref = refs[:-2], refs[-2], refs[-1]
    for k in range(size):
        total = terms[0][k].astype(F32)
        for term in terms[1:]:
            total = total + term[k].astype(F32)
        out_ref[k] = total
        out_ref[size + k] = part_ref[k]


def last_body(size, nrep, mix_ref, noise_ref, *rest):
    joined, (updated_ref, score_ref) = rest[:nrep], rest[nrep:]
    z, r = lax.axis_index("obs"), lax.axis_index("rep")
    reach = noise_ref.shape[-1] // 128
    delta = jnp.tile(mix_ref[0:1, :], (1, reach))
    root = jnp.tile(mix_ref[1:2, :], (1, reach))
    for away in range(nrep):
        rep = source(r, away, nrep)
        for k in range(size):
            block = source(z, k, size)
            total = joined[away][k]
            score_ref[block, rep] = total
            updated_ref[block, rep] = (
                joined[away][size + k] + delta * total + root * noise_ref[block, rep]
            )


def on_device(
    particles,
    obs_embed,
    step_index,
    noise,
    w_query,
    w_key,
    w_value,
    w_time,
    w_score,
    prior_in,
    prior_time,
    prior_out,
):
    size, nrep, nhid = lax.axis_size("obs"), lax.axis_size("rep"), lax.axis_size("hid")
    home = particles[0]
    block_rows, width = home.shape
    stripe = block_rows // size
    sub = stripe // nrep
    rows = size * sub
    heads = w_key.shape[1] // DH
    emb = obs_embed.shape[1]
    count = obs_embed.shape[0] * size * nrep - 1
    shifts = range(1, size)

    def shape(*dims, dtype=F32):
        return jax.ShapeDtypeStruct(dims, dtype)

    def scratch(blocks):
        return [
            pltpu.VMEM((blocks * heads * rows, emb), BF16),
            pltpu.VMEM((blocks * rows, heads * DH), F32),
        ]

    hbm = pl.BlockSpec(memory_space=pltpu.HBM)
    far_first = [*range(size // 2, size), *range(1, size // 2)]

    def exchanged(sends):
        moved = {by: passed_along(sends[by - 1], "obs", by) for by in far_first}
        return [moved[by] for by in shifts]

    seen = [passed_along(obs_embed, "rep", by) for by in range(1, nrep)]
    time_weight = in_hbm(w_time.T)
    theta, mine, time_weight, *sends = call(
        functools.partial(prep_body, size),
        "prep",
        [
            shape(rows, width, dtype=BF16),
            shape(sub, width),
            shape(*time_weight.shape, dtype=BF16),
        ]
        + [shape(rows + sub, width, dtype=BF16) for _ in shifts],
        [hbm] * 2,
        [
            pltpu.VMEM((size, sub, width), F32),
            pltpu.VMEM((rows, width), F32),
            pltpu.SemaphoreType.DMA((2,)),
        ],
    )(in_hbm(home.reshape(size, nrep, sub, width)), time_weight)
    got = exchanged(sends)

    pair_flops = 4 * rows * heads * obs_embed.shape[0] * nrep * emb
    feats = w_time.shape[0]
    operands = [in_hbm(x) for x in (w_query, w_key, obs_embed, w_value, w_score)]
    home_terms, bias, mix, feat, *held = call(
        functools.partial(home_body, size, nrep, heads, feats),
        "home_block",
        [
            shape(size, sub, width),
            shape(heads, 128),
            shape(2, 128),
            shape(16, feats, dtype=BF16),
        ]
        + [shape(*x.shape, dtype=x.dtype) for x in operands],
        [pl.BlockSpec(memory_space=pltpu.SMEM)]
        + [spec()] * (1 + nrep)
        + [hbm] * len(operands),
        scratch(1) + [pltpu.SemaphoreType.DMA((len(operands),))],
        pair_flops,
        24,
    )(step_index, time_weight, theta, *seen, *operands)
    query, key, e_home, value, out_weight = held
    weights = [*seen, e_home, query, key, value, out_weight, bias]
    mid_terms = call(
        functools.partial(mid_body, size),
        "mid_block",
        shape(size, sub, width),
        [spec()] * (1 + len(weights)),
        scratch(1),
        pair_flops,
        24,
    )(got[0], *weights)
    own, part, *leave = call(
        functools.partial(far_body, size, nrep),
        "far_blocks",
        [shape(size, sub, width), shape(size, sub, width)]
        + [shape(size, sub, width, dtype=BF16) for _ in shifts],
        [spec()] * (2 + size + len(weights)),
        scratch(size - 2) + [pltpu.VMEM(((size - 2) * size, sub, width), F32)],
        pair_flops * (size - 2),
        24,
    )(home_terms, mid_terms, mine, *got, *weights)
    prior = call(
        functools.partial(prior_body, size, float(count)),
        "prior",
        shape(size, sub, width),
        [spec()] * 5,
        [pltpu.VMEM((rows, width), F32)],
        4 * rows * width * prior_in.shape[1],
        8,
    )(part, feat, prior_time, prior_in, prior_out)
    arrived = exchanged(leave)
    two = nhid == 2
    summed = call(
        functools.partial(sum_body, size),
        "sum_obs",
        shape(size, sub, width, dtype=BF16 if two else F32),
        [spec()] * (size + 1),
    )(own, prior, *arrived)
    if two:
        partial_sums = [summed, passed_along(summed, "hid", 1)]
    else:
        partial_sums = [lax.psum(summed, "hid")]
    joined = call(
        functools.partial(join_body, size),
        "join",
        shape(2 * size, sub, width),
        [spec()] * (len(partial_sums) + 1),
    )(*partial_sums, part)
    joined = [joined] + [passed_along(joined, "rep", by) for by in range(1, nrep)]
    whole = shape(size, nrep, sub, width)
    updated, score = call(
        functools.partial(last_body, size, nrep),
        "last",
        [whole, whole],
        [spec()] * (2 + nrep),
    )(mix, noise.reshape(size, nrep, sub, width), *joined)
    return (updated.reshape(noise.shape), score.reshape(noise.shape))


def solution(mesh):
    in_specs = (
        P(("groups", "obs"), None, None),
        P(("groups", "obs", "rep"), None),
        P("groups"),
        P("groups", "obs", None),
        P(None, "hid"),
        P(None, "hid"),
        P(None, "hid"),
        P(None, "hid"),
        P("hid", None),
        P(None, "hid"),
        P(None, "hid"),
        P("hid", None),
    )
    out_specs = (P("groups", "obs", None), P("groups", "obs", None))
    return jax.shard_map(
        on_device, mesh=mesh, in_specs=in_specs, out_specs=out_specs, check_vma=False
    )
```

```python
import functools
import math

import jax
import jax.numpy as jnp
from jax import lax
from jax.experimental import pallas as pl
from jax.experimental.pallas import tpu as pltpu
from jax.sharding import PartitionSpec as P

DH = 128
STEPS = 64

SIG_LO = 0.05
SIG_HI = 1.0

F32 = jnp.float32
BF16 = jnp.bfloat16
NT = (((1,), (1,)), ((), ()))
TILE = 512


def partner(index, by, size):
    if size & (size - 1) == 0:
        return index ^ by
    return (index + by) % size


def source(index, by, size):
    return partner(index, by if size & (size - 1) == 0 else size - by, size)


def passed_along(shard, axis, by):
    size = lax.axis_size(axis)
    return lax.ppermute(shard, axis, [(i, partner(i, by, size)) for i in range(size)])


def plan(level, feature_count):
    growth = math.log(SIG_HI / SIG_LO) / (STEPS - 1)
    sigma_now = SIG_LO * jnp.exp(growth * level)
    sigma_prev = SIG_LO * jnp.exp(growth * (level - 1.0))
    delta = sigma_now * sigma_now - sigma_prev * sigma_prev
    halves = feature_count // 2
    lane = lax.broadcasted_iota(jnp.int32, (1, halves), 1).astype(F32)
    angles = 10.0 * jnp.log(sigma_now[:, :1]) * jnp.exp(-math.log(1000.0) / halves * lane)
    features = jnp.concatenate([jnp.sin(angles), jnp.cos(angles)], 1).astype(BF16)
    return (features, delta)


def dot(a, b):
    return jnp.dot(a, b, preferred_element_type=F32)


def halves_of(x):
    high = x.astype(BF16)
    return high, (x - high.astype(F32)).astype(BF16)


def split_dot(x, weight):
    rows = x.shape[0]
    both = dot(jnp.concatenate(halves_of(x), 0), weight)
    return both[:rows] + both[rows:]


def half_silu(y):
    return y + y * jnp.tanh(y)


def put_stripes(stage, first, count, values):
    sub = stage.shape[1]
    for s in range(count):
        stage[first + s] = values[s * sub : (s + 1) * sub]


def spec():
    return pl.BlockSpec(memory_space=pltpu.VMEM)


def in_hbm(x):
    return pltpu.with_memory_space_constraint(x, pltpu.HBM)


def call(body, name, out_shape, in_specs, scratch=(), flops=0, limit=4, out_spec=None):
    return pl.pallas_call(
        body,
        name=name,
        out_shape=out_shape,
        in_specs=in_specs,
        out_specs=jax.tree.map(lambda _: out_spec or spec(), out_shape),
        scratch_shapes=list(scratch),
        cost_estimate=pl.CostEstimate(flops=flops, bytes_accessed=flops // 1000, transcendentals=0),
        compiler_params=pltpu.CompilerParams(vmem_limit_bytes=limit << 20),
    )


def pieces(rows, wanted=4):
    count = max(n for n in (1, 2, wanted) if rows % (16 * n) == 0 or n == 1)
    step = rows // count
    return [pl.ds(i * step, step) for i in range(count)]


class Copies:
    def __init__(self, sems):
        self.sems, self.used, self.waiting = sems, 0, {}

    def start(self, source, target):
        parts = []
        for rows in pieces(target.shape[0]):
            copy = pltpu.make_async_copy(source.at[rows], target.at[rows], self.sems.at[self.used])
            copy.start()
            self.used += 1
            parts.append(copy)
        self.waiting[id(target)] = parts

    def ready(self, target):
        for copy in self.waiting.pop(id(target), ()):
            copy.wait()


def copy_count(arrays):
    return sum(len(pieces(x.shape[0])) for x in arrays)


def prep_body(size, home_ref, wt_hbm, theta_ref, mine_ref, wt_ref, *refs):
    sends, (held, stage, sems) = refs[: size - 1], refs[size - 1 :]
    z, r = lax.axis_index("obs"), lax.axis_index("rep")
    sub = held.shape[1]
    pairs = [(home_ref.at[s, r], held.at[s]) for s in range(size)] + [(wt_hbm, wt_ref)]
    copies = [pltpu.make_async_copy(*pair, sems.at[i]) for i, pair in enumerate(pairs)]
    for copy in copies:
        copy.start()
    for s in range(size):
        copies[s].wait()
        stage[s * sub : (s + 1) * sub, :] = held[s]
    theta = stage[...].astype(BF16)
    theta_ref[...] = theta
    mine_ref[...] = held[z]
    rows = theta.shape[0]
    for by, send in enumerate(sends, 1):
        send[:rows, :] = theta
        send[rows:, :] = halves_of(held[partner(z, by, size)])[1]
    copies[size].wait()


def pair_terms(theta, e_refs, weight_refs, qk_ref, pool_ref, ready=lambda ref: None):
    wq_ref, wk_ref, wv_ref, ws_ref, bias_ref = weight_refs
    scale = 0.5 / math.sqrt(DH)
    blocks = len(theta)
    rows = theta[0].shape[0]
    heads = wk_ref.shape[1] // DH
    every = theta[0] if blocks == 1 else jnp.concatenate(theta, 0)
    ready(wq_ref)
    queries = dot(every, wq_ref[...]).astype(BF16)
    ready(wk_ref)
    for h in range(heads):
        cols = slice(h * DH, (h + 1) * DH)
        turned = lax.dot_general(queries[:, cols], wk_ref[:, cols], NT, preferred_element_type=F32)
        turned = (turned * scale).astype(BF16)
        for b in range(blocks):
            at = (b * heads + h) * rows
            qk_ref[at : at + rows, :] = turned[b * rows : (b + 1) * rows]

    def weights(scores):
        parts = []
        for h in range(heads):
            bias = jnp.tile(bias_ref[h : h + 1, :], (1, scores.shape[1] // 128))
            parts.append(half_silu(scores[h * rows : (h + 1) * rows] + bias).astype(BF16))
        return jnp.concatenate(parts, 0)

    for b in range(blocks):
        span = slice(b * heads * rows, (b + 1) * heads * rows)
        total = None
        for e_ref in e_refs:
            tile = math.gcd(TILE, e_ref.shape[0])
            ready(e_ref)
            for j in range(e_ref.shape[0] // tile):
                seen = e_ref[j * tile : (j + 1) * tile, :]
                scores = lax.dot_general(qk_ref[span, :], seen, NT, preferred_element_type=F32)
                term = dot(weights(scores), seen)
                total = term if total is None else total + term
        ready(wv_ref)
        for h in range(heads):
            cols = slice(h * DH, (h + 1) * DH)
            pool_ref[b * rows : (b + 1) * rows, cols] = split_dot(
                total[h * rows : (h + 1) * rows], wv_ref[:, cols]
            )
    ready(ws_ref)
    return split_dot(pool_ref[...], ws_ref[...])


def home_body(size, nrep, heads, feats, level_ref, wt_ref, theta_ref, *refs):
    others, refs = refs[: nrep - 1], refs[nrep - 1 :]
    hbm, (terms_ref, bias_ref, mix_ref, feat_ref, *held) = refs[:5], refs[5:14]
    qk_ref, pool_ref, sems = refs[14:]
    copies = Copies(sems)
    for i in range(2):
        copies.start(hbm[i], held[i])
    level = jnp.broadcast_to(level_ref[...].astype(F32), (1, 128))
    features, delta = plan(level, feats)
    mix_ref[0:1, :] = delta
    mix_ref[1:2, :] = jnp.sqrt(delta)
    feat = jnp.broadcast_to(features, (16, feats))
    feat_ref[...] = feat
    head_bias = lax.dot_general(wt_ref[...], feat, NT, preferred_element_type=F32) * 0.5
    bias_ref[...] = jnp.broadcast_to(head_bias[:, 0:1], (heads, 128))
    for i in range(2, 5):
        copies.start(hbm[i], held[i])
    wq_ref, wk_ref, e_ref, wv_ref, ws_ref = held
    weights = (wq_ref, wk_ref, wv_ref, ws_ref, bias_ref)
    terms = pair_terms([theta_ref[...]], [*others, e_ref], weights, qk_ref, pool_ref, copies.ready)
    put_stripes(terms_ref, 0, size, terms)


def mid_body(size, got_ref, *refs):
    e_refs, (terms_ref, qk_ref, pool_ref) = refs[:-8], refs[-3:]
    rows = terms_ref.shape[0] * terms_ref.shape[1]
    terms = pair_terms([got_ref[:rows, :]], e_refs, refs[-8:-3], qk_ref, pool_ref)
    put_stripes(terms_ref, 0, size, terms)


def far_body(size, nrep, *refs):
    nblk = size - 2
    home_ref, mid_ref, mine_ref = refs[:3]
    got, rest = refs[3 : 2 + size], refs[2 + size :]
    e_refs, rest = rest[:nrep], rest[nrep:]
    weights, (own_ref, part_ref) = rest[:5], rest[5:7]
    sends = rest[7 : 6 + size]
    qk_ref, pool_ref, stage = rest[6 + size :]
    z = lax.axis_index("obs")
    sub = own_ref.shape[1]
    rows = size * sub
    part_ref[0] = mine_ref[...]
    for b in range(1, size):
        put_stripes(stage, 0, size, got[b - 1][:rows, :].astype(F32))
        part_ref[b] = stage[z] + got[b - 1][rows:, :].astype(F32)
    theta = [ref[:rows, :] for ref in got[1:]]
    terms = pair_terms(theta, e_refs, weights, qk_ref, pool_ref)
    put_stripes(stage, 0, nblk * size, terms)
    for k in range(size):
        held, first = (stage, (k - 2) * size) if k >= 2 else ((home_ref, mid_ref)[k], 0)
        own_ref[k] = held[first + z]
        for by, send in enumerate(sends, 1):
            send[k] = held[first + partner(z, by, size)].astype(BF16)


def prior_body(size, count, part_ref, feat_ref, *refs):
    hbm, (out_ref, stage), held, sems = refs[:3], refs[3:5], refs[5:8], refs[8]
    copies = Copies(sems)
    for i in range(3):
        copies.start(hbm[i], held[i])
    pin_ref, pt_ref, pout_ref = held
    sub = part_ref.shape[1]
    for k in range(size):
        stage[k * sub : (k + 1) * sub, :] = part_ref[k]
    copies.ready(pin_ref)
    copies.ready(pt_ref)
    pre = dot(stage[...].astype(BF16), pin_ref[...]) + dot(feat_ref[...], pt_ref[...])[0:1]
    copies.ready(pout_ref)
    prior = dot(half_silu(0.5 * pre).astype(BF16), pout_ref[...])
    put_stripes(out_ref, 0, size, prior * -count)


def sum_body(size, order, *rest):
    own_ref, prior_ref, out_ref = rest[-3:]
    away = dict(zip(order, rest))
    for k in range(size):
        total = own_ref[k] + prior_ref[k]
        for by in range(1, size):
            total = total + away[by][source(k, by, size)].astype(F32)
        out_ref[k] = total.astype(out_ref.dtype)


def join_body(size, *refs):
    terms, part_ref, out_ref = refs[:-2], refs[-2], refs[-1]
    for k in range(size):
        total = terms[0][k].astype(F32)
        for term in terms[1:]:
            total = total + term[k].astype(F32)
        out_ref[k] = total
        out_ref[size + k] = part_ref[k]


def last_body(size, nrep, mix_ref, noise_ref, *rest):
    joined, rest = rest[:nrep], rest[nrep:]
    hbm, held, sems = rest[:2], rest[2:4], rest[4]
    z, r = lax.axis_index("obs"), lax.axis_index("rep")
    reach = noise_ref.shape[-1] // 128
    delta = jnp.tile(mix_ref[0:1, :], (1, reach))
    root = jnp.tile(mix_ref[1:2, :], (1, reach))
    copies = []
    for away in range(nrep):
        rep = source(r, away, nrep)
        for k in range(size):
            block = source(z, k, size)
            total = joined[away][k]
            shifted = joined[away][size + k] + delta * total + root * noise_ref[block, rep]
            for i, value in enumerate((shifted, total)):
                held[i][away, k] = value
                at = (block, rep)
                copies.append(
                    pltpu.make_async_copy(held[i].at[away, k], hbm[i].at[at], sems.at[away, k, i])
                )
                copies[-1].start()
    for copy in copies:
        copy.wait()


def on_device(
    particles,
    obs_embed,
    step_index,
    noise,
    w_query,
    w_key,
    w_value,
    w_time,
    w_score,
    prior_in,
    prior_time,
    prior_out,
):
    size, nrep, nhid = lax.axis_size("obs"), lax.axis_size("rep"), lax.axis_size("hid")
    home = particles[0]
    block_rows, width = home.shape
    stripe = block_rows // size
    sub = stripe // nrep
    rows = size * sub
    heads = w_key.shape[1] // DH
    emb = obs_embed.shape[1]
    count = obs_embed.shape[0] * size * nrep - 1
    shifts = range(1, size)

    def shape(*dims, dtype=F32):
        return jax.ShapeDtypeStruct(dims, dtype)

    def scratch(blocks):
        return [
            pltpu.VMEM((blocks * heads * rows, emb), BF16),
            pltpu.VMEM((blocks * rows, heads * DH), F32),
        ]

    hbm = pl.BlockSpec(memory_space=pltpu.HBM)
    far_first = [*range(size // 2, size), *range(1, size // 2)]

    def exchanged(sends):
        moved = {by: passed_along(sends[by - 1], "obs", by) for by in far_first}
        return [moved[by] for by in shifts]

    seen = [passed_along(obs_embed, "rep", by) for by in range(1, nrep)]
    level = passed_along(step_index, "rep", 1).reshape(1, 1)
    time_weight = in_hbm(w_time.T)
    theta, mine, time_weight, *sends = call(
        functools.partial(prep_body, size),
        "prep",
        [
            shape(rows, width, dtype=BF16),
            shape(sub, width),
            shape(*time_weight.shape, dtype=BF16),
        ]
        + [shape(rows + sub, width, dtype=BF16) for _ in shifts],
        [hbm] * 2,
        [
            pltpu.VMEM((size, sub, width), F32),
            pltpu.VMEM((rows, width), F32),
            pltpu.SemaphoreType.DMA((size + 1,)),
        ],
    )(in_hbm(home.reshape(size, nrep, sub, width)), time_weight)
    got = exchanged(sends)

    pair_flops = 4 * rows * heads * obs_embed.shape[0] * nrep * emb
    feats = w_time.shape[0]
    operands = [in_hbm(x) for x in (w_query, w_key, obs_embed, w_value, w_score)]
    home_terms, bias, mix, feat, *held = call(
        functools.partial(home_body, size, nrep, heads, feats),
        "home_block",
        [
            shape(size, sub, width),
            shape(heads, 128),
            shape(2, 128),
            shape(16, feats, dtype=BF16),
        ]
        + [shape(*x.shape, dtype=x.dtype) for x in operands],
        [spec()] * (2 + nrep)
        + [hbm] * len(operands),
        scratch(1) + [pltpu.SemaphoreType.DMA((copy_count(operands),))],
        pair_flops,
        24,
    )(level, time_weight, theta, *seen, *operands)
    query, key, e_home, value, out_weight = held
    weights = [*seen, e_home, query, key, value, out_weight, bias]
    mid_terms = call(
        functools.partial(mid_body, size),
        "mid_block",
        shape(size, sub, width),
        [spec()] * (1 + len(weights)),
        scratch(1),
        pair_flops,
        24,
    )(got[0], *weights)
    own, part, *leave = call(
        functools.partial(far_body, size, nrep),
        "far_blocks",
        [shape(size, sub, width), shape(size, sub, width)]
        + [shape(size, sub, width, dtype=BF16) for _ in shifts],
        [spec()] * (2 + size + len(weights)),
        scratch(size - 2) + [pltpu.VMEM(((size - 2) * size, sub, width), F32)],
        pair_flops * (size - 2),
        24,
    )(home_terms, mid_terms, mine, *got, *weights)
    operands = [in_hbm(x) for x in (prior_in, prior_time, prior_out)]
    prior = call(
        functools.partial(prior_body, size, float(count)),
        "prior",
        shape(size, sub, width),
        [spec()] * 2 + [hbm] * 3,
        [pltpu.VMEM((rows, width), F32)]
        + [pltpu.VMEM(x.shape, x.dtype) for x in operands]
        + [pltpu.SemaphoreType.DMA((copy_count(operands),))],
        4 * rows * width * prior_in.shape[1],
        8,
    )(part, feat, *operands)
    arrived = exchanged(leave)
    two = nhid == 2
    summed = call(
        functools.partial(sum_body, size, far_first),
        "sum_obs",
        shape(size, sub, width, dtype=BF16 if two else F32),
        [spec()] * (size + 1),
    )(*[arrived[by - 1] for by in far_first], own, prior)
    if two:
        partial_sums = [summed, passed_along(summed, "hid", 1)]
    else:
        partial_sums = [lax.psum(summed, "hid")]
    joined = call(
        functools.partial(join_body, size),
        "join",
        shape(2 * size, sub, width),
        [spec()] * (len(partial_sums) + 1),
    )(*partial_sums, part)
    joined = [joined] + [passed_along(joined, "rep", by) for by in range(1, nrep)]
    whole = shape(size, nrep, sub, width)
    updated, score = call(
        functools.partial(last_body, size, nrep),
        "last",
        [whole, whole],
        [spec()] * (2 + nrep),
        [pltpu.VMEM((nrep, size, sub, width), F32)] * 2
        + [pltpu.SemaphoreType.DMA((nrep, size, 2))],
        out_spec=hbm,
    )(mix, noise.reshape(size, nrep, sub, width), *joined)
    return (updated.reshape(noise.shape), score.reshape(noise.shape))


def solution(mesh):
    in_specs = (
        P(("groups", "obs"), None, None),
        P(("groups", "obs", "rep"), None),
        P("groups"),
        P("groups", "obs", None),
        P(None, "hid"),
        P(None, "hid"),
        P(None, "hid"),
        P(None, "hid"),
        P("hid", None),
        P(None, "hid"),
        P(None, "hid"),
        P("hid", None),
    )
    out_specs = (P("groups", "obs", None), P("groups", "obs", None))
    return jax.shard_map(
        on_device, mesh=mesh, in_specs=in_specs, out_specs=out_specs, check_vma=False
    )
```

```python
import functools
import math

import jax
import jax.numpy as jnp
from jax import lax
from jax.experimental import pallas as pl
from jax.experimental.pallas import tpu as pltpu
from jax.sharding import PartitionSpec as P

DH = 128
STEPS = 64

SIG_LO = 0.05
SIG_HI = 1.0

F32 = jnp.float32
BF16 = jnp.bfloat16
NT = (((1,), (1,)), ((), ()))
TILE = 512


def partner(index, by, size):
    if size & (size - 1) == 0:
        return index ^ by
    return (index + by) % size


def source(index, by, size):
    return partner(index, by if size & (size - 1) == 0 else size - by, size)


def passed_along(shard, axis, by):
    size = lax.axis_size(axis)
    return lax.ppermute(shard, axis, [(i, partner(i, by, size)) for i in range(size)])


def plan(level, feature_count):
    growth = math.log(SIG_HI / SIG_LO) / (STEPS - 1)
    sigma_now = SIG_LO * jnp.exp(growth * level)
    sigma_prev = SIG_LO * jnp.exp(growth * (level - 1.0))
    delta = sigma_now * sigma_now - sigma_prev * sigma_prev
    halves = feature_count // 2
    lane = lax.broadcasted_iota(jnp.int32, (1, halves), 1).astype(F32)
    angles = 10.0 * jnp.log(sigma_now[:, :1]) * jnp.exp(-math.log(1000.0) / halves * lane)
    features = jnp.concatenate([jnp.sin(angles), jnp.cos(angles)], 1).astype(BF16)
    return (features, delta)


def dot(a, b):
    return jnp.dot(a, b, preferred_element_type=F32)


def halves_of(x):
    high = x.astype(BF16)
    return high, (x - high.astype(F32)).astype(BF16)


def split_dot(x, weight):
    rows = x.shape[0]
    both = dot(jnp.concatenate(halves_of(x), 0), weight)
    return both[:rows] + both[rows:]


def half_silu(y):
    return y + y * jnp.tanh(y)


def put_stripes(stage, first, count, values):
    sub = stage.shape[1]
    for s in range(count):
        stage[first + s] = values[s * sub : (s + 1) * sub]


def spec():
    return pl.BlockSpec(memory_space=pltpu.VMEM)


def in_hbm(x):
    return pltpu.with_memory_space_constraint(x, pltpu.HBM)


def call(body, name, out_shape, in_specs, scratch=(), flops=0, limit=4):
    return pl.pallas_call(
        body,
        name=name,
        out_shape=out_shape,
        in_specs=in_specs,
        out_specs=jax.tree.map(lambda _: spec(), out_shape),
        scratch_shapes=list(scratch),
        cost_estimate=pl.CostEstimate(flops=flops, bytes_accessed=flops // 1000, transcendentals=0),
        compiler_params=pltpu.CompilerParams(vmem_limit_bytes=limit << 20),
    )


def copies_of(sources, targets, sems):
    return [
        pltpu.make_async_copy(source, target, sems.at[i])
        for i, (source, target) in enumerate(zip(sources, targets))
    ]


def wait_for(copies):
    for copy in copies:
        copy.wait()


def prep_body(size, home_ref, wt_hbm, theta_ref, mine_ref, wt_ref, *refs):
    sends, (held, stage, sems) = refs[: size - 1], refs[size - 1 :]
    z, r = lax.axis_index("obs"), lax.axis_index("rep")
    sub = held.shape[1]
    pairs = [(home_ref.at[s, r], held.at[s]) for s in range(size)] + [(wt_hbm, wt_ref)]
    copies = [pltpu.make_async_copy(*pair, sems.at[i]) for i, pair in enumerate(pairs)]
    for copy in copies:
        copy.start()
    for s in range(size):
        copies[s].wait()
        stage[s * sub : (s + 1) * sub, :] = held[s]
    theta = stage[...].astype(BF16)
    theta_ref[...] = theta
    mine_ref[...] = held[z]
    rows = theta.shape[0]
    for by, send in enumerate(sends, 1):
        send[:rows, :] = theta
        send[rows:, :] = halves_of(held[partner(z, by, size)])[1]
    copies[size].wait()


def pair_terms(theta, e_refs, weight_refs, scratch, first=(), rest=()):
    wq_ref, wk_ref, wv_ref, ws_ref, bias_ref = weight_refs
    qk_ref, total_ref, pool_ref = scratch
    scale = 0.5 / math.sqrt(DH)
    blocks = len(theta)
    rows = theta[0].shape[0]
    heads = wk_ref.shape[1] // DH
    every = theta[0] if blocks == 1 else jnp.concatenate(theta, 0)
    wait_for(first)
    queries = dot(every, wq_ref[...]).astype(BF16)
    for h in range(heads):
        cols = slice(h * DH, (h + 1) * DH)
        turned = lax.dot_general(queries[:, cols], wk_ref[:, cols], NT, preferred_element_type=F32)
        turned = (turned * scale).astype(BF16)
        for b in range(blocks):
            at = (b * heads + h) * rows
            qk_ref[at : at + rows, :] = turned[b * rows : (b + 1) * rows]

    def weights(scores):
        parts = []
        for h in range(heads):
            bias = jnp.tile(bias_ref[h : h + 1, :], (1, scores.shape[1] // 128))
            parts.append(half_silu(scores[h * rows : (h + 1) * rows] + bias).astype(BF16))
        return jnp.concatenate(parts, 0)

    wait_for(rest)
    fresh = True
    for e_ref in e_refs:
        tile = math.gcd(TILE, e_ref.shape[0])
        for j in range(e_ref.shape[0] // tile):
            seen = e_ref[j * tile : (j + 1) * tile, :]
            for b in range(blocks):
                span = slice(b * heads * rows, (b + 1) * heads * rows)
                scores = lax.dot_general(qk_ref[span, :], seen, NT, preferred_element_type=F32)
                term = dot(weights(scores), seen)
                total_ref[span, :] = term if fresh else total_ref[span, :] + term
            fresh = False
    for h in range(heads):
        cols = slice(h * DH, (h + 1) * DH)
        for b in range(blocks):
            at = (b * heads + h) * rows
            pool_ref[b * rows : (b + 1) * rows, cols] = split_dot(
                total_ref[at : at + rows, :], wv_ref[:, cols]
            )
    return split_dot(pool_ref[...], ws_ref[...])


def home_body(size, nrep, heads, feats, level_ref, wt_ref, theta_ref, *refs):
    others, refs = refs[: nrep - 1], refs[nrep - 1 :]
    hbm, (terms_ref, bias_ref, mix_ref, feat_ref, *held) = refs[:5], refs[5:14]
    scratch, sems = refs[14:17], refs[17]
    copies = copies_of(hbm, held, sems)
    for copy in copies:
        copy.start()
    level = jnp.broadcast_to(level_ref[...].astype(F32), (1, 128))
    features, delta = plan(level, feats)
    mix_ref[0:1, :] = delta
    mix_ref[1:2, :] = jnp.sqrt(delta)
    feat = jnp.broadcast_to(features, (16, feats))
    feat_ref[...] = feat
    head_bias = lax.dot_general(wt_ref[...], feat, NT, preferred_element_type=F32) * 0.5
    bias_ref[...] = jnp.broadcast_to(head_bias[:, 0:1], (heads, 128))
    wq_ref, wk_ref, e_ref, wv_ref, ws_ref = held
    weights = (wq_ref, wk_ref, wv_ref, ws_ref, bias_ref)
    seen = [*others, e_ref]
    terms = pair_terms([theta_ref[...]], seen, weights, scratch, copies[:2], copies[2:])
    put_stripes(terms_ref, 0, size, terms)


def mid_body(size, got_ref, *refs):
    e_refs, weights, (terms_ref, *scratch) = refs[:-9], refs[-9:-4], refs[-4:]
    rows = terms_ref.shape[0] * terms_ref.shape[1]
    terms = pair_terms([got_ref[:rows, :]], e_refs, weights, scratch)
    put_stripes(terms_ref, 0, size, terms)


def far_body(size, nrep, *refs):
    nblk = size - 2
    home_ref, mid_ref, mine_ref = refs[:3]
    got, rest = refs[3 : 2 + size], refs[2 + size :]
    e_refs, rest = rest[:nrep], rest[nrep:]
    weights, (own_ref, part_ref) = rest[:5], rest[5:7]
    sends = rest[7 : 6 + size]
    *scratch, stage = rest[6 + size :]
    z = lax.axis_index("obs")
    sub = own_ref.shape[1]
    rows = size * sub
    part_ref[0] = mine_ref[...]
    for b in range(1, size):
        put_stripes(stage, 0, size, got[b - 1][:rows, :].astype(F32))
        part_ref[b] = stage[z] + got[b - 1][rows:, :].astype(F32)
    theta = [ref[:rows, :] for ref in got[1:]]
    terms = pair_terms(theta, e_refs, weights, scratch)
    put_stripes(stage, 0, nblk * size, terms)
    for k in range(size):
        held, first = (stage, (k - 2) * size) if k >= 2 else ((home_ref, mid_ref)[k], 0)
        own_ref[k] = held[first + z]
        for by, send in enumerate(sends, 1):
            send[k] = held[first + partner(z, by, size)].astype(BF16)


def prior_body(size, count, part_ref, feat_ref, *refs):
    hbm, (out_ref, stage), held, sems = refs[:3], refs[3:5], refs[5:8], refs[8]
    copies = copies_of(hbm, held, sems)
    for copy in copies:
        copy.start()
    pin_ref, pt_ref, pout_ref = held
    sub = part_ref.shape[1]
    for k in range(size):
        stage[k * sub : (k + 1) * sub, :] = part_ref[k]
    wait_for(copies)
    pre = dot(stage[...].astype(BF16), pin_ref[...]) + dot(feat_ref[...], pt_ref[...])[0:1]
    prior = dot(half_silu(0.5 * pre).astype(BF16), pout_ref[...])
    put_stripes(out_ref, 0, size, prior * -count)


def sum_body(size, order, *rest):
    own_ref, prior_ref, out_ref = rest[-3:]
    away = dict(zip(order, rest))
    for k in range(size):
        total = own_ref[k] + prior_ref[k]
        for by in range(1, size):
            total = total + away[by][source(k, by, size)].astype(F32)
        out_ref[k] = total.astype(out_ref.dtype)


def join_body(size, *refs):
    terms, out_ref = refs[:-1], refs[-1]
    for k in range(size):
        total = terms[0][k].astype(F32)
        for term in terms[1:]:
            total = total + term[k].astype(F32)
        out_ref[k] = total


def last_body(size, nrep, mix_ref, noise_ref, *rest):
    joined, parts, (updated_ref, score_ref) = rest[:nrep], rest[nrep:-2], rest[-2:]
    z, r = lax.axis_index("obs"), lax.axis_index("rep")
    reach = noise_ref.shape[-1] // 128
    delta = jnp.tile(mix_ref[0:1, :], (1, reach))
    root = jnp.tile(mix_ref[1:2, :], (1, reach))
    for away in range(nrep):
        rep = source(r, away, nrep)
        for k in range(size):
            block = source(z, k, size)
            total = joined[away][k]
            score_ref[block, rep] = total
            updated_ref[block, rep] = parts[away][k] + delta * total + root * noise_ref[block, rep]


def on_device(
    particles,
    obs_embed,
    step_index,
    noise,
    w_query,
    w_key,
    w_value,
    w_time,
    w_score,
    prior_in,
    prior_time,
    prior_out,
):
    size, nrep, nhid = lax.axis_size("obs"), lax.axis_size("rep"), lax.axis_size("hid")
    home = particles[0]
    block_rows, width = home.shape
    stripe = block_rows // size
    sub = stripe // nrep
    rows = size * sub
    heads = w_key.shape[1] // DH
    emb = obs_embed.shape[1]
    count = obs_embed.shape[0] * size * nrep - 1
    shifts = range(1, size)

    def shape(*dims, dtype=F32):
        return jax.ShapeDtypeStruct(dims, dtype)

    def scratch(blocks):
        return [
            pltpu.VMEM((blocks * heads * rows, emb), BF16),
            pltpu.VMEM((blocks * heads * rows, emb), F32),
            pltpu.VMEM((blocks * rows, heads * DH), F32),
        ]

    hbm = pl.BlockSpec(memory_space=pltpu.HBM)
    far_first = [*range(size // 2, size), *range(1, size // 2)]

    def exchanged(sends):
        moved = {by: passed_along(sends[by - 1], "obs", by) for by in far_first}
        return [moved[by] for by in shifts]

    seen = [passed_along(obs_embed, "rep", by) for by in range(1, nrep)]
    level = passed_along(step_index, "rep", 1).reshape(1, 1)
    time_weight = in_hbm(w_time.T)
    theta, mine, time_weight, *sends = call(
        functools.partial(prep_body, size),
        "prep",
        [
            shape(rows, width, dtype=BF16),
            shape(sub, width),
            shape(*time_weight.shape, dtype=BF16),
        ]
        + [shape(rows + sub, width, dtype=BF16) for _ in shifts],
        [hbm] * 2,
        [
            pltpu.VMEM((size, sub, width), F32),
            pltpu.VMEM((rows, width), F32),
            pltpu.SemaphoreType.DMA((size + 1,)),
        ],
    )(in_hbm(home.reshape(size, nrep, sub, width)), time_weight)
    got = exchanged(sends)

    pair_flops = 4 * rows * heads * obs_embed.shape[0] * nrep * emb
    feats = w_time.shape[0]
    operands = [in_hbm(x) for x in (w_query, w_key, obs_embed, w_value, w_score)]
    home_terms, bias, mix, feat, *held = call(
        functools.partial(home_body, size, nrep, heads, feats),
        "home_block",
        [
            shape(size, sub, width),
            shape(heads, 128),
            shape(2, 128),
            shape(16, feats, dtype=BF16),
        ]
        + [shape(*x.shape, dtype=x.dtype) for x in operands],
        [spec()] * (2 + nrep)
        + [hbm] * len(operands),
        scratch(1) + [pltpu.SemaphoreType.DMA((len(operands),))],
        pair_flops,
        24,
    )(level, time_weight, theta, *seen, *operands)
    query, key, e_home, value, out_weight = held
    weights = [*seen, e_home, query, key, value, out_weight, bias]
    mid_terms = call(
        functools.partial(mid_body, size),
        "mid_block",
        shape(size, sub, width),
        [spec()] * (1 + len(weights)),
        scratch(1),
        pair_flops,
        24,
    )(got[0], *weights)
    own, part, *leave = call(
        functools.partial(far_body, size, nrep),
        "far_blocks",
        [shape(size, sub, width), shape(size, sub, width)]
        + [shape(size, sub, width, dtype=BF16) for _ in shifts],
        [spec()] * (2 + size + len(weights)),
        scratch(size - 2) + [pltpu.VMEM(((size - 2) * size, sub, width), F32)],
        pair_flops * (size - 2),
        24,
    )(home_terms, mid_terms, mine, *got, *weights)
    operands = [in_hbm(x) for x in (prior_in, prior_time, prior_out)]
    prior = call(
        functools.partial(prior_body, size, float(count)),
        "prior",
        shape(size, sub, width),
        [spec()] * 2 + [hbm] * 3,
        [pltpu.VMEM((rows, width), F32)]
        + [pltpu.VMEM(x.shape, x.dtype) for x in operands]
        + [pltpu.SemaphoreType.DMA((len(operands),))],
        4 * rows * width * prior_in.shape[1],
        8,
    )(part, feat, *operands)
    arrived = exchanged(leave)
    two = nhid == 2
    summed = call(
        functools.partial(sum_body, size, far_first),
        "sum_obs",
        shape(size, sub, width, dtype=BF16 if two else F32),
        [spec()] * (size + 1),
    )(*[arrived[by - 1] for by in far_first], own, prior)
    if two:
        partial_sums = [summed, passed_along(summed, "hid", 1)]
    else:
        partial_sums = [lax.psum(summed, "hid")]
    joined = call(
        functools.partial(join_body, size),
        "join",
        shape(size, sub, width),
        [spec()] * len(partial_sums),
    )(*partial_sums)
    joined = [joined] + [passed_along(joined, "rep", by) for by in range(1, nrep)]
    parts = [part] + [passed_along(part, "rep", by) for by in range(1, nrep)]
    whole = shape(size, nrep, sub, width)
    updated, score = call(
        functools.partial(last_body, size, nrep),
        "last",
        [whole, whole],
        [spec()] * (2 + 2 * nrep),
    )(mix, noise.reshape(size, nrep, sub, width), *joined, *parts)
    return (updated.reshape(noise.shape), score.reshape(noise.shape))


def solution(mesh):
    in_specs = (
        P(("groups", "obs"), None, None),
        P(("groups", "obs", "rep"), None),
        P("groups"),
        P("groups", "obs", None),
        P(None, "hid"),
        P(None, "hid"),
        P(None, "hid"),
        P(None, "hid"),
        P("hid", None),
        P(None, "hid"),
        P(None, "hid"),
        P("hid", None),
    )
    out_specs = (P("groups", "obs", None), P("groups", "obs", None))
    return jax.shard_map(
        on_device, mesh=mesh, in_specs=in_specs, out_specs=out_specs, check_vma=False
    )
```

```python
import functools
import math

import jax
import jax.numpy as jnp
from jax import lax
from jax.experimental import pallas as pl
from jax.experimental.pallas import tpu as pltpu
from jax.sharding import PartitionSpec as P

DH = 128
STEPS = 64

SIG_LO = 0.05
SIG_HI = 1.0

F32 = jnp.float32
BF16 = jnp.bfloat16
NT = (((1,), (1,)), ((), ()))
TILE = 512
PREP_FLOPS = 4 << 30


def partner(index, by, size):
    if size & (size - 1) == 0:
        return index ^ by
    return (index + by) % size


def source(index, by, size):
    return partner(index, by if size & (size - 1) == 0 else size - by, size)


def passed_along(shard, axis, by):
    size = lax.axis_size(axis)
    return lax.ppermute(shard, axis, [(i, partner(i, by, size)) for i in range(size)])


def plan(level, feature_count):
    growth = math.log(SIG_HI / SIG_LO) / (STEPS - 1)
    sigma_now = SIG_LO * jnp.exp(growth * level)
    sigma_prev = SIG_LO * jnp.exp(growth * (level - 1.0))
    delta = sigma_now * sigma_now - sigma_prev * sigma_prev
    halves = feature_count // 2
    lane = lax.broadcasted_iota(jnp.int32, (1, halves), 1).astype(F32)
    angles = 10.0 * jnp.log(sigma_now[:, :1]) * jnp.exp(-math.log(1000.0) / halves * lane)
    features = jnp.concatenate([jnp.sin(angles), jnp.cos(angles)], 1).astype(BF16)
    return (features, delta)


def dot(a, b):
    return jnp.dot(a, b, preferred_element_type=F32)


def halves_of(x):
    high = x.astype(BF16)
    return high, (x - high.astype(F32)).astype(BF16)


def split_dot(x, weight):
    rows = x.shape[0]
    both = dot(jnp.concatenate(halves_of(x), 0), weight)
    return both[:rows] + both[rows:]


def half_silu(y):
    return y + y * jnp.tanh(y)


def put_stripes(stage, first, count, values):
    sub = stage.shape[1]
    for s in range(count):
        stage[first + s] = values[s * sub : (s + 1) * sub]


def spec():
    return pl.BlockSpec(memory_space=pltpu.VMEM)


def in_hbm(x):
    return pltpu.with_memory_space_constraint(x, pltpu.HBM)


def call(body, name, out_shape, in_specs, scratch=(), flops=0, limit=4):
    return pl.pallas_call(
        body,
        name=name,
        out_shape=out_shape,
        in_specs=in_specs,
        out_specs=jax.tree.map(lambda _: spec(), out_shape),
        scratch_shapes=list(scratch),
        cost_estimate=pl.CostEstimate(flops=flops, bytes_accessed=flops // 1000, transcendentals=0),
        compiler_params=pltpu.CompilerParams(vmem_limit_bytes=limit << 20),
    )


def copies_of(sources, targets, sems):
    return [
        pltpu.make_async_copy(source, target, sems.at[i])
        for i, (source, target) in enumerate(zip(sources, targets))
    ]


def wait_for(copies):
    for copy in copies:
        copy.wait()


def prep_body(size, home_ref, wt_hbm, theta_ref, mine_ref, wt_ref, *refs):
    sends, (held, stage, sems) = refs[: size - 1], refs[size - 1 :]
    z, r = lax.axis_index("obs"), lax.axis_index("rep")
    sub = held.shape[1]
    pairs = [(home_ref.at[s, r], held.at[s]) for s in range(size)] + [(wt_hbm, wt_ref)]
    copies = [pltpu.make_async_copy(*pair, sems.at[i]) for i, pair in enumerate(pairs)]
    for copy in copies:
        copy.start()
    for s in range(size):
        copies[s].wait()
        stage[s * sub : (s + 1) * sub, :] = held[s]
    theta = stage[...].astype(BF16)
    theta_ref[...] = theta
    mine_ref[...] = held[z]
    rows = theta.shape[0]
    for by, send in enumerate(sends, 1):
        send[:rows, :] = theta
        send[rows:, :] = halves_of(held[partner(z, by, size)])[1]
    copies[size].wait()


def pair_terms(theta, e_refs, weight_refs, scratch):
    wq_ref, wk_ref, wv_ref, ws_ref, bias_ref = weight_refs
    qk_ref, total_ref, pool_ref = scratch
    scale = 0.5 / math.sqrt(DH)
    blocks = len(theta)
    rows = theta[0].shape[0]
    heads = wk_ref.shape[1] // DH
    every = theta[0] if blocks == 1 else jnp.concatenate(theta, 0)
    queries = dot(every, wq_ref[...]).astype(BF16)
    for h in range(heads):
        cols = slice(h * DH, (h + 1) * DH)
        turned = lax.dot_general(queries[:, cols], wk_ref[:, cols], NT, preferred_element_type=F32)
        turned = (turned * scale).astype(BF16)
        for b in range(blocks):
            at = (b * heads + h) * rows
            qk_ref[at : at + rows, :] = turned[b * rows : (b + 1) * rows]

    def weights(scores):
        parts = []
        for h in range(heads):
            bias = jnp.tile(bias_ref[h : h + 1, :], (1, scores.shape[1] // 128))
            parts.append(half_silu(scores[h * rows : (h + 1) * rows] + bias).astype(BF16))
        return jnp.concatenate(parts, 0)

    fresh = True
    for e_ref in e_refs:
        tile = math.gcd(TILE, e_ref.shape[0])
        for j in range(e_ref.shape[0] // tile):
            seen = e_ref[j * tile : (j + 1) * tile, :]
            for b in range(blocks):
                span = slice(b * heads * rows, (b + 1) * heads * rows)
                scores = lax.dot_general(qk_ref[span, :], seen, NT, preferred_element_type=F32)
                term = dot(weights(scores), seen)
                total_ref[span, :] = term if fresh else total_ref[span, :] + term
            fresh = False
    for h in range(heads):
        cols = slice(h * DH, (h + 1) * DH)
        for b in range(blocks):
            at = (b * heads + h) * rows
            pool_ref[b * rows : (b + 1) * rows, cols] = split_dot(
                total_ref[at : at + rows, :], wv_ref[:, cols]
            )
    return split_dot(pool_ref[...], ws_ref[...])


def home_body(size, nrep, heads, feats, level_ref, wt_ref, theta_ref, *refs):
    e_refs, refs = refs[:nrep], refs[nrep:]
    weights, (terms_ref, bias_ref, mix_ref, feat_ref), scratch = refs[:4], refs[4:8], refs[8:]
    level = jnp.broadcast_to(level_ref[...].astype(F32), (1, 128))
    features, delta = plan(level, feats)
    mix_ref[0:1, :] = delta
    mix_ref[1:2, :] = jnp.sqrt(delta)
    feat = jnp.broadcast_to(features, (16, feats))
    feat_ref[...] = feat
    head_bias = lax.dot_general(wt_ref[...], feat, NT, preferred_element_type=F32) * 0.5
    bias_ref[...] = jnp.broadcast_to(head_bias[:, 0:1], (heads, 128))
    terms = pair_terms([theta_ref[...]], e_refs, (*weights, bias_ref), scratch)
    put_stripes(terms_ref, 0, size, terms)


def mid_body(size, got_ref, *refs):
    e_refs, weights, (terms_ref, *scratch) = refs[:-9], refs[-9:-4], refs[-4:]
    rows = terms_ref.shape[0] * terms_ref.shape[1]
    terms = pair_terms([got_ref[:rows, :]], e_refs, weights, scratch)
    put_stripes(terms_ref, 0, size, terms)


def far_body(size, nrep, order, *refs):
    nblk = size - 2
    got, (home_ref, mid_ref, mine_ref), rest = refs[: size - 1], refs[size - 1 : size + 2], refs[size + 2 :]
    got = [ref for _, ref in sorted(zip(order, got), key=lambda pair: pair[0])]
    e_refs, rest = rest[:nrep], rest[nrep:]
    weights, (own_ref, part_ref) = rest[:5], rest[5:7]
    sends = rest[7 : 6 + size]
    *scratch, stage = rest[6 + size :]
    z = lax.axis_index("obs")
    sub = own_ref.shape[1]
    rows = size * sub
    part_ref[0] = mine_ref[...]
    for b in range(1, size):
        put_stripes(stage, 0, size, got[b - 1][:rows, :].astype(F32))
        part_ref[b] = stage[z] + got[b - 1][rows:, :].astype(F32)
    theta = [ref[:rows, :] for ref in got[1:]]
    terms = pair_terms(theta, e_refs, weights, scratch)
    put_stripes(stage, 0, nblk * size, terms)
    for k in range(size):
        held, first = (stage, (k - 2) * size) if k >= 2 else ((home_ref, mid_ref)[k], 0)
        own_ref[k] = held[first + z]
        for by, send in enumerate(sends, 1):
            send[k] = held[first + partner(z, by, size)].astype(BF16)


def prior_body(size, count, part_ref, feat_ref, *refs):
    hbm, (out_ref, stage), held, sems = refs[:3], refs[3:5], refs[5:8], refs[8]
    copies = copies_of(hbm, held, sems)
    for copy in copies:
        copy.start()
    pin_ref, pt_ref, pout_ref = held
    sub = part_ref.shape[1]
    for k in range(size):
        stage[k * sub : (k + 1) * sub, :] = part_ref[k]
    wait_for(copies)
    pre = dot(stage[...].astype(BF16), pin_ref[...]) + dot(feat_ref[...], pt_ref[...])[0:1]
    prior = dot(half_silu(0.5 * pre).astype(BF16), pout_ref[...])
    put_stripes(out_ref, 0, size, prior * -count)


def sum_body(size, order, *rest):
    own_ref, prior_ref, out_ref = rest[-3:]
    away = dict(zip(order, rest))
    for k in range(size):
        total = own_ref[k] + prior_ref[k]
        for by in range(1, size):
            total = total + away[by][source(k, by, size)].astype(F32)
        out_ref[k] = total.astype(out_ref.dtype)


def join_body(size, *refs):
    terms, out_ref = refs[:-1], refs[-1]
    for k in range(size):
        total = terms[0][k].astype(F32)
        for term in terms[1:]:
            total = total + term[k].astype(F32)
        out_ref[k] = total


def last_body(size, nrep, mix_ref, noise_ref, *rest):
    joined, parts, (updated_ref, score_ref) = rest[:nrep], rest[nrep:-2], rest[-2:]
    z, r = lax.axis_index("obs"), lax.axis_index("rep")
    reach = noise_ref.shape[-1] // 128
    delta = jnp.tile(mix_ref[0:1, :], (1, reach))
    root = jnp.tile(mix_ref[1:2, :], (1, reach))
    for away in range(nrep):
        rep = source(r, away, nrep)
        for k in range(size):
            block = source(z, k, size)
            total = joined[away][k]
            score_ref[block, rep] = total
            updated_ref[block, rep] = parts[away][k] + delta * total + root * noise_ref[block, rep]


def on_device(
    particles,
    obs_embed,
    step_index,
    noise,
    w_query,
    w_key,
    w_value,
    w_time,
    w_score,
    prior_in,
    prior_time,
    prior_out,
):
    size, nrep, nhid = lax.axis_size("obs"), lax.axis_size("rep"), lax.axis_size("hid")
    home = particles[0]
    block_rows, width = home.shape
    stripe = block_rows // size
    sub = stripe // nrep
    rows = size * sub
    heads = w_key.shape[1] // DH
    emb = obs_embed.shape[1]
    count = obs_embed.shape[0] * size * nrep - 1
    shifts = range(1, size)

    def shape(*dims, dtype=F32):
        return jax.ShapeDtypeStruct(dims, dtype)

    def scratch(blocks):
        return [
            pltpu.VMEM((blocks * heads * rows, emb), BF16),
            pltpu.VMEM((blocks * heads * rows, emb), F32),
            pltpu.VMEM((blocks * rows, heads * DH), F32),
        ]

    hbm = pl.BlockSpec(memory_space=pltpu.HBM)
    far_first = [*range(size // 2, size), *range(1, size // 2)]

    def exchanged(sends):
        moved = {by: passed_along(sends[by - 1], "obs", by) for by in far_first}
        return [moved[by] for by in shifts]

    seen = [passed_along(obs_embed, "rep", by) for by in range(1, nrep)]
    level = passed_along(step_index, "rep", 1).reshape(1, 1)
    time_weight = in_hbm(w_time.T)
    theta, mine, time_weight, *sends = call(
        functools.partial(prep_body, size),
        "prep",
        [
            shape(rows, width, dtype=BF16),
            shape(sub, width),
            shape(*time_weight.shape, dtype=BF16),
        ]
        + [shape(rows + sub, width, dtype=BF16) for _ in shifts],
        [hbm] * 2,
        [
            pltpu.VMEM((size, sub, width), F32),
            pltpu.VMEM((rows, width), F32),
            pltpu.SemaphoreType.DMA((size + 1,)),
        ],
        PREP_FLOPS,
    )(in_hbm(home.reshape(size, nrep, sub, width)), time_weight)
    got = exchanged(sends)

    pair_flops = 4 * rows * heads * obs_embed.shape[0] * nrep * emb
    feats = w_time.shape[0]
    seen = [obs_embed, *seen]
    weights = [w_query, w_key, w_value, w_score]
    home_terms, bias, mix, feat = call(
        functools.partial(home_body, size, nrep, heads, feats),
        "home_block",
        [
            shape(size, sub, width),
            shape(heads, 128),
            shape(2, 128),
            shape(16, feats, dtype=BF16),
        ],
        [spec()] * (3 + nrep + len(weights)),
        scratch(1),
        pair_flops,
        16,
    )(level, time_weight, theta, *seen, *weights)
    weights = [*seen, *weights, bias]
    mid_terms = call(
        functools.partial(mid_body, size),
        "mid_block",
        shape(size, sub, width),
        [spec()] * (1 + len(weights)),
        scratch(1),
        pair_flops,
        24,
    )(got[0], *weights)
    own, part, *leave = call(
        functools.partial(far_body, size, nrep, far_first),
        "far_blocks",
        [shape(size, sub, width), shape(size, sub, width)]
        + [shape(size, sub, width, dtype=BF16) for _ in shifts],
        [spec()] * (2 + size + len(weights)),
        scratch(size - 2) + [pltpu.VMEM(((size - 2) * size, sub, width), F32)],
        pair_flops * (size - 2),
        24,
    )(*[got[by - 1] for by in far_first], home_terms, mid_terms, mine, *weights)
    operands = [in_hbm(x) for x in (prior_in, prior_time, prior_out)]
    prior = call(
        functools.partial(prior_body, size, float(count)),
        "prior",
        shape(size, sub, width),
        [spec()] * 2 + [hbm] * 3,
        [pltpu.VMEM((rows, width), F32)]
        + [pltpu.VMEM(x.shape, x.dtype) for x in operands]
        + [pltpu.SemaphoreType.DMA((len(operands),))],
        4 * rows * width * prior_in.shape[1],
        8,
    )(part, feat, *operands)
    arrived = exchanged(leave)
    two = nhid == 2
    summed = call(
        functools.partial(sum_body, size, far_first),
        "sum_obs",
        shape(size, sub, width, dtype=BF16 if two else F32),
        [spec()] * (size + 1),
    )(*[arrived[by - 1] for by in far_first], own, prior)
    if two:
        partial_sums = [summed, passed_along(summed, "hid", 1)]
    else:
        partial_sums = [lax.psum(summed, "hid")]
    joined = call(
        functools.partial(join_body, size),
        "join",
        shape(size, sub, width),
        [spec()] * len(partial_sums),
    )(*partial_sums)
    joined = [joined] + [passed_along(joined, "rep", by) for by in range(1, nrep)]
    parts = [part] + [passed_along(part, "rep", by) for by in range(1, nrep)]
    whole = shape(size, nrep, sub, width)
    updated, score = call(
        functools.partial(last_body, size, nrep),
        "last",
        [whole, whole],
        [spec()] * (2 + 2 * nrep),
    )(mix, noise.reshape(size, nrep, sub, width), *joined, *parts)
    return (updated.reshape(noise.shape), score.reshape(noise.shape))


def solution(mesh):
    in_specs = (
        P(("groups", "obs"), None, None),
        P(("groups", "obs", "rep"), None),
        P("groups"),
        P("groups", "obs", None),
        P(None, "hid"),
        P(None, "hid"),
        P(None, "hid"),
        P(None, "hid"),
        P("hid", None),
        P(None, "hid"),
        P(None, "hid"),
        P("hid", None),
    )
    out_specs = (P("groups", "obs", None), P("groups", "obs", None))
    return jax.shard_map(
        on_device, mesh=mesh, in_specs=in_specs, out_specs=out_specs, check_vma=False
    )
```

```python
import functools
import math

import jax
import jax.numpy as jnp
from jax import lax
from jax.experimental import pallas as pl
from jax.experimental.pallas import tpu as pltpu
from jax.sharding import PartitionSpec as P

DH = 128
STEPS = 64

SIG_LO = 0.05
SIG_HI = 1.0

F32 = jnp.float32
BF16 = jnp.bfloat16
NT = (((1,), (1,)), ((), ()))
TILE = 512
PREP_FLOPS = 4 << 30


def partner(index, by, size):
    if size & (size - 1) == 0:
        return index ^ by
    return (index + by) % size


def source(index, by, size):
    return partner(index, by if size & (size - 1) == 0 else size - by, size)


def passed_along(shard, axis, by):
    size = lax.axis_size(axis)
    return lax.ppermute(shard, axis, [(i, partner(i, by, size)) for i in range(size)])


def plan(level, feature_count):
    growth = math.log(SIG_HI / SIG_LO) / (STEPS - 1)
    sigma_now = SIG_LO * jnp.exp(growth * level)
    sigma_prev = SIG_LO * jnp.exp(growth * (level - 1.0))
    delta = sigma_now * sigma_now - sigma_prev * sigma_prev
    halves = feature_count // 2
    lane = lax.broadcasted_iota(jnp.int32, (1, halves), 1).astype(F32)
    angles = 10.0 * jnp.log(sigma_now[:, :1]) * jnp.exp(-math.log(1000.0) / halves * lane)
    features = jnp.concatenate([jnp.sin(angles), jnp.cos(angles)], 1).astype(BF16)
    return (features, delta)


def dot(a, b):
    return jnp.dot(a, b, preferred_element_type=F32)


def halves_of(x):
    high = x.astype(BF16)
    return high, (x - high.astype(F32)).astype(BF16)


def split_dot(x, weight):
    rows = x.shape[0]
    both = dot(jnp.concatenate(halves_of(x), 0), weight)
    return both[:rows] + both[rows:]


def half_silu(y):
    return y + y * jnp.tanh(y)


def put_stripes(target, values):
    count, sub = target.shape[:2]
    for s in range(count):
        target[s] = values[s * sub : (s + 1) * sub]


def others(ref, terms_ref):
    return ref[: padded(terms_ref.shape[0] * terms_ref.shape[1]), :]


def spec():
    return pl.BlockSpec(memory_space=pltpu.VMEM)


def in_hbm(x):
    return pltpu.with_memory_space_constraint(x, pltpu.HBM)


def call(body, name, out_shape, in_specs, scratch=(), flops=0, limit=4):
    return pl.pallas_call(
        body,
        name=name,
        out_shape=out_shape,
        in_specs=in_specs,
        out_specs=jax.tree.map(lambda _: spec(), out_shape),
        scratch_shapes=list(scratch),
        cost_estimate=pl.CostEstimate(flops=flops, bytes_accessed=flops // 1000, transcendentals=0),
        compiler_params=pltpu.CompilerParams(vmem_limit_bytes=limit << 20),
    )


def copies_of(sources, targets, sems):
    return [
        pltpu.make_async_copy(source, target, sems.at[i])
        for i, (source, target) in enumerate(zip(sources, targets))
    ]


def wait_for(copies):
    for copy in copies:
        copy.wait()


def padded(rows):
    return -(-rows // 16) * 16


def prep_body(size, home_ref, wt_hbm, theta_ref, mine_ref, wt_ref, *refs):
    sends, (held, stage, sems) = refs[: size - 1], refs[size - 1 :]
    z, r = lax.axis_index("obs"), lax.axis_index("rep")
    sub = held.shape[1]
    rows = stage.shape[0]
    copies = copies_of([home_ref.at[s, r] for s in range(size)], [held.at[s] for s in range(size)], sems)
    last = pltpu.make_async_copy(wt_hbm, wt_ref, sems.at[size])
    for copy in copies:
        copy.start()
    last.start()
    stage[...] = jnp.zeros_like(stage)
    wait_for(copies)
    for by, target_ref in enumerate((theta_ref, *sends)):
        target = partner(z, by, size)
        for k in range(1, size):
            stage[(k - 1) * sub : k * sub, :] = held[partner(target, k, size)]
        target_ref[:rows, :] = stage[...].astype(BF16)
        high, low = halves_of(held[target])
        target_ref[rows : rows + sub, :] = high
        if by:
            target_ref[rows + padded(sub) :, :] = low
    mine_ref[...] = held[z]
    last.wait()


def pair_terms(theta, e_refs, weight_refs, scratch):
    wq_ref, wk_ref, wv_ref, ws_ref, bias_ref = weight_refs
    qk_ref, total_ref, pool_ref = scratch
    scale = 0.5 / math.sqrt(DH)
    blocks = len(theta)
    rows = theta[0].shape[0]
    heads = wk_ref.shape[1] // DH
    every = theta[0] if blocks == 1 else jnp.concatenate(theta, 0)
    queries = dot(every, wq_ref[...]).astype(BF16)
    for h in range(heads):
        cols = slice(h * DH, (h + 1) * DH)
        turned = lax.dot_general(queries[:, cols], wk_ref[:, cols], NT, preferred_element_type=F32)
        turned = (turned * scale).astype(BF16)
        for b in range(blocks):
            at = (b * heads + h) * rows
            qk_ref[at : at + rows, :] = turned[b * rows : (b + 1) * rows]

    def weights(scores):
        parts = []
        for h in range(heads):
            bias = jnp.tile(bias_ref[h : h + 1, :], (1, scores.shape[1] // 128))
            parts.append(half_silu(scores[h * rows : (h + 1) * rows] + bias).astype(BF16))
        return jnp.concatenate(parts, 0)

    fresh = True
    for e_ref in e_refs:
        tile = math.gcd(TILE, e_ref.shape[0])
        for j in range(e_ref.shape[0] // tile):
            seen = e_ref[j * tile : (j + 1) * tile, :]
            for b in range(blocks):
                span = slice(b * heads * rows, (b + 1) * heads * rows)
                scores = lax.dot_general(qk_ref[span, :], seen, NT, preferred_element_type=F32)
                term = dot(weights(scores), seen)
                total_ref[span, :] = term if fresh else total_ref[span, :] + term
            fresh = False
    for h in range(heads):
        cols = slice(h * DH, (h + 1) * DH)
        for b in range(blocks):
            at = (b * heads + h) * rows
            pool_ref[b * rows : (b + 1) * rows, cols] = split_dot(
                total_ref[at : at + rows, :], wv_ref[:, cols]
            )
    return split_dot(pool_ref[...], ws_ref[...])


def home_body(size, nrep, heads, feats, level_ref, wt_ref, theta_ref, *refs):
    e_refs, refs = refs[:nrep], refs[nrep:]
    weights, (terms_ref, bias_ref, mix_ref, feat_ref), scratch = refs[:4], refs[4:8], refs[8:]
    level = jnp.broadcast_to(level_ref[...].astype(F32), (1, 128))
    features, delta = plan(level, feats)
    mix_ref[0:1, :] = delta
    mix_ref[1:2, :] = jnp.sqrt(delta)
    feat = jnp.broadcast_to(features, (16, feats))
    feat_ref[...] = feat
    head_bias = lax.dot_general(wt_ref[...], feat, NT, preferred_element_type=F32) * 0.5
    bias_ref[...] = jnp.broadcast_to(head_bias[:, 0:1], (heads, 128))
    terms = pair_terms([others(theta_ref, terms_ref)], e_refs, (*weights, bias_ref), scratch)
    put_stripes(terms_ref, terms)


def mid_body(got_ref, *refs):
    e_refs, weights, (terms_ref, *scratch) = refs[:-9], refs[-9:-4], refs[-4:]
    put_stripes(terms_ref, pair_terms([others(got_ref, terms_ref)], e_refs, weights, scratch))


def far_body(size, nrep, *refs):
    home_ref, mid_ref = refs[:2]
    got, rest = refs[2:size], refs[size:]
    e_refs, weights, rest = rest[:nrep], rest[nrep : nrep + 5], rest[nrep + 5 :]
    sends, token_ref, scratch = rest[: size - 1], rest[size - 1], rest[size:]
    sub = home_ref.shape[1]
    terms = pair_terms([others(ref, home_ref) for ref in got], e_refs, weights, scratch)
    rows = terms.shape[0] // len(got)
    for k, send in enumerate(sends):
        for b in range(size):
            if b < 2:
                send[b] = (home_ref, mid_ref)[b][k].astype(BF16)
            else:
                at = (b - 2) * rows + k * sub
                send[b] = terms[at : at + sub].astype(BF16)
    token_ref[...] = terms[:8, :128]


def own_body(size, nrep, count, token_ref, theta_ref, mine_ref, *refs):
    got, refs = refs[: size - 1], refs[size - 1 :]
    e_refs, weights, refs = refs[:nrep], refs[nrep : nrep + 5], refs[nrep + 5 :]
    feat_ref, pt_ref, pin_ref, pout_ref, own_ref, part_ref, *scratch, stage = refs
    sub = own_ref.shape[1]
    rows = padded((size - 1) * sub)
    part_ref[0] = mine_ref[...]
    for b, ref in enumerate((theta_ref, *got)):
        high = ref[rows : rows + sub, :].astype(F32)
        stage[b * sub : (b + 1) * sub, :] = high
        if b:
            part_ref[b] = high + ref[rows + padded(sub) :, :].astype(F32)
    theta = stage[...].astype(BF16)
    pre = dot(theta, pin_ref[...]) + dot(feat_ref[...], pt_ref[...])[0:1]
    prior = dot(half_silu(0.5 * pre).astype(BF16), pout_ref[...])
    terms = pair_terms([theta], e_refs, weights, scratch)
    put_stripes(own_ref, terms - count * prior)


def sum_body(size, order, *rest):
    own_ref, out_ref = rest[-2:]
    away = dict(zip(order, rest))
    for k in range(size):
        total = own_ref[k]
        for by in range(1, size):
            total = total + away[by][source(k, by, size)].astype(F32)
        out_ref[k] = total.astype(out_ref.dtype)


def join_body(size, *refs):
    terms, out_ref = refs[:-1], refs[-1]
    for k in range(size):
        total = terms[0][k].astype(F32)
        for term in terms[1:]:
            total = total + term[k].astype(F32)
        out_ref[k] = total


def last_body(size, nrep, mix_ref, noise_ref, *rest):
    joined, parts, (updated_ref, score_ref) = rest[:nrep], rest[nrep:-2], rest[-2:]
    z, r = lax.axis_index("obs"), lax.axis_index("rep")
    reach = noise_ref.shape[-1] // 128
    delta = jnp.tile(mix_ref[0:1, :], (1, reach))
    root = jnp.tile(mix_ref[1:2, :], (1, reach))
    for away in range(nrep):
        rep = source(r, away, nrep)
        for k in range(size):
            block = source(z, k, size)
            total = joined[away][k]
            score_ref[block, rep] = total
            updated_ref[block, rep] = parts[away][k] + delta * total + root * noise_ref[block, rep]


def on_device(
    particles,
    obs_embed,
    step_index,
    noise,
    w_query,
    w_key,
    w_value,
    w_time,
    w_score,
    prior_in,
    prior_time,
    prior_out,
):
    size, nrep, nhid = lax.axis_size("obs"), lax.axis_size("rep"), lax.axis_size("hid")
    home = particles[0]
    block_rows, width = home.shape
    stripe = block_rows // size
    sub = stripe // nrep
    rows = padded((size - 1) * sub)
    heads = w_key.shape[1] // DH
    emb = obs_embed.shape[1]
    count = obs_embed.shape[0] * size * nrep - 1
    shifts = range(1, size)

    def shape(*dims, dtype=F32):
        return jax.ShapeDtypeStruct(dims, dtype)

    def scratch(blocks, rows=rows):
        return [
            pltpu.VMEM((blocks * heads * rows, emb), BF16),
            pltpu.VMEM((blocks * heads * rows, emb), F32),
            pltpu.VMEM((blocks * rows, heads * DH), F32),
        ]

    hbm = pl.BlockSpec(memory_space=pltpu.HBM)
    far_first = [*range(size // 2, size), *range(1, size // 2)]
    seen = [passed_along(obs_embed, "rep", by) for by in range(1, nrep)]
    level = passed_along(step_index, "rep", 1).reshape(1, 1)
    time_weight = in_hbm(w_time.T)
    theta, mine, time_weight, *sends = call(
        functools.partial(prep_body, size),
        "prep",
        [
            shape(rows + sub, width, dtype=BF16),
            shape(sub, width),
            shape(*time_weight.shape, dtype=BF16),
        ]
        + [shape(rows + padded(sub) + sub, width, dtype=BF16) for _ in shifts],
        [hbm] * 2,
        [
            pltpu.VMEM((size, sub, width), F32),
            pltpu.VMEM((rows, width), F32),
            pltpu.SemaphoreType.DMA((size + 1,)),
        ],
        PREP_FLOPS,
    )(in_hbm(home.reshape(size, nrep, sub, width)), time_weight)
    got = [passed_along(send, "obs", by) for by, send in zip(shifts, sends)]

    pair_flops = 4 * rows * heads * obs_embed.shape[0] * nrep * emb
    feats = w_time.shape[0]
    seen = [obs_embed, *seen]
    weights = [w_query, w_key, w_value, w_score]
    terms_shape = shape(size - 1, sub, width)
    home_terms, bias, mix, feat = call(
        functools.partial(home_body, size, nrep, heads, feats),
        "home_block",
        [terms_shape, shape(heads, 128), shape(2, 128), shape(16, feats, dtype=BF16)],
        [spec()] * (3 + nrep + len(weights)),
        scratch(1),
        pair_flops,
        16,
    )(level, time_weight, theta, *seen, *weights)
    weights = [*seen, *weights, bias]
    mid_terms = call(
        mid_body,
        "mid_block",
        terms_shape,
        [spec()] * (1 + len(weights)),
        scratch(1),
        pair_flops,
        16,
    )(got[0], *weights)
    *leave, token = call(
        functools.partial(far_body, size, nrep),
        "far_blocks",
        [shape(size, sub, width, dtype=BF16) for _ in shifts] + [shape(8, 128)],
        [spec()] * (size + len(weights)),
        scratch(size - 2),
        pair_flops * (size - 2),
        24,
    )(home_terms, mid_terms, *got[1:], *weights)
    moved = {by: passed_along(leave[by - 1], "obs", by) for by in far_first}
    own, part = call(
        functools.partial(own_body, size, nrep, float(count)),
        "own_rows",
        [shape(size, sub, width), shape(size, sub, width)],
        [spec()] * (3 + size - 1 + len(weights) + 4),
        scratch(1, size * sub) + [pltpu.VMEM((size * sub, width), F32)],
        pair_flops,
        20,
    )(token, theta, mine, *got, *weights, feat, prior_time, prior_in, prior_out)
    two = nhid == 2
    summed = call(
        functools.partial(sum_body, size, far_first),
        "sum_obs",
        shape(size, sub, width, dtype=BF16 if two else F32),
        [spec()] * size,
    )(*[moved[by] for by in far_first], own)
    if two:
        partial_sums = [summed, passed_along(summed, "hid", 1)]
    else:
        partial_sums = [lax.psum(summed, "hid")]
    joined = call(
        functools.partial(join_body, size),
        "join",
        shape(size, sub, width),
        [spec()] * len(partial_sums),
    )(*partial_sums)
    joined = [joined] + [passed_along(joined, "rep", by) for by in range(1, nrep)]
    parts = [part] + [passed_along(part, "rep", by) for by in range(1, nrep)]
    whole = shape(size, nrep, sub, width)
    updated, score = call(
        functools.partial(last_body, size, nrep),
        "last",
        [whole, whole],
        [spec()] * (2 + 2 * nrep),
    )(mix, noise.reshape(size, nrep, sub, width), *joined, *parts)
    return (updated.reshape(noise.shape), score.reshape(noise.shape))


def solution(mesh):
    in_specs = (
        P(("groups", "obs"), None, None),
        P(("groups", "obs", "rep"), None),
        P("groups"),
        P("groups", "obs", None),
        P(None, "hid"),
        P(None, "hid"),
        P(None, "hid"),
        P(None, "hid"),
        P("hid", None),
        P(None, "hid"),
        P(None, "hid"),
        P("hid", None),
    )
    out_specs = (P("groups", "obs", None), P("groups", "obs", None))
    return jax.shard_map(
        on_device, mesh=mesh, in_specs=in_specs, out_specs=out_specs, check_vma=False
    )
```

```python
import functools
import math

import jax
import jax.numpy as jnp
from jax import lax
from jax.experimental import pallas as pl
from jax.experimental.pallas import tpu as pltpu
from jax.sharding import PartitionSpec as P

DH = 128
STEPS = 64

SIG_LO = 0.05
SIG_HI = 1.0

F32 = jnp.float32
BF16 = jnp.bfloat16
NT = (((1,), (1,)), ((), ()))
TILE = 512
PREP_FLOPS = 4 << 30


def partner(index, by, size):
    if size & (size - 1) == 0:
        return index ^ by
    return (index + by) % size


def source(index, by, size):
    return partner(index, by if size & (size - 1) == 0 else size - by, size)


def passed_along(shard, axis, by):
    size = lax.axis_size(axis)
    return lax.ppermute(shard, axis, [(i, partner(i, by, size)) for i in range(size)])


def plan(level, feature_count):
    growth = math.log(SIG_HI / SIG_LO) / (STEPS - 1)
    sigma_now = SIG_LO * jnp.exp(growth * level)
    sigma_prev = SIG_LO * jnp.exp(growth * (level - 1.0))
    delta = sigma_now * sigma_now - sigma_prev * sigma_prev
    halves = feature_count // 2
    lane = lax.broadcasted_iota(jnp.int32, (1, halves), 1).astype(F32)
    angles = 10.0 * jnp.log(sigma_now[:, :1]) * jnp.exp(-math.log(1000.0) / halves * lane)
    features = jnp.concatenate([jnp.sin(angles), jnp.cos(angles)], 1).astype(BF16)
    return (features, delta)


def dot(a, b):
    return jnp.dot(a, b, preferred_element_type=F32)


def halves_of(x):
    high = x.astype(BF16)
    return high, (x - high.astype(F32)).astype(BF16)


def split_dot(x, weight):
    rows = x.shape[0]
    both = dot(jnp.concatenate(halves_of(x), 0), weight)
    return both[:rows] + both[rows:]


def half_silu(y):
    return y + y * jnp.tanh(y)


def put_stripes(target, values):
    count, sub = target.shape[:2]
    for s in range(count):
        target[s] = values[s * sub : (s + 1) * sub]


def others(ref, terms_ref):
    return ref[: padded(terms_ref.shape[0] * terms_ref.shape[1]), :]


def spec():
    return pl.BlockSpec(memory_space=pltpu.VMEM)


def in_hbm(x):
    return pltpu.with_memory_space_constraint(x, pltpu.HBM)


def call(body, name, out_shape, in_specs, scratch=(), flops=0, limit=4):
    return pl.pallas_call(
        body,
        name=name,
        out_shape=out_shape,
        in_specs=in_specs,
        out_specs=jax.tree.map(lambda _: spec(), out_shape),
        scratch_shapes=list(scratch),
        cost_estimate=pl.CostEstimate(flops=flops, bytes_accessed=flops // 1000, transcendentals=0),
        compiler_params=pltpu.CompilerParams(vmem_limit_bytes=limit << 20),
    )


def copies_of(sources, targets, sems):
    return [
        pltpu.make_async_copy(source, target, sems.at[i])
        for i, (source, target) in enumerate(zip(sources, targets))
    ]


def wait_for(copies):
    for copy in copies:
        copy.wait()


def padded(rows):
    return -(-rows // 16) * 16


def prep_body(size, home_ref, wt_hbm, theta_ref, mine_ref, wt_ref, *refs):
    sends, (held, stage, sems) = refs[: size - 1], refs[size - 1 :]
    z, r = lax.axis_index("obs"), lax.axis_index("rep")
    sub = held.shape[1]
    rows = stage.shape[0]
    copies = copies_of([home_ref.at[s, r] for s in range(size)], [held.at[s] for s in range(size)], sems)
    last = pltpu.make_async_copy(wt_hbm, wt_ref, sems.at[size])
    for copy in copies:
        copy.start()
    last.start()
    stage[...] = jnp.zeros_like(stage)
    wait_for(copies)
    for by, target_ref in enumerate((theta_ref, *sends)):
        target = partner(z, by, size)
        for k in range(1, size):
            stage[(k - 1) * sub : k * sub, :] = held[partner(target, k, size)]
        target_ref[:rows, :] = stage[...].astype(BF16)
        target_ref[rows:, :] = held[target].astype(BF16)
    mine_ref[...] = held[z]
    last.wait()


def pair_terms(theta, e_refs, weight_refs, scratch, planned=None):
    wq_ref, wk_ref, wv_ref, ws_ref, bias_ref = weight_refs
    qk_ref, total_ref, pool_ref = scratch
    scale = 0.5 / math.sqrt(DH)
    blocks = len(theta)
    rows = theta[0].shape[0]
    heads = wk_ref.shape[1] // DH
    every = theta[0] if blocks == 1 else jnp.concatenate(theta, 0)
    queries = dot(every, wq_ref[...]).astype(BF16)
    for h in range(heads):
        cols = slice(h * DH, (h + 1) * DH)
        turned = lax.dot_general(queries[:, cols], wk_ref[:, cols], NT, preferred_element_type=F32)
        turned = (turned * scale).astype(BF16)
        for b in range(blocks):
            at = (b * heads + h) * rows
            qk_ref[at : at + rows, :] = turned[b * rows : (b + 1) * rows]

    if planned:
        planned()

    def weights(scores):
        parts = []
        for h in range(heads):
            bias = jnp.tile(bias_ref[h : h + 1, :], (1, scores.shape[1] // 128))
            parts.append(half_silu(scores[h * rows : (h + 1) * rows] + bias).astype(BF16))
        return jnp.concatenate(parts, 0)

    fresh = True
    for e_ref in e_refs:
        tile = math.gcd(TILE, e_ref.shape[0])
        for j in range(e_ref.shape[0] // tile):
            seen = e_ref[j * tile : (j + 1) * tile, :]
            for b in range(blocks):
                span = slice(b * heads * rows, (b + 1) * heads * rows)
                scores = lax.dot_general(qk_ref[span, :], seen, NT, preferred_element_type=F32)
                term = dot(weights(scores), seen)
                total_ref[span, :] = term if fresh else total_ref[span, :] + term
            fresh = False
    for h in range(heads):
        cols = slice(h * DH, (h + 1) * DH)
        for b in range(blocks):
            at = (b * heads + h) * rows
            pool_ref[b * rows : (b + 1) * rows, cols] = split_dot(
                total_ref[at : at + rows, :], wv_ref[:, cols]
            )
    return split_dot(pool_ref[...], ws_ref[...])


def home_body(size, nrep, heads, feats, level_hbm, wt_ref, theta_ref, *refs):
    e_refs, refs = refs[:nrep], refs[nrep:]
    weights, (terms_ref, bias_ref, mix_ref, feat_ref), scratch = refs[:4], refs[4:8], refs[8:11]
    level_ref, sem = refs[11:]
    copy = pltpu.make_async_copy(level_hbm, level_ref, sem)
    copy.start()

    def planned():
        copy.wait()
        level = jnp.broadcast_to(level_ref[...].astype(F32), (1, 128))
        features, delta = plan(level, feats)
        mix_ref[0:1, :] = delta
        mix_ref[1:2, :] = jnp.sqrt(delta)
        feat = jnp.broadcast_to(features, (16, feats))
        feat_ref[...] = feat
        head_bias = lax.dot_general(wt_ref[...], feat, NT, preferred_element_type=F32) * 0.5
        bias_ref[...] = jnp.broadcast_to(head_bias[:, 0:1], (heads, 128))

    theta = [others(theta_ref, terms_ref)]
    put_stripes(terms_ref, pair_terms(theta, e_refs, (*weights, bias_ref), scratch, planned))


def mid_body(got_ref, *refs):
    e_refs, weights, (terms_ref, *scratch) = refs[:-9], refs[-9:-4], refs[-4:]
    put_stripes(terms_ref, pair_terms([others(got_ref, terms_ref)], e_refs, weights, scratch))


def far_body(size, nrep, *refs):
    home_ref, mid_ref = refs[:2]
    got, rest = refs[2:size], refs[size:]
    e_refs, weights, rest = rest[:nrep], rest[nrep : nrep + 5], rest[nrep + 5 :]
    sends, token_ref, scratch = rest[: size - 1], rest[size - 1], rest[size:]
    sub = home_ref.shape[1]
    terms = pair_terms([others(ref, home_ref) for ref in got], e_refs, weights, scratch)
    rows = terms.shape[0] // len(got)
    for k, send in enumerate(sends):
        for b in range(size):
            if b < 2:
                send[b] = (home_ref, mid_ref)[b][k].astype(BF16)
            else:
                at = (b - 2) * rows + k * sub
                send[b] = terms[at : at + sub].astype(BF16)
    token_ref[...] = terms[:8, :128]


def own_body(size, nrep, count, token_ref, theta_ref, mine_ref, *refs):
    got, refs = refs[: size - 1], refs[size - 1 :]
    e_refs, weights, refs = refs[:nrep], refs[nrep : nrep + 5], refs[nrep + 5 :]
    feat_ref, pt_ref, pin_ref, pout_ref, own_ref, part_ref, *scratch, stage = refs
    sub = own_ref.shape[1]
    rows = padded((size - 1) * sub)
    part_ref[0] = mine_ref[...]
    for b, ref in enumerate((theta_ref, *got)):
        owned = ref[rows:, :].astype(F32)
        stage[b * sub : (b + 1) * sub, :] = owned
        if b:
            part_ref[b] = owned
    theta = stage[...].astype(BF16)
    pre = dot(theta, pin_ref[...]) + dot(feat_ref[...], pt_ref[...])[0:1]
    prior = dot(half_silu(0.5 * pre).astype(BF16), pout_ref[...])
    terms = pair_terms([theta], e_refs, weights, scratch)
    put_stripes(own_ref, terms - count * prior)


def sum_body(size, order, *rest):
    own_ref, out_ref = rest[-2:]
    away = dict(zip(order, rest))
    for k in range(size):
        total = own_ref[k]
        for by in range(1, size):
            total = total + away[by][source(k, by, size)].astype(F32)
        out_ref[k] = total.astype(out_ref.dtype)


def join_body(size, *refs):
    terms, out_ref = refs[:-1], refs[-1]
    for k in range(size):
        total = terms[0][k].astype(F32)
        for term in terms[1:]:
            total = total + term[k].astype(F32)
        out_ref[k] = total


def last_body(size, nrep, mix_ref, noise_ref, *rest):
    joined, parts, (updated_ref, score_ref) = rest[:nrep], rest[nrep:-2], rest[-2:]
    z, r = lax.axis_index("obs"), lax.axis_index("rep")
    reach = noise_ref.shape[-1] // 128
    delta = jnp.tile(mix_ref[0:1, :], (1, reach))
    root = jnp.tile(mix_ref[1:2, :], (1, reach))
    for away in range(nrep):
        rep = source(r, away, nrep)
        for k in range(size):
            block = source(z, k, size)
            total = joined[away][k]
            score_ref[block, rep] = total
            updated_ref[block, rep] = parts[away][k] + delta * total + root * noise_ref[block, rep]


def on_device(
    particles,
    obs_embed,
    step_index,
    noise,
    w_query,
    w_key,
    w_value,
    w_time,
    w_score,
    prior_in,
    prior_time,
    prior_out,
):
    size, nrep, nhid = lax.axis_size("obs"), lax.axis_size("rep"), lax.axis_size("hid")
    home = particles[0]
    block_rows, width = home.shape
    stripe = block_rows // size
    sub = stripe // nrep
    rows = padded((size - 1) * sub)
    heads = w_key.shape[1] // DH
    emb = obs_embed.shape[1]
    count = obs_embed.shape[0] * size * nrep - 1
    shifts = range(1, size)

    def shape(*dims, dtype=F32):
        return jax.ShapeDtypeStruct(dims, dtype)

    def scratch(blocks, rows=rows):
        return [
            pltpu.VMEM((blocks * heads * rows, emb), BF16),
            pltpu.VMEM((blocks * heads * rows, emb), F32),
            pltpu.VMEM((blocks * rows, heads * DH), F32),
        ]

    hbm = pl.BlockSpec(memory_space=pltpu.HBM)
    far_first = [*range(size // 2, size), *range(1, size // 2)]
    seen = [passed_along(obs_embed, "rep", by) for by in range(1, nrep)]
    level = passed_along(step_index, "rep", 1).reshape(1, 1)
    time_weight = in_hbm(w_time.T)
    theta, mine, time_weight, *sends = call(
        functools.partial(prep_body, size),
        "prep",
        [
            shape(rows + sub, width, dtype=BF16),
            shape(sub, width),
            shape(*time_weight.shape, dtype=BF16),
        ]
        + [shape(rows + sub, width, dtype=BF16) for _ in shifts],
        [hbm] * 2,
        [
            pltpu.VMEM((size, sub, width), F32),
            pltpu.VMEM((rows, width), F32),
            pltpu.SemaphoreType.DMA((size + 1,)),
        ],
        PREP_FLOPS,
    )(in_hbm(home.reshape(size, nrep, sub, width)), time_weight)
    got = [passed_along(send, "obs", by) for by, send in zip(shifts, sends)]

    pair_flops = 4 * rows * heads * obs_embed.shape[0] * nrep * emb
    feats = w_time.shape[0]
    seen = [obs_embed, *seen]
    weights = [w_query, w_key, w_value, w_score]
    terms_shape = shape(size - 1, sub, width)
    home_terms, bias, mix, feat = call(
        functools.partial(home_body, size, nrep, heads, feats),
        "home_block",
        [terms_shape, shape(heads, 128), shape(2, 128), shape(16, feats, dtype=BF16)],
        [hbm] + [spec()] * (2 + nrep + len(weights)),
        scratch(1) + [pltpu.VMEM((1, 1), jnp.int32), pltpu.SemaphoreType.DMA(())],
        pair_flops,
        16,
    )(in_hbm(level), time_weight, theta, *seen, *weights)
    weights = [*seen, *weights, bias]
    mid_terms = call(
        mid_body,
        "mid_block",
        terms_shape,
        [spec()] * (1 + len(weights)),
        scratch(1),
        pair_flops,
        16,
    )(got[0], *weights)
    *leave, token = call(
        functools.partial(far_body, size, nrep),
        "far_blocks",
        [shape(size, sub, width, dtype=BF16) for _ in shifts] + [shape(8, 128)],
        [spec()] * (size + len(weights)),
        scratch(size - 2),
        pair_flops * (size - 2),
        24,
    )(home_terms, mid_terms, *got[1:], *weights)
    moved = {by: passed_along(leave[by - 1], "obs", by) for by in far_first}
    own, part = call(
        functools.partial(own_body, size, nrep, float(count)),
        "own_rows",
        [shape(size, sub, width), shape(size, sub, width)],
        [spec()] * (3 + size - 1 + len(weights) + 4),
        scratch(1, size * sub) + [pltpu.VMEM((size * sub, width), F32)],
        pair_flops,
        20,
    )(token, theta, mine, *got, *weights, feat, prior_time, prior_in, prior_out)
    two = nhid == 2
    summed = call(
        functools.partial(sum_body, size, far_first),
        "sum_obs",
        shape(size, sub, width, dtype=BF16 if two else F32),
        [spec()] * size,
    )(*[moved[by] for by in far_first], own)
    if two:
        partial_sums = [summed, passed_along(summed, "hid", 1)]
    else:
        partial_sums = [lax.psum(summed, "hid")]
    joined = call(
        functools.partial(join_body, size),
        "join",
        shape(size, sub, width),
        [spec()] * len(partial_sums),
    )(*partial_sums)
    joined = [joined] + [passed_along(joined, "rep", by) for by in range(1, nrep)]
    parts = [part] + [passed_along(part, "rep", by) for by in range(1, nrep)]
    whole = shape(size, nrep, sub, width)
    updated, score = call(
        functools.partial(last_body, size, nrep),
        "last",
        [whole, whole],
        [spec()] * (2 + 2 * nrep),
    )(mix, noise.reshape(size, nrep, sub, width), *joined, *parts)
    return (updated.reshape(noise.shape), score.reshape(noise.shape))


def solution(mesh):
    in_specs = (
        P(("groups", "obs"), None, None),
        P(("groups", "obs", "rep"), None),
        P("groups"),
        P("groups", "obs", None),
        P(None, "hid"),
        P(None, "hid"),
        P(None, "hid"),
        P(None, "hid"),
        P("hid", None),
        P(None, "hid"),
        P(None, "hid"),
        P("hid", None),
    )
    out_specs = (P("groups", "obs", None), P("groups", "obs", None))
    return jax.shard_map(
        on_device, mesh=mesh, in_specs=in_specs, out_specs=out_specs, check_vma=False
    )
```

```python
import functools
import math

import jax
import jax.numpy as jnp
from jax import lax
from jax.experimental import pallas as pl
from jax.experimental.pallas import tpu as pltpu
from jax.sharding import PartitionSpec as P

DH = 128
STEPS = 64

SIG_LO = 0.05
SIG_HI = 1.0

F32 = jnp.float32
BF16 = jnp.bfloat16
NT = (((1,), (1,)), ((), ()))
TILE = 512
PREP_FLOPS = 4 << 30


def partner(index, by, size):
    if size & (size - 1) == 0:
        return index ^ by
    return (index + by) % size


def source(index, by, size):
    return partner(index, by if size & (size - 1) == 0 else size - by, size)


def passed_along(shard, axis, by):
    size = lax.axis_size(axis)
    return lax.ppermute(shard, axis, [(i, partner(i, by, size)) for i in range(size)])


def plan(level, feature_count):
    growth = math.log(SIG_HI / SIG_LO) / (STEPS - 1)
    sigma_now = SIG_LO * jnp.exp(growth * level)
    sigma_prev = SIG_LO * jnp.exp(growth * (level - 1.0))
    delta = sigma_now * sigma_now - sigma_prev * sigma_prev
    halves = feature_count // 2
    lane = lax.broadcasted_iota(jnp.int32, (1, halves), 1).astype(F32)
    angles = 10.0 * jnp.log(sigma_now[:, :1]) * jnp.exp(-math.log(1000.0) / halves * lane)
    features = jnp.concatenate([jnp.sin(angles), jnp.cos(angles)], 1).astype(BF16)
    return (features, delta)


def dot(a, b):
    return jnp.dot(a, b, preferred_element_type=F32)


def halves_of(x):
    high = x.astype(BF16)
    return high, (x - high.astype(F32)).astype(BF16)


def split_dot(x, weight):
    rows = x.shape[0]
    both = dot(jnp.concatenate(halves_of(x), 0), weight)
    return both[:rows] + both[rows:]


def half_silu(y):
    return y + y * jnp.tanh(y)


def put_stripes(target, values):
    count, sub = target.shape[:2]
    for s in range(count):
        target[s] = values[s * sub : (s + 1) * sub]


def others(ref, terms_ref):
    return ref[: padded(terms_ref.shape[0] * terms_ref.shape[1]), :]


def spec():
    return pl.BlockSpec(memory_space=pltpu.VMEM)


def in_hbm(x):
    return pltpu.with_memory_space_constraint(x, pltpu.HBM)


def call(body, name, out_shape, in_specs, scratch=(), flops=0, limit=4, out_spec=None, aliases={}):
    return pl.pallas_call(
        body,
        name=name,
        out_shape=out_shape,
        in_specs=in_specs,
        out_specs=jax.tree.map(lambda _: out_spec or spec(), out_shape),
        scratch_shapes=list(scratch),
        input_output_aliases=aliases,
        cost_estimate=pl.CostEstimate(flops=flops, bytes_accessed=flops // 1000, transcendentals=0),
        compiler_params=pltpu.CompilerParams(vmem_limit_bytes=limit << 20),
    )


def copies_of(sources, targets, sems):
    return [
        pltpu.make_async_copy(source, target, sems.at[i])
        for i, (source, target) in enumerate(zip(sources, targets))
    ]


def wait_for(copies):
    for copy in copies:
        copy.wait()


def padded(rows):
    return -(-rows // 16) * 16


def prep_body(size, home_ref, wt_hbm, theta_ref, mine_ref, wt_ref, *refs):
    sends, (held, stage, sems) = refs[: size - 1], refs[size - 1 :]
    z, r = lax.axis_index("obs"), lax.axis_index("rep")
    sub = held.shape[1]
    rows = stage.shape[0]
    copies = copies_of([home_ref.at[s, r] for s in range(size)], [held.at[s] for s in range(size)], sems)
    last = pltpu.make_async_copy(wt_hbm, wt_ref, sems.at[size])
    for copy in copies:
        copy.start()
    last.start()
    stage[...] = jnp.zeros_like(stage)
    wait_for(copies)
    for by, target_ref in enumerate((theta_ref, *sends)):
        target = partner(z, by, size)
        for k in range(1, size):
            stage[(k - 1) * sub : k * sub, :] = held[partner(target, k, size)]
        target_ref[:rows, :] = stage[...].astype(BF16)
        target_ref[rows:, :] = held[target].astype(BF16)
    mine_ref[...] = held[z]
    last.wait()


def pair_terms(theta, e_refs, weight_refs, scratch):
    wq_ref, wk_ref, wv_ref, ws_ref, bias_ref = weight_refs
    qk_ref, total_ref, pool_ref = scratch
    scale = 0.5 / math.sqrt(DH)
    blocks = len(theta)
    rows = theta[0].shape[0]
    heads = wk_ref.shape[1] // DH
    every = theta[0] if blocks == 1 else jnp.concatenate(theta, 0)
    queries = dot(every, wq_ref[...]).astype(BF16)
    for h in range(heads):
        cols = slice(h * DH, (h + 1) * DH)
        turned = lax.dot_general(queries[:, cols], wk_ref[:, cols], NT, preferred_element_type=F32)
        turned = (turned * scale).astype(BF16)
        for b in range(blocks):
            at = (b * heads + h) * rows
            qk_ref[at : at + rows, :] = turned[b * rows : (b + 1) * rows]

    def weights(scores):
        parts = []
        for h in range(heads):
            bias = jnp.tile(bias_ref[h : h + 1, :], (1, scores.shape[1] // 128))
            parts.append(half_silu(scores[h * rows : (h + 1) * rows] + bias).astype(BF16))
        return jnp.concatenate(parts, 0)

    fresh = True
    for e_ref in e_refs:
        tile = math.gcd(TILE, e_ref.shape[0])
        for j in range(e_ref.shape[0] // tile):
            seen = e_ref[j * tile : (j + 1) * tile, :]
            for b in range(blocks):
                span = slice(b * heads * rows, (b + 1) * heads * rows)
                scores = lax.dot_general(qk_ref[span, :], seen, NT, preferred_element_type=F32)
                term = dot(weights(scores), seen)
                total_ref[span, :] = term if fresh else total_ref[span, :] + term
            fresh = False
    for h in range(heads):
        cols = slice(h * DH, (h + 1) * DH)
        for b in range(blocks):
            at = (b * heads + h) * rows
            pool_ref[b * rows : (b + 1) * rows, cols] = split_dot(
                total_ref[at : at + rows, :], wv_ref[:, cols]
            )
    return split_dot(pool_ref[...], ws_ref[...])


def home_body(size, nrep, heads, feats, level_ref, wt_ref, theta_ref, *refs):
    e_refs, refs = refs[:nrep], refs[nrep:]
    weights, (terms_ref, bias_ref, mix_ref, feat_ref), scratch = refs[:4], refs[4:8], refs[8:]
    level = jnp.broadcast_to(level_ref[...].astype(F32), (1, 128))
    features, delta = plan(level, feats)
    mix_ref[0:1, :] = delta
    mix_ref[1:2, :] = jnp.sqrt(delta)
    feat = jnp.broadcast_to(features, (16, feats))
    feat_ref[...] = feat
    head_bias = lax.dot_general(wt_ref[...], feat, NT, preferred_element_type=F32) * 0.5
    bias_ref[...] = jnp.broadcast_to(head_bias[:, 0:1], (heads, 128))
    theta = [others(theta_ref, terms_ref)]
    put_stripes(terms_ref, pair_terms(theta, e_refs, (*weights, bias_ref), scratch))


def mid_body(got_ref, *refs):
    e_refs, weights, (terms_ref, *scratch) = refs[:-9], refs[-9:-4], refs[-4:]
    put_stripes(terms_ref, pair_terms([others(got_ref, terms_ref)], e_refs, weights, scratch))


def far_body(size, nrep, *refs):
    home_ref, mid_ref = refs[:2]
    got, rest = refs[2:size], refs[size:]
    e_refs, weights, rest = rest[:nrep], rest[nrep : nrep + 5], rest[nrep + 5 :]
    sends, token_ref, scratch = rest[: size - 1], rest[size - 1], rest[size:]
    sub = home_ref.shape[1]
    terms = pair_terms([others(ref, home_ref) for ref in got], e_refs, weights, scratch)
    rows = terms.shape[0] // len(got)
    for k, send in enumerate(sends):
        for b in range(size):
            if b < 2:
                send[b] = (home_ref, mid_ref)[b][k].astype(BF16)
            else:
                at = (b - 2) * rows + k * sub
                send[b] = terms[at : at + sub].astype(BF16)
    token_ref[...] = terms[:8, :128]


def own_body(size, nrep, count, token_ref, theta_ref, mine_ref, *refs):
    got, refs = refs[: size - 1], refs[size - 1 :]
    e_refs, weights, refs = refs[:nrep], refs[nrep : nrep + 5], refs[nrep + 5 :]
    feat_ref, pt_ref, pin_ref, pout_ref, own_ref, part_ref, *scratch, stage = refs
    sub = own_ref.shape[1]
    rows = padded((size - 1) * sub)
    part_ref[0] = mine_ref[...]
    for b, ref in enumerate((theta_ref, *got)):
        owned = ref[rows:, :].astype(F32)
        stage[b * sub : (b + 1) * sub, :] = owned
        if b:
            part_ref[b] = owned
    theta = stage[...].astype(BF16)
    pre = dot(theta, pin_ref[...]) + dot(feat_ref[...], pt_ref[...])[0:1]
    prior = dot(half_silu(0.5 * pre).astype(BF16), pout_ref[...])
    terms = pair_terms([theta], e_refs, weights, scratch)
    put_stripes(own_ref, terms - count * prior)


def sum_body(size, order, *rest):
    own_ref, out_ref = rest[-2:]
    away = dict(zip(order, rest))
    for k in range(size):
        total = own_ref[k]
        for by in range(1, size):
            total = total + away[by][source(k, by, size)].astype(F32)
        out_ref[k] = total.astype(out_ref.dtype)


def join_body(size, *refs):
    terms, out_ref = refs[:-1], refs[-1]
    for k in range(size):
        total = terms[0][k].astype(F32)
        for term in terms[1:]:
            total = total + term[k].astype(F32)
        out_ref[k] = total


def write_body(size, nrep, reps, mix_ref, noise_ref, *refs):
    n = len(reps)
    totals, parts = refs[:n], refs[n : 2 * n]
    updated_ref, score_ref, updated_hold, score_hold, sems = refs[-5:]
    z, r = lax.axis_index("obs"), lax.axis_index("rep")
    reach = noise_ref.shape[-1] // 128
    delta = jnp.tile(mix_ref[0:1, :], (1, reach))
    root = jnp.tile(mix_ref[1:2, :], (1, reach))
    copies = []
    for i, away in enumerate(reps):
        rep = source(r, away, nrep)
        for k in range(size):
            block = source(z, k, size)
            total = totals[i][k]
            score_hold[i, k] = total
            updated_hold[i, k] = parts[i][k] + delta * total + root * noise_ref[block, rep]
            for which, (held, out) in enumerate(
                ((score_hold, score_ref), (updated_hold, updated_ref))
            ):
                copies.append(
                    pltpu.make_async_copy(held.at[i, k], out.at[block, rep], sems.at[i, k, which])
                )
                copies[-1].start()
    wait_for(copies)


def on_device(
    particles,
    obs_embed,
    step_index,
    noise,
    w_query,
    w_key,
    w_value,
    w_time,
    w_score,
    prior_in,
    prior_time,
    prior_out,
):
    size, nrep, nhid = lax.axis_size("obs"), lax.axis_size("rep"), lax.axis_size("hid")
    home = particles[0]
    block_rows, width = home.shape
    stripe = block_rows // size
    sub = stripe // nrep
    rows = padded((size - 1) * sub)
    heads = w_key.shape[1] // DH
    emb = obs_embed.shape[1]
    count = obs_embed.shape[0] * size * nrep - 1
    shifts = range(1, size)

    def shape(*dims, dtype=F32):
        return jax.ShapeDtypeStruct(dims, dtype)

    def scratch(blocks, rows=rows):
        return [
            pltpu.VMEM((blocks * heads * rows, emb), BF16),
            pltpu.VMEM((blocks * heads * rows, emb), F32),
            pltpu.VMEM((blocks * rows, heads * DH), F32),
        ]

    hbm = pl.BlockSpec(memory_space=pltpu.HBM)
    far_first = [*range(size // 2, size), *range(1, size // 2)]
    seen = [passed_along(obs_embed, "rep", by) for by in range(1, nrep)]
    level = passed_along(step_index, "rep", 1).reshape(1, 1)
    time_weight = in_hbm(w_time.T)
    theta, mine, time_weight, *sends = call(
        functools.partial(prep_body, size),
        "prep",
        [
            shape(rows + sub, width, dtype=BF16),
            shape(sub, width),
            shape(*time_weight.shape, dtype=BF16),
        ]
        + [shape(rows + sub, width, dtype=BF16) for _ in shifts],
        [hbm] * 2,
        [
            pltpu.VMEM((size, sub, width), F32),
            pltpu.VMEM((rows, width), F32),
            pltpu.SemaphoreType.DMA((size + 1,)),
        ],
        PREP_FLOPS,
    )(in_hbm(home.reshape(size, nrep, sub, width)), time_weight)
    got = [passed_along(send, "obs", by) for by, send in zip(shifts, sends)]

    pair_flops = 4 * rows * heads * obs_embed.shape[0] * nrep * emb
    feats = w_time.shape[0]
    seen = [obs_embed, *seen]
    weights = [w_query, w_key, w_value, w_score]
    terms_shape = shape(size - 1, sub, width)
    home_terms, bias, mix, feat = call(
        functools.partial(home_body, size, nrep, heads, feats),
        "home_block",
        [terms_shape, shape(heads, 128), shape(2, 128), shape(16, feats, dtype=BF16)],
        [spec()] * (3 + nrep + len(weights)),
        scratch(1),
        pair_flops,
        16,
    )(level, time_weight, theta, *seen, *weights)
    weights = [*seen, *weights, bias]
    mid_terms = call(
        mid_body,
        "mid_block",
        terms_shape,
        [spec()] * (1 + len(weights)),
        scratch(1),
        pair_flops,
        16,
    )(got[0], *weights)
    *leave, token = call(
        functools.partial(far_body, size, nrep),
        "far_blocks",
        [shape(size, sub, width, dtype=BF16) for _ in shifts] + [shape(8, 128)],
        [spec()] * (size + len(weights)),
        scratch(size - 2),
        pair_flops * (size - 2),
        24,
    )(home_terms, mid_terms, *got[1:], *weights)
    moved = {by: passed_along(leave[by - 1], "obs", by) for by in far_first}
    own, part = call(
        functools.partial(own_body, size, nrep, float(count)),
        "own_rows",
        [shape(size, sub, width), shape(size, sub, width)],
        [spec()] * (3 + size - 1 + len(weights) + 4),
        scratch(1, size * sub) + [pltpu.VMEM((size * sub, width), F32)],
        pair_flops,
        20,
    )(token, theta, mine, *got, *weights, feat, prior_time, prior_in, prior_out)
    two = nhid == 2
    summed = call(
        functools.partial(sum_body, size, far_first),
        "sum_obs",
        shape(size, sub, width, dtype=BF16 if two else F32),
        [spec()] * size,
    )(*[moved[by] for by in far_first], own)
    if two:
        partial_sums = [summed, passed_along(summed, "hid", 1)]
    else:
        partial_sums = [lax.psum(summed, "hid")]
    joined = call(
        functools.partial(join_body, size),
        "join",
        shape(size, sub, width),
        [spec()] * len(partial_sums),
    )(*partial_sums)
    joined = [joined] + [passed_along(joined, "rep", by) for by in range(1, nrep)]
    parts = [part] + [passed_along(part, "rep", by) for by in range(1, nrep)]
    whole = shape(size, nrep, sub, width)
    noise_rows = noise.reshape(size, nrep, sub, width)
    outputs = ()
    for reps in ((0,), tuple(range(1, nrep))):
        n = len(reps)
        operands = [mix, noise_rows, *[joined[i] for i in reps], *[parts[i] for i in reps]]
        outputs = call(
            functools.partial(write_body, size, nrep, reps),
            "write_%d" % reps[0],
            [whole, whole],
            [spec()] * len(operands) + [hbm] * len(outputs),
            [pltpu.VMEM((n, size, sub, width), F32)] * 2
            + [pltpu.SemaphoreType.DMA((n, size, 2))],
            1 << 30,
            out_spec=hbm,
            aliases={len(operands) + i: i for i in range(len(outputs))},
        )(*operands, *outputs)
    updated, score = outputs
    return (updated.reshape(noise.shape), score.reshape(noise.shape))


def solution(mesh):
    in_specs = (
        P(("groups", "obs"), None, None),
        P(("groups", "obs", "rep"), None),
        P("groups"),
        P("groups", "obs", None),
        P(None, "hid"),
        P(None, "hid"),
        P(None, "hid"),
        P(None, "hid"),
        P("hid", None),
        P(None, "hid"),
        P(None, "hid"),
        P("hid", None),
    )
    out_specs = (P("groups", "obs", None), P("groups", "obs", None))
    return jax.shard_map(
        on_device, mesh=mesh, in_specs=in_specs, out_specs=out_specs, check_vma=False
    )
```

```python
import functools
import math

import jax
import jax.numpy as jnp
from jax import lax
from jax.experimental import pallas as pl
from jax.experimental.pallas import tpu as pltpu
from jax.sharding import PartitionSpec as P

DH = 128
STEPS = 64

SIG_LO = 0.05
SIG_HI = 1.0

F32 = jnp.float32
BF16 = jnp.bfloat16
NT = (((1,), (1,)), ((), ()))
TILE = 512
PREP_FLOPS = 4 << 30


def partner(index, by, size):
    if size & (size - 1) == 0:
        return index ^ by
    return (index + by) % size


def source(index, by, size):
    return partner(index, by if size & (size - 1) == 0 else size - by, size)


def passed_along(shard, axis, by):
    size = lax.axis_size(axis)
    return lax.ppermute(shard, axis, [(i, partner(i, by, size)) for i in range(size)])


def plan(level, feature_count):
    growth = math.log(SIG_HI / SIG_LO) / (STEPS - 1)
    sigma_now = SIG_LO * jnp.exp(growth * level)
    sigma_prev = SIG_LO * jnp.exp(growth * (level - 1.0))
    delta = sigma_now * sigma_now - sigma_prev * sigma_prev
    halves = feature_count // 2
    lane = lax.broadcasted_iota(jnp.int32, (1, halves), 1).astype(F32)
    angles = 10.0 * jnp.log(sigma_now[:, :1]) * jnp.exp(-math.log(1000.0) / halves * lane)
    features = jnp.concatenate([jnp.sin(angles), jnp.cos(angles)], 1).astype(BF16)
    return (features, delta)


def dot(a, b):
    return jnp.dot(a, b, preferred_element_type=F32)


def halves_of(x):
    high = x.astype(BF16)
    return high, (x - high.astype(F32)).astype(BF16)


def split_dot(x, weight):
    rows = x.shape[0]
    both = dot(jnp.concatenate(halves_of(x), 0), weight)
    return both[:rows] + both[rows:]


def half_silu(y):
    return y + y * jnp.tanh(y)


def put_stripes(target, values):
    count, sub = target.shape[:2]
    for s in range(count):
        target[s] = values[s * sub : (s + 1) * sub]


def others(ref, terms_ref):
    return ref[: padded(terms_ref.shape[0] * terms_ref.shape[1]), :]


def spec():
    return pl.BlockSpec(memory_space=pltpu.VMEM)


def in_hbm(x):
    return pltpu.with_memory_space_constraint(x, pltpu.HBM)


def call(body, name, out_shape, in_specs, scratch=(), flops=0, limit=4, out_spec=None, aliases={}):
    return pl.pallas_call(
        body,
        name=name,
        out_shape=out_shape,
        in_specs=in_specs,
        out_specs=jax.tree.map(lambda _: out_spec or spec(), out_shape),
        scratch_shapes=list(scratch),
        input_output_aliases=aliases,
        cost_estimate=pl.CostEstimate(flops=flops, bytes_accessed=flops // 1000, transcendentals=0),
        compiler_params=pltpu.CompilerParams(vmem_limit_bytes=limit << 20),
    )


def copies_of(sources, targets, sems):
    return [
        pltpu.make_async_copy(source, target, sems.at[i])
        for i, (source, target) in enumerate(zip(sources, targets))
    ]


def wait_for(copies):
    for copy in copies:
        copy.wait()


def padded(rows):
    return -(-rows // 16) * 16


def prep_body(size, home_ref, wt_hbm, theta_ref, mine_ref, wt_ref, *refs):
    sends, (held, stage, sems) = refs[: size - 1], refs[size - 1 :]
    z, r = lax.axis_index("obs"), lax.axis_index("rep")
    sub = held.shape[1]
    rows = stage.shape[0]
    copies = copies_of([home_ref.at[s, r] for s in range(size)], [held.at[s] for s in range(size)], sems)
    last = pltpu.make_async_copy(wt_hbm, wt_ref, sems.at[size])
    for copy in copies:
        copy.start()
    last.start()
    stage[...] = jnp.zeros_like(stage)
    wait_for(copies)
    for by, target_ref in enumerate((theta_ref, *sends)):
        target = partner(z, by, size)
        for k in range(1, size):
            stage[(k - 1) * sub : k * sub, :] = held[partner(target, k, size)]
        target_ref[:rows, :] = stage[...].astype(BF16)
        target_ref[rows:, :] = held[target].astype(BF16)
    mine_ref[...] = held[z]
    last.wait()


def pair_terms(theta, e_refs, weight_refs, scratch):
    wq_ref, wk_ref, wv_ref, ws_ref, bias_ref = weight_refs
    qk_ref, total_ref, pool_ref = scratch
    scale = 0.5 / math.sqrt(DH)
    blocks = len(theta)
    rows = theta[0].shape[0]
    heads = wk_ref.shape[1] // DH
    every = theta[0] if blocks == 1 else jnp.concatenate(theta, 0)
    queries = dot(every, wq_ref[...]).astype(BF16)
    for h in range(heads):
        cols = slice(h * DH, (h + 1) * DH)
        turned = lax.dot_general(queries[:, cols], wk_ref[:, cols], NT, preferred_element_type=F32)
        turned = (turned * scale).astype(BF16)
        for b in range(blocks):
            at = (b * heads + h) * rows
            qk_ref[at : at + rows, :] = turned[b * rows : (b + 1) * rows]

    def weights(scores):
        parts = []
        for h in range(heads):
            bias = jnp.tile(bias_ref[h : h + 1, :], (1, scores.shape[1] // 128))
            parts.append(half_silu(scores[h * rows : (h + 1) * rows] + bias).astype(BF16))
        return jnp.concatenate(parts, 0)

    fresh = True
    for e_ref in e_refs:
        tile = math.gcd(TILE, e_ref.shape[0])
        for j in range(e_ref.shape[0] // tile):
            seen = e_ref[j * tile : (j + 1) * tile, :]
            for b in range(blocks):
                span = slice(b * heads * rows, (b + 1) * heads * rows)
                scores = lax.dot_general(qk_ref[span, :], seen, NT, preferred_element_type=F32)
                term = dot(weights(scores), seen)
                total_ref[span, :] = term if fresh else total_ref[span, :] + term
            fresh = False
    for h in range(heads):
        cols = slice(h * DH, (h + 1) * DH)
        for b in range(blocks):
            at = (b * heads + h) * rows
            pool_ref[b * rows : (b + 1) * rows, cols] = split_dot(
                total_ref[at : at + rows, :], wv_ref[:, cols]
            )
    return split_dot(pool_ref[...], ws_ref[...])


def home_body(size, nrep, heads, feats, level_ref, wt_ref, theta_ref, *refs):
    e_refs, refs = refs[:nrep], refs[nrep:]
    weights, (terms_ref, bias_ref, mix_ref, feat_ref), scratch = refs[:4], refs[4:8], refs[8:]
    level = jnp.broadcast_to(level_ref[...].astype(F32), (1, 128))
    features, delta = plan(level, feats)
    mix_ref[0:1, :] = delta
    mix_ref[1:2, :] = jnp.sqrt(delta)
    feat = jnp.broadcast_to(features, (16, feats))
    feat_ref[...] = feat
    head_bias = lax.dot_general(wt_ref[...], feat, NT, preferred_element_type=F32) * 0.5
    bias_ref[...] = jnp.broadcast_to(head_bias[:, 0:1], (heads, 128))
    theta = [others(theta_ref, terms_ref)]
    put_stripes(terms_ref, pair_terms(theta, e_refs, (*weights, bias_ref), scratch))


def mid_body(got_ref, *refs):
    e_refs, weights, (terms_ref, *scratch) = refs[:-9], refs[-9:-4], refs[-4:]
    put_stripes(terms_ref, pair_terms([others(got_ref, terms_ref)], e_refs, weights, scratch))


def far_body(size, nrep, *refs):
    home_ref, mid_ref = refs[:2]
    got, rest = refs[size - 1 : 1 : -1], refs[size:]
    e_refs, weights, rest = rest[:nrep], rest[nrep : nrep + 5], rest[nrep + 5 :]
    sends, token_ref, scratch = rest[: size - 1], rest[size - 1], rest[size:]
    sub = home_ref.shape[1]
    terms = pair_terms([others(ref, home_ref) for ref in got], e_refs, weights, scratch)
    rows = terms.shape[0] // len(got)
    for k, send in enumerate(sends):
        for b in range(size):
            if b < 2:
                send[b] = (home_ref, mid_ref)[b][k].astype(BF16)
            else:
                at = (b - 2) * rows + k * sub
                send[b] = terms[at : at + sub].astype(BF16)
    token_ref[...] = terms[:8, :128]


def own_body(size, nrep, count, token_ref, theta_ref, mine_ref, *refs):
    got, refs = refs[: size - 1], refs[size - 1 :]
    e_refs, weights, refs = refs[:nrep], refs[nrep : nrep + 5], refs[nrep + 5 :]
    feat_ref, pt_ref, pin_ref, pout_ref, own_ref, part_ref, *scratch, stage = refs
    sub = own_ref.shape[1]
    rows = padded((size - 1) * sub)
    part_ref[0] = mine_ref[...]
    for b, ref in enumerate((theta_ref, *got)):
        owned = ref[rows:, :].astype(F32)
        stage[b * sub : (b + 1) * sub, :] = owned
        if b:
            part_ref[b] = owned
    theta = stage[...].astype(BF16)
    pre = dot(theta, pin_ref[...]) + dot(feat_ref[...], pt_ref[...])[0:1]
    prior = dot(half_silu(0.5 * pre).astype(BF16), pout_ref[...])
    terms = pair_terms([theta], e_refs, weights, scratch)
    put_stripes(own_ref, terms - count * prior)


def sum_body(size, order, *rest):
    own_ref, out_ref = rest[-2:]
    away = dict(zip(order, rest))
    for k in range(size):
        total = own_ref[k]
        for by in range(1, size):
            total = total + away[by][source(k, by, size)].astype(F32)
        out_ref[k] = total.astype(out_ref.dtype)


def join_body(size, *refs):
    terms, out_ref = refs[:-1], refs[-1]
    for k in range(size):
        total = terms[0][k].astype(F32)
        for term in terms[1:]:
            total = total + term[k].astype(F32)
        out_ref[k] = total


def write_body(size, nrep, reps, mix_ref, noise_ref, *refs):
    n = len(reps)
    totals, parts = refs[:n], refs[n : 2 * n]
    updated_ref, score_ref, updated_hold, score_hold, sems = refs[-5:]
    z, r = lax.axis_index("obs"), lax.axis_index("rep")
    reach = noise_ref.shape[-1] // 128
    delta = jnp.tile(mix_ref[0:1, :], (1, reach))
    root = jnp.tile(mix_ref[1:2, :], (1, reach))
    copies = []
    for i, away in enumerate(reps):
        rep = source(r, away, nrep)
        for k in range(size):
            block = source(z, k, size)
            total = totals[i][k]
            score_hold[i, k] = total
            updated_hold[i, k] = parts[i][k] + delta * total + root * noise_ref[block, rep]
            for which, (held, out) in enumerate(
                ((score_hold, score_ref), (updated_hold, updated_ref))
            ):
                copies.append(
                    pltpu.make_async_copy(held.at[i, k], out.at[block, rep], sems.at[i, k, which])
                )
                copies[-1].start()
    wait_for(copies)


def on_device(
    particles,
    obs_embed,
    step_index,
    noise,
    w_query,
    w_key,
    w_value,
    w_time,
    w_score,
    prior_in,
    prior_time,
    prior_out,
):
    size, nrep, nhid = lax.axis_size("obs"), lax.axis_size("rep"), lax.axis_size("hid")
    home = particles[0]
    block_rows, width = home.shape
    stripe = block_rows // size
    sub = stripe // nrep
    rows = padded((size - 1) * sub)
    heads = w_key.shape[1] // DH
    emb = obs_embed.shape[1]
    count = obs_embed.shape[0] * size * nrep - 1
    shifts = range(1, size)

    def shape(*dims, dtype=F32):
        return jax.ShapeDtypeStruct(dims, dtype)

    def scratch(blocks, rows=rows):
        return [
            pltpu.VMEM((blocks * heads * rows, emb), BF16),
            pltpu.VMEM((blocks * heads * rows, emb), F32),
            pltpu.VMEM((blocks * rows, heads * DH), F32),
        ]

    hbm = pl.BlockSpec(memory_space=pltpu.HBM)
    far_first = range(size - 1, 0, -1)
    seen = [passed_along(obs_embed, "rep", by) for by in range(1, nrep)]
    level = passed_along(step_index, "rep", 1).reshape(1, 1)
    time_weight = in_hbm(w_time.T)
    theta, mine, time_weight, *sends = call(
        functools.partial(prep_body, size),
        "prep",
        [
            shape(rows + sub, width, dtype=BF16),
            shape(sub, width),
            shape(*time_weight.shape, dtype=BF16),
        ]
        + [shape(rows + sub, width, dtype=BF16) for _ in shifts],
        [hbm] * 2,
        [
            pltpu.VMEM((size, sub, width), F32),
            pltpu.VMEM((rows, width), F32),
            pltpu.SemaphoreType.DMA((size + 1,)),
        ],
        PREP_FLOPS,
    )(in_hbm(home.reshape(size, nrep, sub, width)), time_weight)
    got = [passed_along(send, "obs", by) for by, send in zip(shifts, sends)]

    pair_flops = 4 * rows * heads * obs_embed.shape[0] * nrep * emb
    feats = w_time.shape[0]
    seen = [obs_embed, *seen]
    weights = [w_query, w_key, w_value, w_score]
    terms_shape = shape(size - 1, sub, width)
    home_terms, bias, mix, feat = call(
        functools.partial(home_body, size, nrep, heads, feats),
        "home_block",
        [terms_shape, shape(heads, 128), shape(2, 128), shape(16, feats, dtype=BF16)],
        [spec()] * (3 + nrep + len(weights)),
        scratch(1),
        pair_flops,
        16,
    )(level, time_weight, theta, *seen, *weights)
    weights = [*seen, *weights, bias]
    mid_terms = call(
        mid_body,
        "mid_block",
        terms_shape,
        [spec()] * (1 + len(weights)),
        scratch(1),
        pair_flops,
        16,
    )(got[0], *weights)
    *leave, token = call(
        functools.partial(far_body, size, nrep),
        "far_blocks",
        [shape(size, sub, width, dtype=BF16) for _ in shifts] + [shape(8, 128)],
        [spec()] * (size + len(weights)),
        scratch(size - 2),
        pair_flops * (size - 2),
        24,
    )(home_terms, mid_terms, *got[:0:-1], *weights)
    moved = {by: passed_along(leave[by - 1], "obs", by) for by in far_first}
    own, part = call(
        functools.partial(own_body, size, nrep, float(count)),
        "own_rows",
        [shape(size, sub, width), shape(size, sub, width)],
        [spec()] * (3 + size - 1 + len(weights) + 4),
        scratch(1, size * sub) + [pltpu.VMEM((size * sub, width), F32)],
        pair_flops,
        20,
    )(token, theta, mine, *got, *weights, feat, prior_time, prior_in, prior_out)
    two = nhid == 2
    summed = call(
        functools.partial(sum_body, size, far_first),
        "sum_obs",
        shape(size, sub, width, dtype=BF16 if two else F32),
        [spec()] * size,
    )(*[moved[by] for by in far_first], own)
    if two:
        partial_sums = [summed, passed_along(summed, "hid", 1)]
    else:
        partial_sums = [lax.psum(summed, "hid")]
    joined = call(
        functools.partial(join_body, size),
        "join",
        shape(size, sub, width),
        [spec()] * len(partial_sums),
    )(*partial_sums)
    joined = [joined] + [passed_along(joined, "rep", by) for by in range(1, nrep)]
    parts = [part] + [passed_along(part, "rep", by) for by in range(1, nrep)]
    whole = shape(size, nrep, sub, width)
    noise_rows = noise.reshape(size, nrep, sub, width)
    outputs = ()
    for reps in ((0,), tuple(range(1, nrep))):
        n = len(reps)
        operands = [mix, noise_rows, *[joined[i] for i in reps], *[parts[i] for i in reps]]
        outputs = call(
            functools.partial(write_body, size, nrep, reps),
            "write_%d" % reps[0],
            [whole, whole],
            [spec()] * len(operands) + [hbm] * len(outputs),
            [pltpu.VMEM((n, size, sub, width), F32)] * 2
            + [pltpu.SemaphoreType.DMA((n, size, 2))],
            1 << 30,
            out_spec=hbm,
            aliases={len(operands) + i: i for i in range(len(outputs))},
        )(*operands, *outputs)
    updated, score = outputs
    return (updated.reshape(noise.shape), score.reshape(noise.shape))


def solution(mesh):
    in_specs = (
        P(("groups", "obs"), None, None),
        P(("groups", "obs", "rep"), None),
        P("groups"),
        P("groups", "obs", None),
        P(None, "hid"),
        P(None, "hid"),
        P(None, "hid"),
        P(None, "hid"),
        P("hid", None),
        P(None, "hid"),
        P(None, "hid"),
        P("hid", None),
    )
    out_specs = (P("groups", "obs", None), P("groups", "obs", None))
    return jax.shard_map(
        on_device, mesh=mesh, in_specs=in_specs, out_specs=out_specs, check_vma=False
    )
```

```python
import functools
import math

import jax
import jax.numpy as jnp
from jax import lax
from jax.experimental import pallas as pl
from jax.experimental.pallas import tpu as pltpu
from jax.sharding import PartitionSpec as P

DH = 128
STEPS = 64

SIG_LO = 0.05
SIG_HI = 1.0

F32 = jnp.float32
BF16 = jnp.bfloat16
NT = (((1,), (1,)), ((), ()))
TILE = 512
PREP_FLOPS = 4 << 30


def partner(index, by, size):
    if size & (size - 1) == 0:
        return index ^ by
    return (index + by) % size


def source(index, by, size):
    return partner(index, by if size & (size - 1) == 0 else size - by, size)


def passed_along(shard, axis, by):
    size = lax.axis_size(axis)
    return lax.ppermute(shard, axis, [(i, partner(i, by, size)) for i in range(size)])


def plan(level, feature_count):
    growth = math.log(SIG_HI / SIG_LO) / (STEPS - 1)
    sigma_now = SIG_LO * jnp.exp(growth * level)
    sigma_prev = SIG_LO * jnp.exp(growth * (level - 1.0))
    delta = sigma_now * sigma_now - sigma_prev * sigma_prev
    halves = feature_count // 2
    lane = lax.broadcasted_iota(jnp.int32, (1, halves), 1).astype(F32)
    angles = 10.0 * jnp.log(sigma_now[:, :1]) * jnp.exp(-math.log(1000.0) / halves * lane)
    features = jnp.concatenate([jnp.sin(angles), jnp.cos(angles)], 1).astype(BF16)
    return (features, delta)


def dot(a, b):
    return jnp.dot(a, b, preferred_element_type=F32)


def halves_of(x):
    high = x.astype(BF16)
    return high, (x - high.astype(F32)).astype(BF16)


def split_dot(x, weight):
    rows = x.shape[0]
    both = dot(jnp.concatenate(halves_of(x), 0), weight)
    return both[:rows] + both[rows:]


def half_silu(y):
    return y + y * jnp.tanh(y)


def put_stripes(target, values):
    count, sub = target.shape[:2]
    for s in range(count):
        target[s] = values[s * sub : (s + 1) * sub]


def others(ref, terms_ref):
    return ref[: padded(terms_ref.shape[0] * terms_ref.shape[1]), :]


def spec():
    return pl.BlockSpec(memory_space=pltpu.VMEM)


def in_hbm(x):
    return pltpu.with_memory_space_constraint(x, pltpu.HBM)


def call(body, name, out_shape, in_specs, scratch=(), flops=0, limit=4, out_spec=None, aliases={}):
    return pl.pallas_call(
        body,
        name=name,
        out_shape=out_shape,
        in_specs=in_specs,
        out_specs=jax.tree.map(lambda _: out_spec or spec(), out_shape),
        scratch_shapes=list(scratch),
        input_output_aliases=aliases,
        cost_estimate=pl.CostEstimate(flops=flops, bytes_accessed=flops // 1000, transcendentals=0),
        compiler_params=pltpu.CompilerParams(vmem_limit_bytes=limit << 20),
    )


def copies_of(sources, targets, sems):
    return [
        pltpu.make_async_copy(source, target, sems.at[i])
        for i, (source, target) in enumerate(zip(sources, targets))
    ]


def wait_for(copies):
    for copy in copies:
        copy.wait()


def padded(rows):
    return -(-rows // 16) * 16


def prep_body(size, home_ref, wt_hbm, theta_ref, mine_ref, wt_ref, *refs):
    sends, (held, stage, sems) = refs[: size - 1], refs[size - 1 :]
    z, r = lax.axis_index("obs"), lax.axis_index("rep")
    sub = held.shape[1]
    rows = stage.shape[0]
    copies = copies_of([home_ref.at[s, r] for s in range(size)], [held.at[s] for s in range(size)], sems)
    last = pltpu.make_async_copy(wt_hbm, wt_ref, sems.at[size])
    for copy in copies:
        copy.start()
    last.start()
    stage[...] = jnp.zeros_like(stage)
    wait_for(copies)
    for by, target_ref in enumerate((theta_ref, *sends)):
        target = partner(z, by, size)
        for k in range(1, size):
            stage[(k - 1) * sub : k * sub, :] = held[partner(target, k, size)]
        target_ref[:rows, :] = stage[...].astype(BF16)
        target_ref[rows:, :] = held[target].astype(BF16)
    mine_ref[...] = held[z]
    last.wait()


def pair_terms(theta, e_refs, weight_refs, scratch):
    wq_ref, wk_ref, wv_ref, ws_ref, bias_ref = weight_refs
    qk_ref, total_ref, pool_ref = scratch
    scale = 0.5 / math.sqrt(DH)
    blocks = len(theta)
    rows = theta[0].shape[0]
    heads = wk_ref.shape[1] // DH
    every = theta[0] if blocks == 1 else jnp.concatenate(theta, 0)
    queries = dot(every, wq_ref[...]).astype(BF16)
    for h in range(heads):
        cols = slice(h * DH, (h + 1) * DH)
        turned = lax.dot_general(queries[:, cols], wk_ref[:, cols], NT, preferred_element_type=F32)
        turned = (turned * scale).astype(BF16)
        for b in range(blocks):
            at = (b * heads + h) * rows
            qk_ref[at : at + rows, :] = turned[b * rows : (b + 1) * rows]

    def weights(scores):
        parts = []
        for h in range(heads):
            bias = jnp.tile(bias_ref[h : h + 1, :], (1, scores.shape[1] // 128))
            parts.append(half_silu(scores[h * rows : (h + 1) * rows] + bias).astype(BF16))
        return jnp.concatenate(parts, 0)

    fresh = True
    for e_ref in e_refs:
        tile = math.gcd(TILE, e_ref.shape[0])
        for j in range(e_ref.shape[0] // tile):
            seen = e_ref[j * tile : (j + 1) * tile, :]
            for b in range(blocks):
                span = slice(b * heads * rows, (b + 1) * heads * rows)
                scores = lax.dot_general(qk_ref[span, :], seen, NT, preferred_element_type=F32)
                term = dot(weights(scores), seen)
                total_ref[span, :] = term if fresh else total_ref[span, :] + term
            fresh = False
    for h in range(heads):
        cols = slice(h * DH, (h + 1) * DH)
        for b in range(blocks):
            at = (b * heads + h) * rows
            pool_ref[b * rows : (b + 1) * rows, cols] = split_dot(
                total_ref[at : at + rows, :], wv_ref[:, cols]
            )
    return split_dot(pool_ref[...], ws_ref[...])


def home_body(size, nrep, heads, feats, level_ref, wt_ref, theta_ref, *refs):
    e_refs, refs = refs[:nrep], refs[nrep:]
    weights, (terms_ref, bias_ref, mix_ref, feat_ref), scratch = refs[:4], refs[4:8], refs[8:]
    level = jnp.broadcast_to(level_ref[...].astype(F32), (1, 128))
    features, delta = plan(level, feats)
    mix_ref[0:1, :] = delta
    mix_ref[1:2, :] = jnp.sqrt(delta)
    feat = jnp.broadcast_to(features, (16, feats))
    feat_ref[...] = feat
    head_bias = lax.dot_general(wt_ref[...], feat, NT, preferred_element_type=F32) * 0.5
    bias_ref[...] = jnp.broadcast_to(head_bias[:, 0:1], (heads, 128))
    theta = [others(theta_ref, terms_ref)]
    put_stripes(terms_ref, pair_terms(theta, e_refs, (*weights, bias_ref), scratch))


def mid_body(got_ref, *refs):
    e_refs, weights, (terms_ref, *scratch) = refs[:-9], refs[-9:-4], refs[-4:]
    put_stripes(terms_ref, pair_terms([others(got_ref, terms_ref)], e_refs, weights, scratch))


def far_body(size, nrep, *refs):
    home_ref, mid_ref = refs[:2]
    got, rest = refs[2:size], refs[size:]
    e_refs, weights, rest = rest[:nrep], rest[nrep : nrep + 5], rest[nrep + 5 :]
    sends, token_ref, scratch = rest[: size - 1], rest[size - 1], rest[size:]
    sub = home_ref.shape[1]
    terms = pair_terms([others(ref, home_ref) for ref in got], e_refs, weights, scratch)
    rows = terms.shape[0] // len(got)
    for k, send in enumerate(sends):
        for b in range(size):
            if b < 2:
                send[b] = (home_ref, mid_ref)[b][k].astype(BF16)
            else:
                at = (b - 2) * rows + k * sub
                send[b] = terms[at : at + sub].astype(BF16)
    token_ref[...] = terms[:8, :128]


def own_body(size, nrep, count, token_ref, theta_ref, mine_ref, *refs):
    got, refs = refs[: size - 1], refs[size - 1 :]
    e_refs, weights, refs = refs[:nrep], refs[nrep : nrep + 5], refs[nrep + 5 :]
    feat_ref, pt_ref, pin_ref, pout_ref, own_ref, part_ref, *scratch, stage = refs
    sub = own_ref.shape[1]
    rows = padded((size - 1) * sub)
    part_ref[0] = mine_ref[...]
    for b, ref in enumerate((theta_ref, *got)):
        owned = ref[rows:, :].astype(F32)
        stage[b * sub : (b + 1) * sub, :] = owned
        if b:
            part_ref[b] = owned
    theta = stage[...].astype(BF16)
    pre = dot(theta, pin_ref[...]) + dot(feat_ref[...], pt_ref[...])[0:1]
    prior = dot(half_silu(0.5 * pre).astype(BF16), pout_ref[...])
    terms = pair_terms([theta], e_refs, weights, scratch)
    put_stripes(own_ref, terms - count * prior)


def sum_body(size, order, *rest):
    own_ref, out_ref = rest[-2:]
    away = dict(zip(order, rest))
    for k in range(size):
        total = own_ref[k]
        for by in range(1, size):
            total = total + away[by][source(k, by, size)].astype(F32)
        out_ref[k] = total.astype(out_ref.dtype)


def join_body(size, *refs):
    terms, out_ref = refs[:-1], refs[-1]
    for k in range(size):
        total = terms[0][k].astype(F32)
        for term in terms[1:]:
            total = total + term[k].astype(F32)
        out_ref[k] = total


def write_body(size, nrep, reps, mix_ref, noise_ref, *refs):
    n = len(reps)
    totals, parts = refs[:n], refs[n : 2 * n]
    updated_ref, score_ref, updated_hold, score_hold, sems = refs[-5:]
    z, r = lax.axis_index("obs"), lax.axis_index("rep")
    reach = noise_ref.shape[-1] // 128
    delta = jnp.tile(mix_ref[0:1, :], (1, reach))
    root = jnp.tile(mix_ref[1:2, :], (1, reach))
    copies = []
    for i, away in enumerate(reps):
        rep = source(r, away, nrep)
        for k in range(size):
            block = source(z, k, size)
            total = totals[i][k]
            score_hold[i, k] = total
            updated_hold[i, k] = parts[i][k] + delta * total + root * noise_ref[block, rep]
            for which, (held, out) in enumerate(
                ((score_hold, score_ref), (updated_hold, updated_ref))
            ):
                copies.append(
                    pltpu.make_async_copy(held.at[i, k], out.at[block, rep], sems.at[i, k, which])
                )
                copies[-1].start()
    wait_for(copies)


def on_device(
    particles,
    obs_embed,
    step_index,
    noise,
    w_query,
    w_key,
    w_value,
    w_time,
    w_score,
    prior_in,
    prior_time,
    prior_out,
):
    size, nrep, nhid = lax.axis_size("obs"), lax.axis_size("rep"), lax.axis_size("hid")
    home = particles[0]
    block_rows, width = home.shape
    stripe = block_rows // size
    sub = stripe // nrep
    rows = padded((size - 1) * sub)
    heads = w_key.shape[1] // DH
    emb = obs_embed.shape[1]
    count = obs_embed.shape[0] * size * nrep - 1
    shifts = range(1, size)

    def shape(*dims, dtype=F32):
        return jax.ShapeDtypeStruct(dims, dtype)

    def scratch(blocks, rows=rows):
        return [
            pltpu.VMEM((blocks * heads * rows, emb), BF16),
            pltpu.VMEM((blocks * heads * rows, emb), F32),
            pltpu.VMEM((blocks * rows, heads * DH), F32),
        ]

    hbm = pl.BlockSpec(memory_space=pltpu.HBM)
    far_first = range(size - 1, 0, -1)
    seen = [passed_along(obs_embed, "rep", by) for by in range(1, nrep)]
    level = passed_along(step_index, "rep", 1).reshape(1, 1)
    time_weight = in_hbm(w_time.T)
    theta, mine, time_weight, *sends = call(
        functools.partial(prep_body, size),
        "prep",
        [
            shape(rows + sub, width, dtype=BF16),
            shape(sub, width),
            shape(*time_weight.shape, dtype=BF16),
        ]
        + [shape(rows + sub, width, dtype=BF16) for _ in shifts],
        [hbm] * 2,
        [
            pltpu.VMEM((size, sub, width), F32),
            pltpu.VMEM((rows, width), F32),
            pltpu.SemaphoreType.DMA((size + 1,)),
        ],
        PREP_FLOPS,
    )(in_hbm(home.reshape(size, nrep, sub, width)), time_weight)
    got = [passed_along(send, "obs", by) for by, send in zip(shifts, sends)]

    pair_flops = 4 * rows * heads * obs_embed.shape[0] * nrep * emb
    feats = w_time.shape[0]
    seen = [obs_embed, *seen]
    weights = [w_query, w_key, w_value, w_score]
    terms_shape = shape(size - 1, sub, width)
    home_terms, bias, mix, feat = call(
        functools.partial(home_body, size, nrep, heads, feats),
        "home_block",
        [terms_shape, shape(heads, 128), shape(2, 128), shape(16, feats, dtype=BF16)],
        [spec()] * (3 + nrep + len(weights)),
        scratch(1),
        pair_flops,
        16,
    )(level, time_weight, theta, *seen, *weights)
    weights = [*seen, *weights, bias]
    mid_terms = call(
        mid_body,
        "mid_block",
        terms_shape,
        [spec()] * (1 + len(weights)),
        scratch(1),
        pair_flops,
        16,
    )(got[0], *weights)
    *leave, token = call(
        functools.partial(far_body, size, nrep),
        "far_blocks",
        [shape(size, sub, width, dtype=BF16) for _ in shifts] + [shape(8, 128)],
        [spec()] * (size + len(weights)),
        scratch(size - 2),
        pair_flops * (size - 2),
        24,
    )(home_terms, mid_terms, *got[1:], *weights)
    moved = {by: passed_along(leave[by - 1], "obs", by) for by in far_first}
    own, part = call(
        functools.partial(own_body, size, nrep, float(count)),
        "own_rows",
        [shape(size, sub, width), shape(size, sub, width)],
        [spec()] * (3 + size - 1 + len(weights) + 4),
        scratch(1, size * sub) + [pltpu.VMEM((size * sub, width), F32)],
        pair_flops,
        20,
    )(token, theta, mine, *got, *weights, feat, prior_time, prior_in, prior_out)
    two = nhid == 2
    summed = call(
        functools.partial(sum_body, size, far_first),
        "sum_obs",
        shape(size, sub, width, dtype=BF16 if two else F32),
        [spec()] * size,
    )(*[moved[by] for by in far_first], own)
    if two:
        partial_sums = [summed, passed_along(summed, "hid", 1)]
    else:
        partial_sums = [lax.psum(summed, "hid")]
    joined = call(
        functools.partial(join_body, size),
        "join",
        shape(size, sub, width),
        [spec()] * len(partial_sums),
    )(*partial_sums)
    joined = [joined] + [passed_along(joined, "rep", by) for by in range(1, nrep)]
    parts = [part] + [passed_along(part, "rep", by) for by in range(1, nrep)]
    whole = shape(size, nrep, sub, width)
    noise_rows = noise.reshape(size, nrep, sub, width)
    outputs = ()
    for reps in ((0,), tuple(range(1, nrep))):
        n = len(reps)
        operands = [mix, noise_rows, *[joined[i] for i in reps], *[parts[i] for i in reps]]
        outputs = call(
            functools.partial(write_body, size, nrep, reps),
            "write_%d" % reps[0],
            [whole, whole],
            [spec()] * len(operands) + [hbm] * len(outputs),
            [pltpu.VMEM((n, size, sub, width), F32)] * 2
            + [pltpu.SemaphoreType.DMA((n, size, 2))],
            1 << 30,
            out_spec=hbm,
            aliases={len(operands) + i: i for i in range(len(outputs))},
        )(*operands, *outputs)
    updated, score = outputs
    return (updated.reshape(noise.shape), score.reshape(noise.shape))


def solution(mesh):
    in_specs = (
        P(("groups", "obs"), None, None),
        P(("groups", "obs", "rep"), None),
        P("groups"),
        P("groups", "obs", None),
        P(None, "hid"),
        P(None, "hid"),
        P(None, "hid"),
        P(None, "hid"),
        P("hid", None),
        P(None, "hid"),
        P(None, "hid"),
        P("hid", None),
    )
    out_specs = (P("groups", "obs", None), P("groups", "obs", None))
    return jax.shard_map(
        on_device, mesh=mesh, in_specs=in_specs, out_specs=out_specs, check_vma=False
    )
```

```python
import functools
import math

import jax
import jax.numpy as jnp
from jax import lax
from jax.experimental import pallas as pl
from jax.experimental.pallas import tpu as pltpu
from jax.sharding import PartitionSpec as P

DH = 128
STEPS = 64

SIG_LO = 0.05
SIG_HI = 1.0

F32 = jnp.float32
BF16 = jnp.bfloat16
NT = (((1,), (1,)), ((), ()))
TILE = 512
PREP_FLOPS = 4 << 30


def partner(index, by, size):
    if size & (size - 1) == 0:
        return index ^ by
    return (index + by) % size


def source(index, by, size):
    return partner(index, by if size & (size - 1) == 0 else size - by, size)


def passed_along(shard, axis, by):
    size = lax.axis_size(axis)
    return lax.ppermute(shard, axis, [(i, partner(i, by, size)) for i in range(size)])


def plan(level, feature_count):
    growth = math.log(SIG_HI / SIG_LO) / (STEPS - 1)
    sigma_now = SIG_LO * jnp.exp(growth * level)
    sigma_prev = SIG_LO * jnp.exp(growth * (level - 1.0))
    delta = sigma_now * sigma_now - sigma_prev * sigma_prev
    halves = feature_count // 2
    lane = lax.broadcasted_iota(jnp.int32, (1, halves), 1).astype(F32)
    log_sigma = math.log(SIG_LO) + growth * level[:, :1]
    angles = 10.0 * log_sigma * jnp.exp(-math.log(1000.0) / halves * lane)
    waves = jnp.sin(jnp.concatenate([angles, angles + 0.5 * math.pi], 0))
    features = jnp.concatenate([waves[0:1], waves[1:2]], 1).astype(BF16)
    return (features, delta)


def dot(a, b):
    return jnp.dot(a, b, preferred_element_type=F32)


def halves_of(x):
    high = x.astype(BF16)
    return high, (x - high.astype(F32)).astype(BF16)


def split_dot(x, weight):
    rows = x.shape[0]
    both = dot(jnp.concatenate(halves_of(x), 0), weight)
    return both[:rows] + both[rows:]


def half_silu(y):
    return y + y * jnp.tanh(y)


def put_stripes(target, values):
    count, sub = target.shape[:2]
    for s in range(count):
        target[s] = values[s * sub : (s + 1) * sub]


def others(ref, terms_ref):
    return ref[: padded(terms_ref.shape[0] * terms_ref.shape[1]), :]


def spec():
    return pl.BlockSpec(memory_space=pltpu.VMEM)


def in_hbm(x):
    return pltpu.with_memory_space_constraint(x, pltpu.HBM)


def call(body, name, out_shape, in_specs, scratch=(), flops=0, limit=4, out_spec=None, aliases={}):
    return pl.pallas_call(
        body,
        name=name,
        out_shape=out_shape,
        in_specs=in_specs,
        out_specs=jax.tree.map(lambda _: out_spec or spec(), out_shape),
        scratch_shapes=list(scratch),
        input_output_aliases=aliases,
        cost_estimate=pl.CostEstimate(flops=flops, bytes_accessed=flops // 1000, transcendentals=0),
        compiler_params=pltpu.CompilerParams(vmem_limit_bytes=limit << 20),
    )


def copies_of(sources, targets, sems):
    return [
        pltpu.make_async_copy(source, target, sems.at[i])
        for i, (source, target) in enumerate(zip(sources, targets))
    ]


def wait_for(copies):
    for copy in copies:
        copy.wait()


def padded(rows):
    return -(-rows // 16) * 16


def prep_body(size, home_ref, wt_hbm, theta_ref, mine_ref, wt_ref, *refs):
    sends, (held, stage, sems) = refs[: size - 1], refs[size - 1 :]
    z, r = lax.axis_index("obs"), lax.axis_index("rep")
    sub = held.shape[1]
    rows = stage.shape[0]
    copies = copies_of([home_ref.at[s, r] for s in range(size)], [held.at[s] for s in range(size)], sems)
    last = pltpu.make_async_copy(wt_hbm, wt_ref, sems.at[size])
    for copy in copies:
        copy.start()
    last.start()
    stage[...] = jnp.zeros_like(stage)
    wait_for(copies)
    for by, target_ref in enumerate((theta_ref, *sends)):
        target = partner(z, by, size)
        for k in range(1, size):
            stage[(k - 1) * sub : k * sub, :] = held[partner(target, k, size)]
        target_ref[:rows, :] = stage[...].astype(BF16)
        target_ref[rows:, :] = held[target].astype(BF16)
    mine_ref[...] = held[z]
    last.wait()


def pair_terms(theta, e_refs, weight_refs, scratch):
    wq_ref, wk_ref, wv_ref, ws_ref, bias_ref = weight_refs
    qk_ref, total_ref, pool_ref = scratch
    scale = 0.5 / math.sqrt(DH)
    blocks = len(theta)
    rows = theta[0].shape[0]
    heads = wk_ref.shape[1] // DH
    every = theta[0] if blocks == 1 else jnp.concatenate(theta, 0)
    queries = dot(every, wq_ref[...]).astype(BF16)
    for h in range(heads):
        cols = slice(h * DH, (h + 1) * DH)
        turned = lax.dot_general(queries[:, cols], wk_ref[:, cols], NT, preferred_element_type=F32)
        turned = (turned * scale).astype(BF16)
        for b in range(blocks):
            at = (b * heads + h) * rows
            qk_ref[at : at + rows, :] = turned[b * rows : (b + 1) * rows]

    def weights(scores):
        parts = []
        for h in range(heads):
            bias = jnp.tile(bias_ref[h : h + 1, :], (1, scores.shape[1] // 128))
            parts.append(half_silu(scores[h * rows : (h + 1) * rows] + bias).astype(BF16))
        return jnp.concatenate(parts, 0)

    fresh = True
    for e_ref in e_refs:
        tile = math.gcd(TILE, e_ref.shape[0])
        for j in range(e_ref.shape[0] // tile):
            seen = e_ref[j * tile : (j + 1) * tile, :]
            for b in range(blocks):
                span = slice(b * heads * rows, (b + 1) * heads * rows)
                scores = lax.dot_general(qk_ref[span, :], seen, NT, preferred_element_type=F32)
                term = dot(weights(scores), seen)
                total_ref[span, :] = term if fresh else total_ref[span, :] + term
            fresh = False
    for h in range(heads):
        cols = slice(h * DH, (h + 1) * DH)
        for b in range(blocks):
            at = (b * heads + h) * rows
            pool_ref[b * rows : (b + 1) * rows, cols] = split_dot(
                total_ref[at : at + rows, :], wv_ref[:, cols]
            )
    return split_dot(pool_ref[...], ws_ref[...])


def home_body(size, nrep, heads, feats, level_ref, wt_ref, theta_ref, *refs):
    e_refs, refs = refs[:nrep], refs[nrep:]
    weights, (terms_ref, bias_ref, mix_ref, feat_ref), scratch = refs[:4], refs[4:8], refs[8:]
    level = jnp.broadcast_to(level_ref[...].astype(F32), (1, 128))
    features, delta = plan(level, feats)
    mix_ref[0:1, :] = delta
    mix_ref[1:2, :] = jnp.sqrt(delta)
    feat = jnp.broadcast_to(features, (16, feats))
    feat_ref[...] = feat
    head_bias = lax.dot_general(wt_ref[...], feat, NT, preferred_element_type=F32) * 0.5
    bias_ref[...] = jnp.broadcast_to(head_bias[:, 0:1], (heads, 128))
    theta = [others(theta_ref, terms_ref)]
    put_stripes(terms_ref, pair_terms(theta, e_refs, (*weights, bias_ref), scratch))


def mid_body(got_ref, *refs):
    e_refs, weights, (terms_ref, *scratch) = refs[:-9], refs[-9:-4], refs[-4:]
    put_stripes(terms_ref, pair_terms([others(got_ref, terms_ref)], e_refs, weights, scratch))


def far_body(size, nrep, *refs):
    home_ref, mid_ref = refs[:2]
    got, rest = refs[2:size], refs[size:]
    e_refs, weights, rest = rest[:nrep], rest[nrep : nrep + 5], rest[nrep + 5 :]
    sends, token_ref, scratch = rest[: size - 1], rest[size - 1], rest[size:]
    sub = home_ref.shape[1]
    terms = pair_terms([others(ref, home_ref) for ref in got], e_refs, weights, scratch)
    rows = terms.shape[0] // len(got)
    for k, send in enumerate(sends):
        for b in range(size):
            if b < 2:
                send[b] = (home_ref, mid_ref)[b][k].astype(BF16)
            else:
                at = (b - 2) * rows + k * sub
                send[b] = terms[at : at + sub].astype(BF16)
    token_ref[...] = terms[:8, :128]


def own_body(size, nrep, count, token_ref, theta_ref, mine_ref, *refs):
    got, refs = refs[: size - 1], refs[size - 1 :]
    e_refs, weights, refs = refs[:nrep], refs[nrep : nrep + 5], refs[nrep + 5 :]
    feat_ref, pt_ref, pin_ref, pout_ref, own_ref, part_ref, *scratch, stage = refs
    sub = own_ref.shape[1]
    rows = padded((size - 1) * sub)
    part_ref[0] = mine_ref[...]
    for b, ref in enumerate((theta_ref, *got)):
        owned = ref[rows:, :].astype(F32)
        stage[b * sub : (b + 1) * sub, :] = owned
        if b:
            part_ref[b] = owned
    theta = stage[...].astype(BF16)
    pre = dot(theta, pin_ref[...]) + dot(feat_ref[...], pt_ref[...])[0:1]
    prior = dot(half_silu(0.5 * pre).astype(BF16), pout_ref[...])
    terms = pair_terms([theta], e_refs, weights, scratch)
    put_stripes(own_ref, terms - count * prior)


def sum_body(size, order, *rest):
    own_ref, out_ref = rest[-2:]
    away = dict(zip(order, rest))
    for k in range(size):
        total = own_ref[k]
        for by in range(1, size):
            total = total + away[by][source(k, by, size)].astype(F32)
        out_ref[k] = total.astype(out_ref.dtype)


def join_body(size, *refs):
    terms, out_ref = refs[:-1], refs[-1]
    for k in range(size):
        total = terms[0][k].astype(F32)
        for term in terms[1:]:
            total = total + term[k].astype(F32)
        out_ref[k] = total


def write_body(size, nrep, reps, mix_ref, noise_ref, *refs):
    n = len(reps)
    totals, parts = refs[:n], refs[n : 2 * n]
    updated_ref, score_ref, updated_hold, score_hold, sems = refs[-5:]
    z, r = lax.axis_index("obs"), lax.axis_index("rep")
    reach = noise_ref.shape[-1] // 128
    delta = jnp.tile(mix_ref[0:1, :], (1, reach))
    root = jnp.tile(mix_ref[1:2, :], (1, reach))
    copies = []
    for i, away in enumerate(reps):
        rep = source(r, away, nrep)
        for k in range(size):
            block = source(z, k, size)
            total = totals[i][k]
            score_hold[i, k] = total
            updated_hold[i, k] = parts[i][k] + delta * total + root * noise_ref[block, rep]
            for which, (held, out) in enumerate(
                ((score_hold, score_ref), (updated_hold, updated_ref))
            ):
                copies.append(
                    pltpu.make_async_copy(held.at[i, k], out.at[block, rep], sems.at[i, k, which])
                )
                copies[-1].start()
    wait_for(copies)


def on_device(
    particles,
    obs_embed,
    step_index,
    noise,
    w_query,
    w_key,
    w_value,
    w_time,
    w_score,
    prior_in,
    prior_time,
    prior_out,
):
    size, nrep, nhid = lax.axis_size("obs"), lax.axis_size("rep"), lax.axis_size("hid")
    home = particles[0]
    block_rows, width = home.shape
    stripe = block_rows // size
    sub = stripe // nrep
    rows = padded((size - 1) * sub)
    heads = w_key.shape[1] // DH
    emb = obs_embed.shape[1]
    count = obs_embed.shape[0] * size * nrep - 1
    shifts = range(1, size)

    def shape(*dims, dtype=F32):
        return jax.ShapeDtypeStruct(dims, dtype)

    def scratch(blocks, rows=rows):
        return [
            pltpu.VMEM((blocks * heads * rows, emb), BF16),
            pltpu.VMEM((blocks * heads * rows, emb), F32),
            pltpu.VMEM((blocks * rows, heads * DH), F32),
        ]

    hbm = pl.BlockSpec(memory_space=pltpu.HBM)
    far_first = [*range(size // 2, size), *range(1, size // 2)]
    seen = [passed_along(obs_embed, "rep", by) for by in range(1, nrep)]
    level = passed_along(step_index, "rep", 1).reshape(1, 1)
    time_weight = in_hbm(w_time.T)
    theta, mine, time_weight, *sends = call(
        functools.partial(prep_body, size),
        "prep",
        [
            shape(rows + sub, width, dtype=BF16),
            shape(sub, width),
            shape(*time_weight.shape, dtype=BF16),
        ]
        + [shape(rows + sub, width, dtype=BF16) for _ in shifts],
        [hbm] * 2,
        [
            pltpu.VMEM((size, sub, width), F32),
            pltpu.VMEM((rows, width), F32),
            pltpu.SemaphoreType.DMA((size + 1,)),
        ],
        PREP_FLOPS,
    )(in_hbm(home.reshape(size, nrep, sub, width)), time_weight)
    got = [passed_along(send, "obs", by) for by, send in zip(shifts, sends)]

    pair_flops = 4 * rows * heads * obs_embed.shape[0] * nrep * emb
    feats = w_time.shape[0]
    seen = [obs_embed, *seen]
    weights = [w_query, w_key, w_value, w_score]
    terms_shape = shape(size - 1, sub, width)
    home_terms, bias, mix, feat = call(
        functools.partial(home_body, size, nrep, heads, feats),
        "home_block",
        [terms_shape, shape(heads, 128), shape(2, 128), shape(16, feats, dtype=BF16)],
        [spec()] * (3 + nrep + len(weights)),
        scratch(1),
        pair_flops,
        16,
    )(level, time_weight, theta, *seen, *weights)
    weights = [*seen, *weights, bias]
    mid_terms = call(
        mid_body,
        "mid_block",
        terms_shape,
        [spec()] * (1 + len(weights)),
        scratch(1),
        pair_flops,
        16,
    )(got[0], *weights)
    *leave, token = call(
        functools.partial(far_body, size, nrep),
        "far_blocks",
        [shape(size, sub, width, dtype=BF16) for _ in shifts] + [shape(8, 128)],
        [spec()] * (size + len(weights)),
        scratch(size - 2),
        pair_flops * (size - 2),
        24,
    )(home_terms, mid_terms, *got[1:], *weights)
    moved = {by: passed_along(leave[by - 1], "obs", by) for by in far_first}
    own, part = call(
        functools.partial(own_body, size, nrep, float(count)),
        "own_rows",
        [shape(size, sub, width), shape(size, sub, width)],
        [spec()] * (3 + size - 1 + len(weights) + 4),
        scratch(1, size * sub) + [pltpu.VMEM((size * sub, width), F32)],
        pair_flops,
        20,
    )(token, theta, mine, *got, *weights, feat, prior_time, prior_in, prior_out)
    two = nhid == 2
    summed = call(
        functools.partial(sum_body, size, far_first),
        "sum_obs",
        shape(size, sub, width, dtype=BF16 if two else F32),
        [spec()] * size,
    )(*[moved[by] for by in far_first], own)
    if two:
        partial_sums = [summed, passed_along(summed, "hid", 1)]
    else:
        partial_sums = [lax.psum(summed, "hid")]
    joined = call(
        functools.partial(join_body, size),
        "join",
        shape(size, sub, width),
        [spec()] * len(partial_sums),
    )(*partial_sums)
    joined = [joined] + [passed_along(joined, "rep", by) for by in range(1, nrep)]
    parts = [part] + [passed_along(part, "rep", by) for by in range(1, nrep)]
    whole = shape(size, nrep, sub, width)
    noise_rows = noise.reshape(size, nrep, sub, width)
    outputs = ()
    for reps in ((0,), tuple(range(1, nrep))):
        n = len(reps)
        operands = [mix, noise_rows, *[joined[i] for i in reps], *[parts[i] for i in reps]]
        outputs = call(
            functools.partial(write_body, size, nrep, reps),
            "write_%d" % reps[0],
            [whole, whole],
            [spec()] * len(operands) + [hbm] * len(outputs),
            [pltpu.VMEM((n, size, sub, width), F32)] * 2
            + [pltpu.SemaphoreType.DMA((n, size, 2))],
            1 << 30,
            out_spec=hbm,
            aliases={len(operands) + i: i for i in range(len(outputs))},
        )(*operands, *outputs)
    updated, score = outputs
    return (updated.reshape(noise.shape), score.reshape(noise.shape))


def solution(mesh):
    in_specs = (
        P(("groups", "obs"), None, None),
        P(("groups", "obs", "rep"), None),
        P("groups"),
        P("groups", "obs", None),
        P(None, "hid"),
        P(None, "hid"),
        P(None, "hid"),
        P(None, "hid"),
        P("hid", None),
        P(None, "hid"),
        P(None, "hid"),
        P("hid", None),
    )
    out_specs = (P("groups", "obs", None), P("groups", "obs", None))
    return jax.shard_map(
        on_device, mesh=mesh, in_specs=in_specs, out_specs=out_specs, check_vma=False
    )
```

```python
import functools
import math

import jax
import jax.numpy as jnp
from jax import lax
from jax.experimental import pallas as pl
from jax.experimental.pallas import tpu as pltpu
from jax.sharding import PartitionSpec as P

DH = 128
STEPS = 64

SIG_LO = 0.05
SIG_HI = 1.0

F32 = jnp.float32
BF16 = jnp.bfloat16
NT = (((1,), (1,)), ((), ()))
TILE = 512
PREP_FLOPS = 4 << 30


def partner(index, by, size):
    if size & (size - 1) == 0:
        return index ^ by
    return (index + by) % size


def source(index, by, size):
    return partner(index, by if size & (size - 1) == 0 else size - by, size)


def passed_along(shard, axis, by):
    size = lax.axis_size(axis)
    return lax.ppermute(shard, axis, [(i, partner(i, by, size)) for i in range(size)])


def plan(level, feature_count):
    growth = math.log(SIG_HI / SIG_LO) / (STEPS - 1)
    sigma_now = SIG_LO * jnp.exp(growth * level)
    sigma_prev = SIG_LO * jnp.exp(growth * (level - 1.0))
    delta = sigma_now * sigma_now - sigma_prev * sigma_prev
    halves = feature_count // 2
    lane = lax.broadcasted_iota(jnp.int32, (1, halves), 1).astype(F32)
    log_sigma = math.log(SIG_LO) + growth * level[:, :1]
    angles = 10.0 * log_sigma * jnp.exp(-math.log(1000.0) / halves * lane)
    waves = jnp.sin(jnp.concatenate([angles, angles + 0.5 * math.pi], 0))
    features = jnp.concatenate([waves[0:1], waves[1:2]], 1).astype(BF16)
    return (features, delta)


def dot(a, b):
    return jnp.dot(a, b, preferred_element_type=F32)


def halves_of(x):
    high = x.astype(BF16)
    return high, (x - high.astype(F32)).astype(BF16)


def split_dot(x, weight):
    rows = x.shape[0]
    both = dot(jnp.concatenate(halves_of(x), 0), weight)
    return both[:rows] + both[rows:]


def half_silu(y):
    return y + y * jnp.tanh(y)


def put_stripes(target, values):
    count, sub = target.shape[:2]
    for s in range(count):
        target[s] = values[s * sub : (s + 1) * sub]


def others(ref, terms_ref):
    return ref[: padded(terms_ref.shape[0] * terms_ref.shape[1]), :]


def spec():
    return pl.BlockSpec(memory_space=pltpu.VMEM)


def in_hbm(x):
    return pltpu.with_memory_space_constraint(x, pltpu.HBM)


def call(body, name, out_shape, in_specs, scratch=(), flops=0, limit=4, out_spec=None, aliases={}):
    return pl.pallas_call(
        body,
        name=name,
        out_shape=out_shape,
        in_specs=in_specs,
        out_specs=jax.tree.map(lambda _: out_spec or spec(), out_shape),
        scratch_shapes=list(scratch),
        input_output_aliases=aliases,
        cost_estimate=pl.CostEstimate(flops=flops, bytes_accessed=flops // 1000, transcendentals=0),
        compiler_params=pltpu.CompilerParams(vmem_limit_bytes=limit << 20),
    )


def copies_of(sources, targets, sems):
    return [
        pltpu.make_async_copy(source, target, sems.at[i])
        for i, (source, target) in enumerate(zip(sources, targets))
    ]


def wait_for(copies):
    for copy in copies:
        copy.wait()


def padded(rows):
    return -(-rows // 16) * 16


def prep_body(size, home_ref, wt_hbm, theta_ref, mine_ref, wt_ref, *refs):
    sends, (held, stage, sems) = refs[: size - 1], refs[size - 1 :]
    z, r = lax.axis_index("obs"), lax.axis_index("rep")
    sub = held.shape[1]
    rows = stage.shape[0]
    copies = copies_of([home_ref.at[s, r] for s in range(size)], [held.at[s] for s in range(size)], sems)
    last = pltpu.make_async_copy(wt_hbm, wt_ref, sems.at[size])
    for copy in copies:
        copy.start()
    last.start()
    stage[...] = jnp.zeros_like(stage)
    wait_for(copies)
    for by, target_ref in enumerate((theta_ref, *sends)):
        target = partner(z, by, size)
        for k in range(1, size):
            stage[(k - 1) * sub : k * sub, :] = held[partner(target, k, size)]
        target_ref[:rows, :] = stage[...].astype(BF16)
        target_ref[rows:, :] = held[target].astype(BF16)
    mine_ref[...] = held[z]
    last.wait()


def pair_terms(theta, e_refs, weight_refs, scratch):
    wq_ref, wk_ref, wv_ref, ws_ref, bias_ref = weight_refs
    qk_ref, total_ref, pool_ref = scratch
    scale = 0.5 / math.sqrt(DH)
    blocks = len(theta)
    rows = theta[0].shape[0]
    heads = wk_ref.shape[1] // DH
    every = theta[0] if blocks == 1 else jnp.concatenate(theta, 0)
    queries = dot(every, wq_ref[...]).astype(BF16)
    for h in range(heads):
        cols = slice(h * DH, (h + 1) * DH)
        turned = lax.dot_general(queries[:, cols], wk_ref[:, cols], NT, preferred_element_type=F32)
        turned = (turned * scale).astype(BF16)
        for b in range(blocks):
            at = (b * heads + h) * rows
            qk_ref[at : at + rows, :] = turned[b * rows : (b + 1) * rows]

    def weights(scores):
        parts = []
        for h in range(heads):
            bias = jnp.tile(bias_ref[h : h + 1, :], (1, scores.shape[1] // 128))
            parts.append(half_silu(scores[h * rows : (h + 1) * rows] + bias).astype(BF16))
        return jnp.concatenate(parts, 0)

    fresh = True
    for e_ref in e_refs:
        tile = math.gcd(TILE, e_ref.shape[0])
        for j in range(e_ref.shape[0] // tile):
            seen = e_ref[j * tile : (j + 1) * tile, :]
            for b in range(blocks):
                span = slice(b * heads * rows, (b + 1) * heads * rows)
                scores = lax.dot_general(qk_ref[span, :], seen, NT, preferred_element_type=F32)
                term = dot(weights(scores), seen)
                total_ref[span, :] = term if fresh else total_ref[span, :] + term
            fresh = False
    for h in range(heads):
        cols = slice(h * DH, (h + 1) * DH)
        for b in range(blocks):
            at = (b * heads + h) * rows
            pool_ref[b * rows : (b + 1) * rows, cols] = split_dot(
                total_ref[at : at + rows, :], wv_ref[:, cols]
            )
    return split_dot(pool_ref[...], ws_ref[...])


def home_body(size, nrep, heads, feats, level_ref, wt_ref, theta_ref, *refs):
    e_refs, refs = refs[:nrep], refs[nrep:]
    weights, (terms_ref, bias_ref, mix_ref, feat_ref), scratch = refs[:4], refs[4:8], refs[8:]
    level = jnp.broadcast_to(level_ref[...].astype(F32), (1, 128))
    features, delta = plan(level, feats)
    mix_ref[0:1, :] = delta
    mix_ref[1:2, :] = jnp.sqrt(delta)
    feat = jnp.broadcast_to(features, (16, feats))
    feat_ref[...] = feat
    head_bias = lax.dot_general(wt_ref[...], feat, NT, preferred_element_type=F32) * 0.5
    bias_ref[...] = jnp.broadcast_to(head_bias[:, 0:1], (heads, 128))
    theta = [others(theta_ref, terms_ref)]
    put_stripes(terms_ref, pair_terms(theta, e_refs, (*weights, bias_ref), scratch))


def mid_body(got_ref, *refs):
    e_refs, weights, (terms_ref, *scratch) = refs[:-9], refs[-9:-4], refs[-4:]
    put_stripes(terms_ref, pair_terms([others(got_ref, terms_ref)], e_refs, weights, scratch))


def far_body(size, nrep, *refs):
    home_ref, mid_ref = refs[:2]
    got, rest = refs[2:size], refs[size:]
    e_refs, weights, rest = rest[:nrep], rest[nrep : nrep + 5], rest[nrep + 5 :]
    sends, token_ref, scratch = rest[: size - 1], rest[size - 1], rest[size:]
    sub = home_ref.shape[1]
    terms = pair_terms([others(ref, home_ref) for ref in got], e_refs, weights, scratch)
    rows = terms.shape[0] // len(got)
    for k, send in enumerate(sends):
        for b in range(size):
            if b < 2:
                send[b] = (home_ref, mid_ref)[b][k].astype(BF16)
            else:
                at = (b - 2) * rows + k * sub
                send[b] = terms[at : at + sub].astype(BF16)
    token_ref[...] = terms[:8, :128]


def own_body(size, nrep, count, token_ref, theta_ref, mine_ref, *refs):
    got, refs = refs[: size - 1], refs[size - 1 :]
    e_refs, weights, refs = refs[:nrep], refs[nrep : nrep + 5], refs[nrep + 5 :]
    feat_ref, pt_ref, pin_ref, pout_ref, own_ref, part_ref, *scratch, stage = refs
    sub = own_ref.shape[1]
    rows = padded((size - 1) * sub)
    part_ref[0] = mine_ref[...]
    for b, ref in enumerate((theta_ref, *got)):
        owned = ref[rows:, :].astype(F32)
        stage[b * sub : (b + 1) * sub, :] = owned
        if b:
            part_ref[b] = owned
    theta = stage[...].astype(BF16)
    pre = dot(theta, pin_ref[...]) + dot(feat_ref[...], pt_ref[...])[0:1]
    prior = dot(half_silu(0.5 * pre).astype(BF16), pout_ref[...])
    terms = pair_terms([theta], e_refs, weights, scratch)
    put_stripes(own_ref, terms - count * prior)


def sum_body(size, order, *rest):
    own_ref, out_ref = rest[-2:]
    away = dict(zip(order, rest))
    for k in range(size):
        total = own_ref[k]
        for by in range(1, size):
            total = total + away[by][source(k, by, size)].astype(F32)
        out_ref[k] = total.astype(out_ref.dtype)


def join_body(size, *refs):
    terms, out_ref = refs[:-1], refs[-1]
    for k in range(size):
        total = terms[0][k].astype(F32)
        for term in terms[1:]:
            total = total + term[k].astype(F32)
        out_ref[k] = total


def write_body(size, nrep, reps, mix_ref, noise_ref, *refs):
    n = len(reps)
    totals, parts = refs[:n], refs[n : 2 * n]
    updated_ref, score_ref, updated_hold, score_hold, sems = refs[-5:]
    z, r = lax.axis_index("obs"), lax.axis_index("rep")
    reach = noise_ref.shape[-1] // 128
    delta = jnp.tile(mix_ref[0:1, :], (1, reach))
    root = jnp.tile(mix_ref[1:2, :], (1, reach))
    copies = []
    for i, away in enumerate(reps):
        rep = source(r, away, nrep)
        for k in range(size):
            block = source(z, k, size)
            total = totals[i][k]
            score_hold[i, k] = total
            updated_hold[i, k] = parts[i][k] + delta * total + root * noise_ref[block, rep]
            for which, (held, out) in enumerate(
                ((score_hold, score_ref), (updated_hold, updated_ref))
            ):
                copies.append(
                    pltpu.make_async_copy(held.at[i, k], out.at[block, rep], sems.at[i, k, which])
                )
                copies[-1].start()
    wait_for(copies)


def on_device(
    particles,
    obs_embed,
    step_index,
    noise,
    w_query,
    w_key,
    w_value,
    w_time,
    w_score,
    prior_in,
    prior_time,
    prior_out,
):
    size, nrep, nhid = lax.axis_size("obs"), lax.axis_size("rep"), lax.axis_size("hid")
    home = particles[0]
    block_rows, width = home.shape
    stripe = block_rows // size
    sub = stripe // nrep
    rows = padded((size - 1) * sub)
    heads = w_key.shape[1] // DH
    emb = obs_embed.shape[1]
    count = obs_embed.shape[0] * size * nrep - 1
    shifts = range(1, size)

    def shape(*dims, dtype=F32):
        return jax.ShapeDtypeStruct(dims, dtype)

    def scratch(blocks, rows=rows):
        return [
            pltpu.VMEM((blocks * heads * rows, emb), BF16),
            pltpu.VMEM((blocks * heads * rows, emb), F32),
            pltpu.VMEM((blocks * rows, heads * DH), F32),
        ]

    hbm = pl.BlockSpec(memory_space=pltpu.HBM)
    far_first = [size // 2, *[by for by in shifts if by != size // 2]]
    seen = [passed_along(obs_embed, "rep", by) for by in range(1, nrep)]
    level = passed_along(step_index, "rep", 1).reshape(1, 1)
    time_weight = in_hbm(w_time.T)
    theta, mine, time_weight, *sends = call(
        functools.partial(prep_body, size),
        "prep",
        [
            shape(rows + sub, width, dtype=BF16),
            shape(sub, width),
            shape(*time_weight.shape, dtype=BF16),
        ]
        + [shape(rows + sub, width, dtype=BF16) for _ in shifts],
        [hbm] * 2,
        [
            pltpu.VMEM((size, sub, width), F32),
            pltpu.VMEM((rows, width), F32),
            pltpu.SemaphoreType.DMA((size + 1,)),
        ],
        PREP_FLOPS,
    )(in_hbm(home.reshape(size, nrep, sub, width)), time_weight)
    got = [passed_along(send, "obs", by) for by, send in zip(shifts, sends)]

    pair_flops = 4 * rows * heads * obs_embed.shape[0] * nrep * emb
    feats = w_time.shape[0]
    seen = [obs_embed, *seen]
    weights = [w_query, w_key, w_value, w_score]
    terms_shape = shape(size - 1, sub, width)
    home_terms, bias, mix, feat = call(
        functools.partial(home_body, size, nrep, heads, feats),
        "home_block",
        [terms_shape, shape(heads, 128), shape(2, 128), shape(16, feats, dtype=BF16)],
        [spec()] * (3 + nrep + len(weights)),
        scratch(1),
        pair_flops,
        16,
    )(level, time_weight, theta, *seen, *weights)
    weights = [*seen, *weights, bias]
    mid_terms = call(
        mid_body,
        "mid_block",
        terms_shape,
        [spec()] * (1 + len(weights)),
        scratch(1),
        pair_flops,
        16,
    )(got[0], *weights)
    *leave, token = call(
        functools.partial(far_body, size, nrep),
        "far_blocks",
        [shape(size, sub, width, dtype=BF16) for _ in shifts] + [shape(8, 128)],
        [spec()] * (size + len(weights)),
        scratch(size - 2),
        pair_flops * (size - 2),
        24,
    )(home_terms, mid_terms, *got[1:], *weights)
    moved = {by: passed_along(leave[by - 1], "obs", by) for by in far_first}
    own, part = call(
        functools.partial(own_body, size, nrep, float(count)),
        "own_rows",
        [shape(size, sub, width), shape(size, sub, width)],
        [spec()] * (3 + size - 1 + len(weights) + 4),
        scratch(1, size * sub) + [pltpu.VMEM((size * sub, width), F32)],
        pair_flops,
        20,
    )(token, theta, mine, *got, *weights, feat, prior_time, prior_in, prior_out)
    two = nhid == 2
    summed = call(
        functools.partial(sum_body, size, far_first),
        "sum_obs",
        shape(size, sub, width, dtype=BF16 if two else F32),
        [spec()] * size,
    )(*[moved[by] for by in far_first], own)
    if two:
        partial_sums = [summed, passed_along(summed, "hid", 1)]
    else:
        partial_sums = [lax.psum(summed, "hid")]
    joined = call(
        functools.partial(join_body, size),
        "join",
        shape(size, sub, width),
        [spec()] * len(partial_sums),
    )(*partial_sums)
    joined = [joined] + [passed_along(joined, "rep", by) for by in range(1, nrep)]
    parts = [part] + [passed_along(part, "rep", by) for by in range(1, nrep)]
    whole = shape(size, nrep, sub, width)
    noise_rows = noise.reshape(size, nrep, sub, width)
    outputs = ()
    for reps in ((0,), tuple(range(1, nrep))):
        n = len(reps)
        operands = [mix, noise_rows, *[joined[i] for i in reps], *[parts[i] for i in reps]]
        outputs = call(
            functools.partial(write_body, size, nrep, reps),
            "write_%d" % reps[0],
            [whole, whole],
            [spec()] * len(operands) + [hbm] * len(outputs),
            [pltpu.VMEM((n, size, sub, width), F32)] * 2
            + [pltpu.SemaphoreType.DMA((n, size, 2))],
            1 << 30,
            out_spec=hbm,
            aliases={len(operands) + i: i for i in range(len(outputs))},
        )(*operands, *outputs)
    updated, score = outputs
    return (updated.reshape(noise.shape), score.reshape(noise.shape))


def solution(mesh):
    in_specs = (
        P(("groups", "obs"), None, None),
        P(("groups", "obs", "rep"), None),
        P("groups"),
        P("groups", "obs", None),
        P(None, "hid"),
        P(None, "hid"),
        P(None, "hid"),
        P(None, "hid"),
        P("hid", None),
        P(None, "hid"),
        P(None, "hid"),
        P("hid", None),
    )
    out_specs = (P("groups", "obs", None), P("groups", "obs", None))
    return jax.shard_map(
        on_device, mesh=mesh, in_specs=in_specs, out_specs=out_specs, check_vma=False
    )
```

```python
import functools
import math

import jax
import jax.numpy as jnp
from jax import lax
from jax.experimental import pallas as pl
from jax.experimental.pallas import tpu as pltpu
from jax.sharding import PartitionSpec as P

DH = 128
STEPS = 64

SIG_LO = 0.05
SIG_HI = 1.0

F32 = jnp.float32
BF16 = jnp.bfloat16
NT = (((1,), (1,)), ((), ()))
TILE = 512
PREP_FLOPS = 4 << 30


def partner(index, by, size):
    if size & (size - 1) == 0:
        return index ^ by
    return (index + by) % size


def source(index, by, size):
    return partner(index, by if size & (size - 1) == 0 else size - by, size)


def passed_along(shard, axis, by):
    size = lax.axis_size(axis)
    return lax.ppermute(shard, axis, [(i, partner(i, by, size)) for i in range(size)])


def plan(level, feature_count):
    growth = math.log(SIG_HI / SIG_LO) / (STEPS - 1)
    sigma_now = SIG_LO * jnp.exp(growth * level)
    sigma_prev = SIG_LO * jnp.exp(growth * (level - 1.0))
    delta = sigma_now * sigma_now - sigma_prev * sigma_prev
    halves = feature_count // 2
    lane = lax.broadcasted_iota(jnp.int32, (1, halves), 1).astype(F32)
    log_sigma = math.log(SIG_LO) + growth * level[:, :1]
    angles = 10.0 * log_sigma * jnp.exp(-math.log(1000.0) / halves * lane)
    waves = jnp.sin(jnp.concatenate([angles, angles + 0.5 * math.pi], 0))
    features = jnp.concatenate([waves[0:1], waves[1:2]], 1).astype(BF16)
    return (features, delta)


def dot(a, b):
    return jnp.dot(a, b, preferred_element_type=F32)


def halves_of(x):
    high = x.astype(BF16)
    return high, (x - high.astype(F32)).astype(BF16)


def split_dot(x, weight):
    rows = x.shape[0]
    both = dot(jnp.concatenate(halves_of(x), 0), weight)
    return both[:rows] + both[rows:]


def half_silu(y):
    return y + y * jnp.tanh(y)


def put_stripes(target, values):
    count, sub = target.shape[:2]
    for s in range(count):
        target[s] = values[s * sub : (s + 1) * sub]


def others(ref, terms_ref):
    return ref[: padded(terms_ref.shape[0] * terms_ref.shape[1]), :]


def spec():
    return pl.BlockSpec(memory_space=pltpu.VMEM)


def in_hbm(x):
    return pltpu.with_memory_space_constraint(x, pltpu.HBM)


def call(body, name, out_shape, in_specs, scratch=(), flops=0, limit=4, out_spec=None, aliases={}):
    return pl.pallas_call(
        body,
        name=name,
        out_shape=out_shape,
        in_specs=in_specs,
        out_specs=jax.tree.map(lambda _: out_spec or spec(), out_shape),
        scratch_shapes=list(scratch),
        input_output_aliases=aliases,
        cost_estimate=pl.CostEstimate(flops=flops, bytes_accessed=flops // 1000, transcendentals=0),
        compiler_params=pltpu.CompilerParams(vmem_limit_bytes=limit << 20),
    )


def copies_of(sources, targets, sems):
    return [
        pltpu.make_async_copy(source, target, sems.at[i])
        for i, (source, target) in enumerate(zip(sources, targets))
    ]


def wait_for(copies):
    for copy in copies:
        copy.wait()


def padded(rows):
    return -(-rows // 16) * 16


def prep_body(size, home_ref, wt_hbm, theta_ref, mine_ref, wt_ref, *refs):
    sends, (held, stage, sems) = refs[: size - 1], refs[size - 1 :]
    z, r = lax.axis_index("obs"), lax.axis_index("rep")
    sub = held.shape[1]
    rows = stage.shape[0]
    copies = copies_of([home_ref.at[s, r] for s in range(size)], [held.at[s] for s in range(size)], sems)
    last = pltpu.make_async_copy(wt_hbm, wt_ref, sems.at[size])
    for copy in copies:
        copy.start()
    last.start()
    stage[...] = jnp.zeros_like(stage)
    wait_for(copies)
    for by, target_ref in enumerate((theta_ref, *sends)):
        target = partner(z, by, size)
        for k in range(1, size):
            stage[(k - 1) * sub : k * sub, :] = held[partner(target, k, size)]
        target_ref[:rows, :] = stage[...].astype(BF16)
        target_ref[rows:, :] = held[target].astype(BF16)
    mine_ref[...] = held[z]
    last.wait()


def pair_terms(theta, e_refs, weight_refs, scratch):
    wq_ref, wk_ref, wv_ref, ws_ref, bias_ref = weight_refs
    qk_ref, total_ref, pool_ref = scratch
    scale = 0.5 / math.sqrt(DH)
    blocks = len(theta)
    rows = theta[0].shape[0]
    heads = wk_ref.shape[1] // DH
    every = theta[0] if blocks == 1 else jnp.concatenate(theta, 0)
    queries = dot(every, wq_ref[...]).astype(BF16)
    for h in range(heads):
        cols = slice(h * DH, (h + 1) * DH)
        turned = lax.dot_general(queries[:, cols], wk_ref[:, cols], NT, preferred_element_type=F32)
        turned = (turned * scale).astype(BF16)
        for b in range(blocks):
            at = (b * heads + h) * rows
            qk_ref[at : at + rows, :] = turned[b * rows : (b + 1) * rows]

    def weights(scores):
        parts = []
        for h in range(heads):
            bias = jnp.tile(bias_ref[h : h + 1, :], (1, scores.shape[1] // 128))
            parts.append(half_silu(scores[h * rows : (h + 1) * rows] + bias).astype(BF16))
        return jnp.concatenate(parts, 0)

    fresh = True
    for e_ref in e_refs:
        tile = math.gcd(TILE, e_ref.shape[0])
        for j in range(e_ref.shape[0] // tile):
            seen = e_ref[j * tile : (j + 1) * tile, :]
            for b in range(blocks):
                span = slice(b * heads * rows, (b + 1) * heads * rows)
                scores = lax.dot_general(qk_ref[span, :], seen, NT, preferred_element_type=F32)
                term = dot(weights(scores), seen)
                total_ref[span, :] = term if fresh else total_ref[span, :] + term
            fresh = False
    for h in range(heads):
        cols = slice(h * DH, (h + 1) * DH)
        for b in range(blocks):
            at = (b * heads + h) * rows
            pool_ref[b * rows : (b + 1) * rows, cols] = split_dot(
                total_ref[at : at + rows, :], wv_ref[:, cols]
            )
    return split_dot(pool_ref[...], ws_ref[...])


def home_body(size, nrep, heads, feats, level_ref, wt_ref, theta_ref, *refs):
    e_refs, refs = refs[:nrep], refs[nrep:]
    weights, (terms_ref, bias_ref, mix_ref, feat_ref), scratch = refs[:4], refs[4:8], refs[8:]
    level = jnp.full((1, 128), level_ref[0], jnp.int32).astype(F32)
    features, delta = plan(level, feats)
    mix_ref[0:1, :] = delta
    mix_ref[1:2, :] = jnp.sqrt(delta)
    feat = jnp.broadcast_to(features, (16, feats))
    feat_ref[...] = feat
    head_bias = lax.dot_general(wt_ref[...], feat, NT, preferred_element_type=F32) * 0.5
    bias_ref[...] = jnp.broadcast_to(head_bias[:, 0:1], (heads, 128))
    theta = [others(theta_ref, terms_ref)]
    put_stripes(terms_ref, pair_terms(theta, e_refs, (*weights, bias_ref), scratch))


def mid_body(got_ref, *refs):
    e_refs, weights, (terms_ref, *scratch) = refs[:-9], refs[-9:-4], refs[-4:]
    put_stripes(terms_ref, pair_terms([others(got_ref, terms_ref)], e_refs, weights, scratch))


def far_body(size, nrep, *refs):
    home_ref, mid_ref = refs[:2]
    got, rest = refs[2:size], refs[size:]
    e_refs, weights, rest = rest[:nrep], rest[nrep : nrep + 5], rest[nrep + 5 :]
    sends, token_ref, scratch = rest[: size - 1], rest[size - 1], rest[size:]
    sub = home_ref.shape[1]
    terms = pair_terms([others(ref, home_ref) for ref in got], e_refs, weights, scratch)
    rows = terms.shape[0] // len(got)
    for k, send in enumerate(sends):
        for b in range(size):
            if b < 2:
                send[b] = (home_ref, mid_ref)[b][k].astype(BF16)
            else:
                at = (b - 2) * rows + k * sub
                send[b] = terms[at : at + sub].astype(BF16)
    token_ref[...] = terms[:8, :128]


def own_body(size, nrep, count, token_ref, theta_ref, mine_ref, *refs):
    got, refs = refs[: size - 1], refs[size - 1 :]
    e_refs, weights, refs = refs[:nrep], refs[nrep : nrep + 5], refs[nrep + 5 :]
    feat_ref, pt_ref, pin_ref, pout_ref, own_ref, part_ref, *scratch, stage = refs
    sub = own_ref.shape[1]
    rows = padded((size - 1) * sub)
    part_ref[0] = mine_ref[...]
    for b, ref in enumerate((theta_ref, *got)):
        owned = ref[rows:, :].astype(F32)
        stage[b * sub : (b + 1) * sub, :] = owned
        if b:
            part_ref[b] = owned
    theta = stage[...].astype(BF16)
    pre = dot(theta, pin_ref[...]) + dot(feat_ref[...], pt_ref[...])[0:1]
    prior = dot(half_silu(0.5 * pre).astype(BF16), pout_ref[...])
    terms = pair_terms([theta], e_refs, weights, scratch)
    put_stripes(own_ref, terms - count * prior)


def sum_body(size, order, *rest):
    own_ref, out_ref = rest[-2:]
    away = dict(zip(order, rest))
    for k in range(size):
        total = own_ref[k]
        for by in range(1, size):
            total = total + away[by][source(k, by, size)].astype(F32)
        out_ref[k] = total.astype(out_ref.dtype)


def join_body(size, *refs):
    terms, out_ref = refs[:-1], refs[-1]
    for k in range(size):
        total = terms[0][k].astype(F32)
        for term in terms[1:]:
            total = total + term[k].astype(F32)
        out_ref[k] = total


def write_body(size, nrep, reps, mix_ref, noise_ref, *refs):
    n = len(reps)
    totals, parts = refs[:n], refs[n : 2 * n]
    updated_ref, score_ref, updated_hold, score_hold, sems = refs[-5:]
    z, r = lax.axis_index("obs"), lax.axis_index("rep")
    reach = noise_ref.shape[-1] // 128
    delta = jnp.tile(mix_ref[0:1, :], (1, reach))
    root = jnp.tile(mix_ref[1:2, :], (1, reach))
    copies = []
    for i, away in enumerate(reps):
        rep = source(r, away, nrep)
        for k in range(size):
            block = source(z, k, size)
            total = totals[i][k]
            score_hold[i, k] = total
            updated_hold[i, k] = parts[i][k] + delta * total + root * noise_ref[block, rep]
            for which, (held, out) in enumerate(
                ((score_hold, score_ref), (updated_hold, updated_ref))
            ):
                copies.append(
                    pltpu.make_async_copy(held.at[i, k], out.at[block, rep], sems.at[i, k, which])
                )
                copies[-1].start()
    wait_for(copies)


def on_device(
    particles,
    obs_embed,
    step_index,
    noise,
    w_query,
    w_key,
    w_value,
    w_time,
    w_score,
    prior_in,
    prior_time,
    prior_out,
):
    size, nrep, nhid = lax.axis_size("obs"), lax.axis_size("rep"), lax.axis_size("hid")
    home = particles[0]
    block_rows, width = home.shape
    stripe = block_rows // size
    sub = stripe // nrep
    rows = padded((size - 1) * sub)
    heads = w_key.shape[1] // DH
    emb = obs_embed.shape[1]
    count = obs_embed.shape[0] * size * nrep - 1
    shifts = range(1, size)

    def shape(*dims, dtype=F32):
        return jax.ShapeDtypeStruct(dims, dtype)

    def scratch(blocks, rows=rows):
        return [
            pltpu.VMEM((blocks * heads * rows, emb), BF16),
            pltpu.VMEM((blocks * heads * rows, emb), F32),
            pltpu.VMEM((blocks * rows, heads * DH), F32),
        ]

    hbm = pl.BlockSpec(memory_space=pltpu.HBM)
    far_first = [*range(size // 2, size), *range(1, size // 2)]
    seen = [passed_along(obs_embed, "rep", by) for by in range(1, nrep)]
    time_weight = in_hbm(w_time.T)
    theta, mine, time_weight, *sends = call(
        functools.partial(prep_body, size),
        "prep",
        [
            shape(rows + sub, width, dtype=BF16),
            shape(sub, width),
            shape(*time_weight.shape, dtype=BF16),
        ]
        + [shape(rows + sub, width, dtype=BF16) for _ in shifts],
        [hbm] * 2,
        [
            pltpu.VMEM((size, sub, width), F32),
            pltpu.VMEM((rows, width), F32),
            pltpu.SemaphoreType.DMA((size + 1,)),
        ],
        PREP_FLOPS,
    )(in_hbm(home.reshape(size, nrep, sub, width)), time_weight)
    got = [passed_along(send, "obs", by) for by, send in zip(shifts, sends)]

    pair_flops = 4 * rows * heads * obs_embed.shape[0] * nrep * emb
    feats = w_time.shape[0]
    seen = [obs_embed, *seen]
    weights = [w_query, w_key, w_value, w_score]
    terms_shape = shape(size - 1, sub, width)
    home_terms, bias, mix, feat = call(
        functools.partial(home_body, size, nrep, heads, feats),
        "home_block",
        [terms_shape, shape(heads, 128), shape(2, 128), shape(16, feats, dtype=BF16)],
        [pl.BlockSpec(memory_space=pltpu.SMEM)] + [spec()] * (2 + nrep + len(weights)),
        scratch(1),
        pair_flops,
        16,
    )(step_index, time_weight, theta, *seen, *weights)
    weights = [*seen, *weights, bias]
    mid_terms = call(
        mid_body,
        "mid_block",
        terms_shape,
        [spec()] * (1 + len(weights)),
        scratch(1),
        pair_flops,
        16,
    )(got[0], *weights)
    *leave, token = call(
        functools.partial(far_body, size, nrep),
        "far_blocks",
        [shape(size, sub, width, dtype=BF16) for _ in shifts] + [shape(8, 128)],
        [spec()] * (size + len(weights)),
        scratch(size - 2),
        pair_flops * (size - 2),
        24,
    )(home_terms, mid_terms, *got[1:], *weights)
    moved = {by: passed_along(leave[by - 1], "obs", by) for by in far_first}
    own, part = call(
        functools.partial(own_body, size, nrep, float(count)),
        "own_rows",
        [shape(size, sub, width), shape(size, sub, width)],
        [spec()] * (3 + size - 1 + len(weights) + 4),
        scratch(1, size * sub) + [pltpu.VMEM((size * sub, width), F32)],
        pair_flops,
        20,
    )(token, theta, mine, *got, *weights, feat, prior_time, prior_in, prior_out)
    two = nhid == 2
    summed = call(
        functools.partial(sum_body, size, far_first),
        "sum_obs",
        shape(size, sub, width, dtype=BF16 if two else F32),
        [spec()] * size,
    )(*[moved[by] for by in far_first], own)
    if two:
        partial_sums = [summed, passed_along(summed, "hid", 1)]
    else:
        partial_sums = [lax.psum(summed, "hid")]
    joined = call(
        functools.partial(join_body, size),
        "join",
        shape(size, sub, width),
        [spec()] * len(partial_sums),
    )(*partial_sums)
    joined = [joined] + [passed_along(joined, "rep", by) for by in range(1, nrep)]
    parts = [part] + [passed_along(part, "rep", by) for by in range(1, nrep)]
    whole = shape(size, nrep, sub, width)
    noise_rows = noise.reshape(size, nrep, sub, width)
    outputs = ()
    for reps in ((0,), tuple(range(1, nrep))):
        n = len(reps)
        operands = [mix, noise_rows, *[joined[i] for i in reps], *[parts[i] for i in reps]]
        outputs = call(
            functools.partial(write_body, size, nrep, reps),
            "write_%d" % reps[0],
            [whole, whole],
            [spec()] * len(operands) + [hbm] * len(outputs),
            [pltpu.VMEM((n, size, sub, width), F32)] * 2
            + [pltpu.SemaphoreType.DMA((n, size, 2))],
            1 << 30,
            out_spec=hbm,
            aliases={len(operands) + i: i for i in range(len(outputs))},
        )(*operands, *outputs)
    updated, score = outputs
    return (updated.reshape(noise.shape), score.reshape(noise.shape))


def solution(mesh):
    in_specs = (
        P(("groups", "obs"), None, None),
        P(("groups", "obs", "rep"), None),
        P("groups"),
        P("groups", "obs", None),
        P(None, "hid"),
        P(None, "hid"),
        P(None, "hid"),
        P(None, "hid"),
        P("hid", None),
        P(None, "hid"),
        P(None, "hid"),
        P("hid", None),
    )
    out_specs = (P("groups", "obs", None), P("groups", "obs", None))
    return jax.shard_map(
        on_device, mesh=mesh, in_specs=in_specs, out_specs=out_specs, check_vma=False
    )
```
